32 devices in a mesh: dp: 8 (over z, x), expert: 4 (over y, core).
Axes of the slice: x: 2, y: 2, z: 4, core: 2. Of those that a mesh axis runs over, the one named last changes fastest.
Arguments:
- tokens: bfloat16 [4096, 2048], P(('dp', 'expert')), may hold values from -6 to 6
- d_out: bfloat16 [4096, 2048], P(('dp', 'expert')), may hold values from -6 to 6
- routes: int32 [4096, 2], P(('dp', 'expert')), may hold values from 0 to 3, all different within a row; in each aligned block of 128 rows (0 to 127, 128 to 255, ...) at most 96 rows name the same one
- gate_fixed: int32 [4096, 2], P(('dp', 'expert')), may hold values from 1 to 65535
- w_gate: bfloat16 [4, 2048, 768], P('expert'), may hold values from -0.125 to 0.125
- w_up: bfloat16 [4, 2048, 768], P('expert'), may hold values from -0.125 to 0.125
- w_down: bfloat16 [4, 768, 2048], P('expert'), may hold values from -0.21875 to 0.21875
Outputs:
- d_tokens: bfloat16 [4096, 2048], P(('dp', 'expert'))
- d_wgate: float32 [4, 2048, 768], P('expert', 'dp')
- d_wup: float32 [4, 2048, 768], P('expert', 'dp')
- d_wdown: float32 [4, 768, 2048], P('expert', 'dp')
The draws below stay inside these ranges and needn't reach their ends.
Inputs may be any that keep to these rules, and one draw needn't show every extreme that they name: Each token names 2 different experts; of the routes of one device's 128 tokens (aligned blocks of rows) at most 96 name any one expert, a bound that some block reaches of them.
All inputs are finite; a program needn't handle non-finite values.
Results may differ from the reference program's by a relative error of at most 0.0065.
Values may be sent and summed in bfloat16 or wider, within the bound.
A program may use at most 192 MiB of HBM per device.

```python
import math
import jax
import jax.numpy as jnp
import numpy as np
from jax import lax

D = 2048
I = 768
TOP = 2
TOK_DEV = 128
EXPERTS = 4
CAP = 96
TOKENS = 4096
REPLICAS = 8


def touch_ends(values, stream_key, least, high):
    place = [jax.random.randint(jax.random.fold_in(stream_key, axis), (), 0, length) for axis, length in enumerate(values.shape)]
    widest = values.shape.index(max(values.shape))
    beside = place[:widest] + [(place[widest] + 1) % values.shape[widest]] + place[widest + 1:]
    return values.at[tuple(place)].set(least).at[tuple(beside)].set(high)


def strengthened(values, rng, source, target, parts, factor):
    def block_of(axis_at):
        return (jnp.arange(values.shape[axis_at]) // (values.shape[axis_at] // parts)).reshape((-1,) + (1,) * (values.ndim - 1 - axis_at))

    one_side = jax.random.permutation(rng, parts)[block_of(target)]
    far = (block_of(target) + parts // 2) % parts
    return jnp.where((block_of(source) == one_side) | (block_of(source) == far), factor * values, values)


def block_scale(key, dims, shards, low, top_value):
    def one(position, shards_of):
        steps = jax.random.uniform(jax.random.fold_in(jax.random.fold_in(key, 6), position), (shards_of,), jnp.float32, low / len(shards), top_value / len(shards))
        return jnp.repeat(jnp.exp(steps), dims[position] // shards_of).reshape((-1,) + (1,) * (len(dims) - position - 1))

    gain = one(*shards[0])
    for cut in shards[1:]:
        gain = gain * one(*cut)
    return gain


def routed_block(own_key, own, number, rows, amount, top, most, lean):
    order = jax.random.permutation(own_key, amount)
    packed, common = portions_of(amount, rows * top, most, lean, True), portions_of(amount, rows * top, most, lean, False)
    places = jnp.arange(amount)

    def named(sizes, turn):
        used = int((sizes > 0).sum())
        fixed = max(1, used // 4)
        passed = fixed + (places - fixed + turn * (used - fixed)) % max(1, amount - fixed)
        return jnp.zeros((amount,), jnp.int32).at[order[jnp.where(places < fixed, places, passed)]].set(jnp.asarray(sizes, jnp.int32))

    sizes = jnp.where(number % 4 == 0, named(packed, number // 4), named(common, number - number // 4 - 1))
    mixed = jax.random.permutation(jax.random.fold_in(own, 3), amount)
    giver, receiver = mixed[0:amount // 2 * 2:2], mixed[1:amount // 2 * 2:2]
    margin = jnp.minimum(sizes[giver] - 1, most - sizes[receiver]) // 2
    margin = jnp.where((giver == order[0]) | (receiver == order[0]) | (sizes[receiver] == 0), 0, jnp.maximum(margin, 0))
    passed = jax.random.randint(jax.random.fold_in(own, 4), (amount // 2,), 0, 1 << 20) % (margin + 1)
    sizes = sizes.at[giver].add(-passed).at[receiver].add(passed)
    members = jnp.searchsorted(jnp.cumsum(sizes), jnp.arange(rows * top), side="right").astype(jnp.int32)
    listing = members.reshape(top, rows).T
    listing = listing[jax.random.permutation(jax.random.fold_in(own, 1), rows)]
    turn = jax.random.randint(jax.random.fold_in(own, 2), (rows, 1), 0, top)
    return jnp.take_along_axis(listing, (jnp.arange(top)[None, :] + turn) % top, axis=1)


def portions_of(amount, total, limit, slope, full):
    loads = [(1 << 20) // math.isqrt(standing ** slope) + 1 for standing in range(1, amount + 1)]
    largest = limit if full else min(limit, max(-(-total // amount), total * loads[0] // sum(loads)))
    least = 1 if total - largest >= amount - 1 else 0
    counts, spare = [largest] + [least] * (amount - 1), total - largest - least * (amount - 1)
    while spare > 0:
        candidates = [i for i in range(1, amount) if counts[i] < largest] or [i for i in range(1, amount) if counts[i] < limit]
        pool, budget = sum([loads[i] for i in candidates]), spare
        for i in candidates:
            more = min(limit - counts[i], max(1, budget * loads[i] // pool), spare)
            counts[i] = counts[i] + more
            spare = spare - more
    return np.array(counts)


def scatter_about(rng, dims, width, reach, cuts=(), held_as=jnp.bfloat16):
    entries = jax.random.normal(rng, dims, jnp.float32) * width
    if len(cuts) > 0:
        entries = block_scale(rng, dims, cuts, -0.22, 0.18) * entries
    return jnp.clip(entries, min=-reach, max=reach).astype(held_as)


def bell_draw_with(own_key, shape, deviation, bound, cuts, heavy, kind=jnp.bfloat16):
    entries = deviation * jax.random.normal(own_key, shape, jnp.float32)
    if cuts:
        entries = entries * block_scale(own_key, shape, cuts, -0.22, 0.18)
    return jnp.clip(strengthened(entries, jax.random.fold_in(own_key, 3), *heavy), -bound, bound).astype(kind)


def setup_inputs(seed: int = 0) -> dict:
    key_list = jax.random.split(jax.random.key(seed), 8)
    tokens = bell_draw_with(key_list[0], (TOKENS, D), 1.0, 6.0, ((0, 32),), (0, 1, 32, 2.75))
    d_out = scatter_about(key_list[1], (TOKENS, D), 1.0, 6.0, ((0, 32),))
    routes_keys = jax.random.split(jax.random.fold_in(key_list[2], 1), TOKENS // TOK_DEV)
    routes_turns = jax.random.permutation(jax.random.fold_in(key_list[2], 3), TOKENS // TOK_DEV)
    routes = jax.vmap(lambda own, number: routed_block(jax.random.fold_in(key_list[2], 2), own, number, TOK_DEV, EXPERTS, TOP, CAP, 2))(routes_keys, routes_turns).reshape((TOKENS, TOP))
    gate_fixed = touch_ends(jax.random.randint(key_list[3], (TOKENS, TOP), 1, 65536), jax.random.fold_in(key_list[3], 1), 1, 65535).astype(jnp.int32)
    w_gate = scatter_about(key_list[4], (EXPERTS, D, I), D ** -0.5, 0.125, ((0, 4),))
    w_up = scatter_about(key_list[5], (EXPERTS, D, I), D ** -0.5, 0.125, ((0, 4),))
    w_down = scatter_about(key_list[6], (EXPERTS, I, D), I ** -0.5, 0.21875, ((0, 4),))
    return dict(tokens=tokens, d_out=d_out, routes=routes, gate_fixed=gate_fixed, w_gate=w_gate, w_up=w_up, w_down=w_down)


def reference(tokens, d_out, routes, gate_fixed, w_gate, w_up, w_down):
    token_count, top_count = routes.shape
    route_total = token_count * top_count
    gate_value = (gate_fixed.astype(jnp.float32) / 65536.0).reshape(-1)
    expert_ids = routes.reshape(-1).astype(jnp.int32)
    ordering = jnp.argsort(expert_ids, stable=True).astype(jnp.int32)
    matches = (expert_ids[:, None] == jnp.arange(EXPERTS, dtype=jnp.int32)[None, :]).astype(jnp.int32)
    counting = jnp.sum(matches, axis=0).astype(jnp.int32)
    offsets = (jnp.cumsum(counting) - counting).astype(jnp.int32)
    row_bound = min(CAP * (token_count // TOK_DEV), route_total)
    padded = jnp.concatenate([ordering, jnp.zeros((row_bound,), jnp.int32)])
    inverse = 1.0 / REPLICAS

    def per_expert(accumulated, expert):
        picked = lax.dynamic_slice(padded, (offsets[expert].astype(jnp.int32),), (row_bound,)).astype(jnp.int32)
        live_rows = jnp.arange(row_bound, dtype=jnp.int32) < counting[expert]
        owner_token = (picked // top_count).astype(jnp.int32)
        rows_x = tokens[owner_token]
        scaled = (gate_value[picked][:, None] * d_out[owner_token].astype(jnp.float32)).astype(jnp.bfloat16)
        scaled = jnp.where(live_rows[:, None], scaled, jnp.zeros_like(scaled))
        gate_matrix = w_gate[expert]
        up_matrix = w_up[expert]
        down_matrix = w_down[expert]
        pre_gate = jnp.dot(rows_x, gate_matrix, preferred_element_type=jnp.float32)
        pre_up = jnp.dot(rows_x, up_matrix, preferred_element_type=jnp.float32)
        sigmoid_gate = jax.nn.sigmoid(pre_gate)
        silu_gate = pre_gate * sigmoid_gate
        hidden = (silu_gate * pre_up).astype(jnp.bfloat16)
        d_hidden = jnp.dot(scaled, down_matrix.T, preferred_element_type=jnp.float32)
        d_gate = (d_hidden * pre_up * sigmoid_gate * (1.0 + pre_gate * (1.0 - sigmoid_gate))).astype(jnp.bfloat16)
        d_up = (d_hidden * silu_gate).astype(jnp.bfloat16)
        route_grad = (jnp.dot(d_gate, gate_matrix.T, preferred_element_type=jnp.float32)
                      + jnp.dot(d_up, up_matrix.T, preferred_element_type=jnp.float32)).astype(jnp.bfloat16)
        contribution = jnp.where(live_rows[:, None], route_grad.astype(jnp.float32), jnp.zeros((), jnp.float32))
        accumulated = accumulated.at[owner_token].add(contribution)
        grad_gate = jnp.dot(rows_x.T, d_gate, preferred_element_type=jnp.float32) * inverse
        grad_up = jnp.dot(rows_x.T, d_up, preferred_element_type=jnp.float32) * inverse
        grad_down = jnp.dot(hidden.T, scaled, preferred_element_type=jnp.float32) * inverse
        return accumulated, (grad_gate, grad_up, grad_down)

    start_grad = jnp.zeros((token_count, tokens.shape[1]), jnp.float32)
    accumulated, grads = lax.scan(per_expert, start_grad, jnp.arange(EXPERTS, dtype=jnp.int32))
    return accumulated.astype(jnp.bfloat16), grads[0], grads[1], grads[2]
```

```python
import functools

import jax
import jax.numpy as jnp
from jax import lax
from jax.experimental import pallas as pl
from jax.experimental.pallas import tpu as pltpu
from jax.sharding import PartitionSpec as P

MESH = pl.DeviceIdType.MESH
BF16 = jnp.bfloat16
F32 = jnp.float32


def greet(targets):
    barrier = pltpu.get_barrier_semaphore()
    for target in targets:
        pl.semaphore_signal(barrier, inc=1, device_id=target, device_id_type=MESH)
    pl.semaphore_wait(barrier, len(targets))


def outer_product(left, right):
    return lax.dot_general(left, right, (((0,), (0,)), ((), ())), preferred_element_type=F32)


def times_transposed(left, right):
    return lax.dot_general(left, right, (((1,), (1,)), ((), ())), preferred_element_type=F32)


def kernel(
    span, replicas, parts,
    x_ref, g_ref, routes_ref, gates_ref, wg_ref, wu_ref, wd_ref,
    tok_out, gate_out, up_out, down_out,
    wg, wu, wd, xs, gs, px, scaled, coef, cs, for_gate, for_up, acts, pact, hidden,
    grads, glines, total, cross_out, cross_in, dgrads, dnear, dlines, back,
    w_sem, own_sem, c_send, c_recv, core_send, core_recv, chip_send, chip_recv, fwd_send, fwd_recv,
    px_send, px_recv, act_send, act_recv, near_send, near_recv, gline_send, gline_recv,
    dline_send, dline_recv, back_send, back_recv, cross_send, cross_recv,
):
    expert = lax.axis_index("expert")
    me = lax.axis_index("dp")
    core = lax.rem(expert, 2)
    chip = expert // 2
    other = chip * 2 + (1 - core)
    chips = span // 2
    outer = replicas // 2
    side = lax.rem(me, 2)
    line = me // 2
    partner = line * 2 + (1 - side)
    lower = lax.rem(line + outer - 1, outer) * 2 + side
    upper = lax.rem(line + 1, outer) * 2 + side
    rows, width = x_ref.shape
    units = hidden.shape[1]
    feature = width // replicas
    shard = units // replicas
    piece_rows = rows // parts
    inverse = 1.0 / replicas

    own_x = pltpu.make_async_copy(x_ref, xs.at[expert], own_sem.at[0])
    own_g = pltpu.make_async_copy(g_ref, gs.at[expert], own_sem.at[1])
    loads = [
        pltpu.make_async_copy(source.at[0], target, w_sem.at[at])
        for at, (source, target) in enumerate(((wg_ref, wg), (wu_ref, wu), (wd_ref, wd)))
    ]
    own_x.start()
    loads[0].start()
    loads[1].start()
    own_g.start()
    loads[2].start()
    places = lax.broadcasted_iota(jnp.int32, coef.shape, 0)
    value = jnp.zeros(coef.shape, F32)
    for k in range(routes_ref.shape[0]):
        gate_value = gates_ref[k : k + 1, :].astype(F32) / 65536.0
        value = value + jnp.where(places == routes_ref[k : k + 1, :], gate_value, 0.0)
    coef[...] = value
    cs[expert] = value

    targets = [{"expert": lax.rem(expert + step, span)} for step in range(1, span)]
    targets += [{"dp": partner}, {"dp": lower}, {"dp": upper}]
    greet(targets)

    def remote(source, target, send, recv, device):
        return pltpu.make_async_remote_copy(
            src_ref=source, dst_ref=target, send_sem=send, recv_sem=recv, device_id=device, device_id_type=MESH
        )

    def piece(ref, part):
        return ref.at[pl.ds(part * piece_rows, piece_rows)]

    sources = (x_ref, g_ref, px.at[expert])
    arrays = (xs, gs, px)

    def coef_copy(step):
        return remote(
            coef, cs.at[expert], c_send.at[step], c_recv.at[step], {"expert": lax.rem(expert + step, span)}
        )

    def core_copy(array):
        return remote(
            sources[array], arrays[array].at[expert], core_send.at[array], core_recv.at[array], {"expert": other}
        )

    def chip_copy(array, part, step):
        there = lax.rem(chip + step, chips) * 2 + core
        return remote(
            piece(sources[array], part), piece(arrays[array].at[expert], part),
            chip_send.at[array, part, step], chip_recv.at[array, part, step], {"expert": there},
        )

    def forward_copy(array, part, step, at_core):
        owner = lax.rem(chip + chips - step, chips) * 2 + at_core
        block = piece(arrays[array].at[owner], part)
        return remote(
            block, block, fwd_send.at[array, part, step], fwd_recv.at[array, part, step], {"expert": other}
        )

    def pass_on(array, step):
        for part in range(parts):
            chip_copy(array, part, step).wait_recv()
            forward_copy(array, part, step, core).start()

    def take_passed(array, step):
        for part in range(parts):
            forward_copy(array, part, step, 1 - core).wait_recv()

    px_copy = remote(x_ref, px.at[expert], px_send, px_recv, {"dp": partner})

    def pair_rows(step):
        base = lax.rem(chip + chips - step, chips) * 2
        return pl.ds(pl.multiple_of(base * rows, 2 * rows), 2 * rows)

    def act_copy(step):
        at = pair_rows(step)
        return remote(
            acts.at[1 - side, at], pact.at[at], act_send.at[step], act_recv.at[step], {"dp": partner}
        )

    def back_copy(step):
        there = lax.rem(expert + step, span)
        return remote(gs.at[there], back.at[step], back_send.at[step], back_recv.at[step], {"expert": there})

    place = jnp.where(line < outer // 2, 2 * line + 1, 2 * (outer - 1 - line))

    def order_at(i):
        j = i + jnp.where(i >= place, 1, 0)
        d = jnp.where(lax.rem(j, 2) == 0, outer - 1 - j // 2, j // 2)
        return jnp.where(i == outer - 1, line, d)

    def is_fed(d):
        return ((d > line) & (line > 0)) | ((d < line) & (line < outer - 1))

    def near_copy(d):
        return remote(
            dgrads.at[d * 2 + (1 - side)], dnear.at[d], near_send.at[d], near_recv.at[d], {"dp": partner}
        )

    def hop(d):
        following = jnp.where(d > line, line + 1, line - 1)
        slot = jnp.where((d < line) & (d == following), outer, d)
        return slot, {"dp": following * 2 + side}

    def gline_copy(d, s):
        slot, device = hop(d)
        return remote(grads.at[d, s], glines.at[slot, s], gline_send.at[d, s], gline_recv.at[slot, s], device)

    def gline_wait(slot, s):
        remote(
            glines.at[slot, s], glines.at[slot, s], gline_send.at[0, s], gline_recv.at[slot, s], {"dp": upper}
        ).wait_recv()

    def dline_copy(d):
        slot, device = hop(d)
        return remote(dgrads.at[d * 2 + side], dlines.at[slot], dline_send.at[d], dline_recv.at[slot], device)

    def dline_wait(slot):
        remote(
            dlines.at[slot], dlines.at[slot], dline_send.at[0], dline_recv.at[slot], {"dp": upper}
        ).wait_recv()

    halves = (1 - side, side)

    for step in range(1, span):
        coef_copy(step).start()
    for part in range(parts):
        for step in range(1, chips):
            chip_copy(0, part, step).start()
    core_copy(0).start()
    px_copy.start()
    core_copy(1).start()
    for part in range(parts):
        for step in range(1, chips):
            chip_copy(1, part, step).start()

    cut = units // 3

    def project(step):
        base = lax.rem(chip + chips - step, chips) * 2
        at = pair_rows(step)
        x = xs[pl.ds(base, 2)].reshape(2 * rows, width)
        for c in range(3):
            columns = slice(c * cut, (c + 1) * cut)
            pre_gate = jnp.dot(x, wg[:, columns], preferred_element_type=F32)
            pre_up = jnp.dot(x, wu[:, columns], preferred_element_type=F32)
            sigmoid_gate = 1.0 / (1.0 + jnp.exp(-pre_gate))
            silu_gate = pre_gate * sigmoid_gate
            hidden[at, columns] = (silu_gate * pre_up).astype(BF16)
            for_up[:, columns] = silu_gate
            for_gate[:, columns] = pre_up * sigmoid_gate * (1.0 + pre_gate * (1.0 - sigmoid_gate))

    def differentiate(step):
        base = lax.rem(chip + chips - step, chips) * 2
        at = pair_rows(step)
        row = lax.broadcasted_iota(jnp.int32, (rows, rows), 0)
        diagonal = row == lax.broadcasted_iota(jnp.int32, (rows, rows), 1)
        for j in range(2):
            owner = base + j
            weight = jnp.sum(jnp.where(diagonal, cs[owner, pl.ds(expert, 1), :], 0.0), axis=1, keepdims=True)
            scaled[pl.ds(pl.multiple_of(owner * rows, rows), rows), :] = (
                weight * gs[owner].astype(F32)
            ).astype(BF16)
        block = scaled[at, :]
        for c in range(3):
            columns = slice(c * cut, (c + 1) * cut)
            d_hidden = times_transposed(block, wd[columns, :])
            acts[0, at, columns] = (d_hidden * for_gate[:, columns]).astype(BF16)
            acts[1, at, columns] = (d_hidden * for_up[:, columns]).astype(BF16)
        act_copy(step).start()

    own_x.wait()
    loads[0].wait()
    loads[1].wait()
    core_copy(0).wait_recv()
    project(0)
    own_g.wait()
    loads[2].wait()
    core_copy(1).wait_recv()
    for step in range(1, span):
        coef_copy(step).wait_recv()
    differentiate(0)
    px_copy.wait_recv()
    core_copy(2).start()
    for step in range(1, chips):
        pass_on(0, step)
        take_passed(0, step)
        project(step)
        if step == 1:
            for part in range(parts):
                for later in range(1, chips):
                    chip_copy(2, part, later).start()
        pass_on(1, step)
        take_passed(1, step)
        differentiate(step)

    half = units // 2
    for part in range(2):
        product = outer_product(hidden[:, part * half : (part + 1) * half], scaled[...])
        for at in range(half // shard):
            dgrads[part * (half // shard) + at] = product[at * shard : (at + 1) * shard].astype(BF16)

    def start_near(i, carry):
        near_copy(order_at(i)).start()
        return carry

    lax.fori_loop(0, outer, start_near, 0)

    for step in range(1, chips):
        pass_on(2, step)
    for step in range(1, chips):
        take_passed(2, step)
    core_copy(2).wait_recv()
    for step in range(chips):
        act_copy(step).wait_recv()

    def product_at(d):
        columns = pl.ds(pl.multiple_of(d * 2 * feature, 2 * feature), 2 * feature)
        return outer_product(xs[:, :, columns].reshape(span * rows, 2 * feature), acts[side]) + outer_product(
            px[:, :, columns].reshape(span * rows, 2 * feature), pact[...]
        )

    def make(i, carry):
        d = order_at(i)
        product = product_at(d)
        grads[d, 0] = product[:feature].astype(BF16)
        grads[d, 1] = product[feature:].astype(BF16)

        @pl.when(jnp.logical_not(is_fed(d)))
        def _():
            for s in halves:
                gline_copy(d, s).start()

        return carry

    lax.fori_loop(0, outer - 1, make, 0)
    product = product_at(line)
    total[0] = product[:feature]
    total[1] = product[feature:]

    for array in range(2):
        for step in range(1, chips):
            for part in range(parts):
                forward_copy(array, part, step, core).wait_send()

    def route_pair(step, carry):
        base = lax.rem(chip + chips - step, chips) * 2
        at = pair_rows(step)
        product = times_transposed(acts[0, at, :], wg[...]) + times_transposed(acts[1, at, :], wu[...])
        gs[base] = product[:rows].astype(BF16)
        gs[base + 1] = product[rows:].astype(BF16)
        return carry

    lax.fori_loop(0, chips, route_pair, 0)
    for step in range(1, span):
        back_copy(step).start()

    def pass_gates(i, carry):
        d = order_at(i)

        @pl.when(is_fed(d))
        def _():
            for s in halves:
                gline_wait(d, s)
                grads[d, s] = (grads[d, s].astype(F32) + glines[d, s].astype(F32)).astype(BF16)
                gline_copy(d, s).start()

        return carry

    lax.fori_loop(0, outer - 1, pass_gates, 0)

    def pass_down(i, carry):
        d = order_at(i)
        near_copy(d).wait_recv()
        fed = is_fed(d)
        at = d * 2 + side

        @pl.when(fed)
        def _():
            dline_wait(d)
            dgrads[at] = (dgrads[at].astype(F32) + dnear[d].astype(F32) + dlines[d].astype(F32)).astype(BF16)

        @pl.when(jnp.logical_not(fed))
        def _():
            dgrads[at] = (dgrads[at].astype(F32) + dnear[d].astype(F32)).astype(BF16)

        dline_copy(d).start()
        return carry

    lax.fori_loop(0, outer - 1, pass_down, 0)
    for step in range(1, span):
        back_copy(step).wait_recv()
    route_sum = gs[expert].astype(F32)
    for step in range(1, span):
        route_sum = route_sum + back[step].astype(F32)
    tok_out[...] = route_sum.astype(BF16)

    cross = remote(cross_out, cross_in, cross_send, cross_recv, {"dp": partner})
    for s in halves:

        @pl.when(line > 0)
        def _():
            gline_wait(line, s)
            total[s] += glines[line, s].astype(F32)

        @pl.when(line < outer - 1)
        def _():
            gline_wait(outer, s)
            total[s] += glines[outer, s].astype(F32)

        if s is halves[0]:
            cross_out[...] = total[s].astype(BF16)
            cross.start()

    near_copy(line).wait_recv()
    down_out[...] = (dgrads[me].astype(F32) + dnear[line].astype(F32)) * inverse

    @pl.when(line > 0)
    def _():
        dline_wait(line)
        down_out[...] += dlines[line].astype(F32) * inverse

    @pl.when(line < outer - 1)
    def _():
        dline_wait(outer)
        down_out[...] += dlines[outer].astype(F32) * inverse

    cross.wait_recv()

    @pl.when(side == 0)
    def _():
        gate_out[...] = total[0] * inverse
        up_out[...] = cross_in[...].astype(F32) * inverse

    @pl.when(side == 1)
    def _():
        up_out[...] = total[1] * inverse
        gate_out[...] = cross_in[...].astype(F32) * inverse

    for step in range(1, span):
        coef_copy(step).wait_send()
        back_copy(step).wait_send()
    for array in range(3):
        core_copy(array).wait_send()
        for step in range(1, chips):
            for part in range(parts):
                chip_copy(array, part, step).wait_send()
                if array == 2:
                    forward_copy(array, part, step, core).wait_send()
    px_copy.wait_send()
    for step in range(chips):
        act_copy(step).wait_send()

    def finish(i, carry):
        d = order_at(i)
        near_copy(d).wait_send()

        @pl.when(i < outer - 1)
        def _():
            dline_copy(d).wait_send()
            for s in halves:
                gline_copy(d, s).wait_send()

        return carry

    lax.fori_loop(0, outer, finish, 0)
    cross.wait_send()


def fused(tokens, d_out, routes, gates, w_gate, w_up, w_down, span, replicas):
    parts = 4
    dma = pltpu.SemaphoreType.DMA
    rows, width = tokens.shape
    units = w_gate.shape[2]
    outer, chips = replicas // 2, span // 2
    feature, shard = width // replicas, units // replicas
    amount = span * rows
    here = pl.BlockSpec(memory_space=pltpu.VMEM)
    away = pl.BlockSpec(memory_space=pl.ANY)
    vmem = pltpu.VMEM
    places = max(8, span)
    return pl.pallas_call(
        functools.partial(kernel, span, replicas, parts),
        out_shape=(
            jax.ShapeDtypeStruct((rows, width), BF16),
            jax.ShapeDtypeStruct((feature, units), F32),
            jax.ShapeDtypeStruct((feature, units), F32),
            jax.ShapeDtypeStruct((shard, width), F32),
        ),
        in_specs=[away, away, here, here, away, away, away],
        out_specs=[here] * 4,
        scratch_shapes=[
            vmem((width, units), BF16), vmem((width, units), BF16), vmem((units, width), BF16),
            vmem((span, rows, width), BF16), vmem((span, rows, width), BF16), vmem((span, rows, width), BF16),
            vmem((amount, width), BF16),
            vmem((places, rows), F32), vmem((span, places, rows), F32),
            vmem((2 * rows, units), F32), vmem((2 * rows, units), F32),
            vmem((2, amount, units), BF16), vmem((amount, units), BF16), vmem((amount, units), BF16),
            vmem((outer, 2, feature, units), BF16), vmem((outer + 1, 2, feature, units), BF16),
            vmem((2, feature, units), F32), vmem((feature, units), BF16), vmem((feature, units), BF16),
            vmem((replicas, shard, width), BF16), vmem((outer, shard, width), BF16),
            vmem((outer + 1, shard, width), BF16),
            vmem((span, rows, width), BF16),
            dma((3,)), dma((2,)), dma((span,)), dma((span,)), dma((3,)), dma((3,)),
            dma((3, parts, chips)), dma((3, parts, chips)), dma((3, parts, chips)), dma((3, parts, chips)),
            dma, dma, dma((chips,)), dma((chips,)), dma((outer,)), dma((outer,)),
            dma((outer, 2)), dma((outer + 1, 2)), dma((outer,)), dma((outer + 1,)),
            dma((span,)), dma((span,)), dma, dma,
        ],
        compiler_params=pltpu.CompilerParams(
            collective_id=0, has_side_effects=True, vmem_limit_bytes=62 << 20
        ),
        name="fused",
    )(tokens, d_out, routes, gates, w_gate, w_up, w_down)


def body(tokens, d_out, routes, gate_fixed, w_gate, w_up, w_down):
    span = lax.axis_size("expert")
    replicas = lax.axis_size("dp")
    d_tokens, out_gate, out_up, out_down = fused(
        tokens, d_out, routes.T, gate_fixed.T, w_gate, w_up, w_down, span, replicas
    )
    return d_tokens, out_gate[None], out_up[None], out_down[None]


def solution(mesh):
    rows = P(("dp", "expert"), None)
    whole = P("expert", None, None)
    cut = P("expert", "dp", None)
    return jax.shard_map(
        body, mesh=mesh, in_specs=(rows,) * 4 + (whole,) * 3, out_specs=(rows, cut, cut, cut), check_vma=False
    )
```

```python
import functools

import jax
import jax.numpy as jnp
from jax import lax
from jax.experimental import pallas as pl
from jax.experimental.pallas import tpu as pltpu
from jax.sharding import PartitionSpec as P

MESH = pl.DeviceIdType.MESH
BF16 = jnp.bfloat16
F32 = jnp.float32


def greet(targets):
    barrier = pltpu.get_barrier_semaphore()
    for target in targets:
        pl.semaphore_signal(barrier, inc=1, device_id=target, device_id_type=MESH)
    pl.semaphore_wait(barrier, len(targets))


def outer_product(left, right):
    return lax.dot_general(left, right, (((0,), (0,)), ((), ())), preferred_element_type=F32)


def times_transposed(left, right):
    return lax.dot_general(left, right, (((1,), (1,)), ((), ())), preferred_element_type=F32)


def kernel(
    span, replicas, parts,
    x_ref, g_ref, routes_ref, gates_ref, wg_ref, wu_ref, wd_ref,
    tok_out, gate_out, up_out, down_out,
    wg, wu, wd, xs, gs, px, scaled, coef, cs, for_gate, for_up, acts, pact, hidden,
    grads, glines, total, cross_out, cross_in, dgrads, dnear, dlines, back, zg, zcs, zhid,
    w_sem, own_sem, c_send, c_recv, core_send, core_recv, chip_send, chip_recv, fwd_send, fwd_recv,
    px_send, px_recv, act_send, act_recv, near_send, near_recv, gline_send, gline_recv,
    dline_send, dline_recv, back_send, back_recv, cross_send, cross_recv,
    z_send, z_recv, zf_send, zf_recv, zh_send, zh_recv, zc_send, zc_recv,
):
    expert = lax.axis_index("expert")
    me = lax.axis_index("dp")
    core = lax.rem(expert, 2)
    chip = expert // 2
    other = chip * 2 + (1 - core)
    chips = span // 2
    outer = replicas // 2
    side = lax.rem(me, 2)
    line = me // 2
    partner = line * 2 + (1 - side)
    lower = lax.rem(line + outer - 1, outer) * 2 + side
    upper = lax.rem(line + 1, outer) * 2 + side
    rows, width = x_ref.shape
    units = hidden.shape[1]
    feature = width // replicas
    shard = units // replicas
    piece_rows = rows // parts
    inverse = 1.0 / replicas
    is_end = (line == 0) | (line == outer - 1)
    is_helper = (line == 1) | (line == outer - 2)
    inner = {"dp": jnp.where(line == 0, 1, outer - 2) * 2 + side}
    ended = jnp.where(line == 1, 0, outer - 1)

    own_x = pltpu.make_async_copy(x_ref, xs.at[expert], own_sem.at[0])
    own_g = pltpu.make_async_copy(g_ref, gs.at[expert], own_sem.at[1])
    loads = [
        pltpu.make_async_copy(source.at[0], target, w_sem.at[at])
        for at, (source, target) in enumerate(((wg_ref, wg), (wu_ref, wu), (wd_ref, wd)))
    ]
    own_x.start()
    loads[0].start()
    loads[1].start()
    own_g.start()
    loads[2].start()
    places = lax.broadcasted_iota(jnp.int32, coef.shape, 0)
    value = jnp.zeros(coef.shape, F32)
    for k in range(routes_ref.shape[0]):
        gate_value = gates_ref[k : k + 1, :].astype(F32) / 65536.0
        value = value + jnp.where(places == routes_ref[k : k + 1, :], gate_value, 0.0)
    coef[...] = value
    cs[expert] = value

    targets = [{"expert": lax.rem(expert + step, span)} for step in range(1, span)]
    targets += [{"dp": partner}, {"dp": lower}, {"dp": upper}]
    greet(targets)

    def remote(source, target, send, recv, device):
        return pltpu.make_async_remote_copy(
            src_ref=source, dst_ref=target, send_sem=send, recv_sem=recv, device_id=device, device_id_type=MESH
        )

    def piece(ref, part):
        return ref.at[pl.ds(part * piece_rows, piece_rows)]

    sources = (x_ref, g_ref, px.at[expert])
    arrays = (xs, gs, px)

    def coef_copy(step):
        return remote(
            coef, cs.at[expert], c_send.at[step], c_recv.at[step], {"expert": lax.rem(expert + step, span)}
        )

    def core_copy(array):
        return remote(
            sources[array], arrays[array].at[expert], core_send.at[array], core_recv.at[array], {"expert": other}
        )

    def chip_copy(array, part, step):
        there = lax.rem(chip + step, chips) * 2 + core
        return remote(
            piece(sources[array], part), piece(arrays[array].at[expert], part),
            chip_send.at[array, part, step], chip_recv.at[array, part, step], {"expert": there},
        )

    def forward_copy(array, part, step, at_core):
        owner = lax.rem(chip + chips - step, chips) * 2 + at_core
        block = piece(arrays[array].at[owner], part)
        return remote(
            block, block, fwd_send.at[array, part, step], fwd_recv.at[array, part, step], {"expert": other}
        )

    def pass_on(array, step):
        for part in range(parts):
            chip_copy(array, part, step).wait_recv()
            forward_copy(array, part, step, core).start()
            if array == 1:

                @pl.when(is_end)
                def _():
                    z_copy(part, step).start()

    def take_passed(array, step):
        for part in range(parts):
            forward_copy(array, part, step, 1 - core).wait_recv()

    px_copy = remote(x_ref, px.at[expert], px_send, px_recv, {"dp": partner})

    def pair_rows(step):
        base = lax.rem(chip + chips - step, chips) * 2
        return pl.ds(pl.multiple_of(base * rows, 2 * rows), 2 * rows)

    def act_copy(step):
        at = pair_rows(step)
        return remote(
            acts.at[1 - side, at], pact.at[at], act_send.at[step], act_recv.at[step], {"dp": partner}
        )

    def back_copy(step):
        there = lax.rem(expert + step, span)
        return remote(gs.at[there], back.at[step], back_send.at[step], back_recv.at[step], {"expert": there})

    upside = line >= outer // 2
    nearest = jnp.where(upside, outer - 1 - line, line)

    def order_at(i):
        j = i + jnp.where(i >= 2 * nearest + 1, 1, 0)
        d = jnp.where(lax.rem(j, 2) == 0, outer - 1 - j // 2, j // 2)
        return jnp.where(i == outer - 1, line, jnp.where(upside, outer - 1 - d, d))

    def is_fed(d):
        return ((d > line) & (line > 0)) | ((d < line) & (line < outer - 1))

    def near_copy(d):
        return remote(
            dgrads.at[d * 2 + (1 - side)], dnear.at[d], near_send.at[d], near_recv.at[d], {"dp": partner}
        )

    def hop(d):
        following = jnp.where(d > line, line + 1, line - 1)
        slot = jnp.where((d < line) & (d == following), outer, d)
        return slot, {"dp": following * 2 + side}

    def gline_copy(d, s):
        slot, device = hop(d)
        return remote(grads.at[d, s], glines.at[slot, s], gline_send.at[d, s], gline_recv.at[slot, s], device)

    def gline_wait(slot, s):
        remote(
            glines.at[slot, s], glines.at[slot, s], gline_send.at[0, s], gline_recv.at[slot, s], {"dp": upper}
        ).wait_recv()

    def dline_copy(d):
        slot, device = hop(d)
        return remote(dgrads.at[d * 2 + side], dlines.at[slot], dline_send.at[d], dline_recv.at[slot], device)

    def dline_wait(slot):
        remote(
            dlines.at[slot], dlines.at[slot], dline_send.at[0], dline_recv.at[slot], {"dp": upper}
        ).wait_recv()

    def is_fed_down(d):
        return ((d > line) & (line > 1)) | ((d < line) & (line < outer - 2))

    def z_copy(part, step):
        owner = lax.rem(chip + chips - step, chips) * 2 + core
        source = g_ref if step == 0 else gs.at[owner]
        return remote(
            piece(source, part), piece(zg.at[owner], part), z_send.at[part, step], z_recv.at[part, step], inner
        )

    def z_forward(part, step, at_core):
        owner = lax.rem(chip + chips - step, chips) * 2 + at_core
        block = piece(zg.at[owner], part)
        return remote(block, block, zf_send.at[part, step], zf_recv.at[part, step], {"expert": other})

    def z_hidden(step):
        at = pair_rows(step)
        return remote(hidden.at[at], zhid.at[at], zh_send.at[step], zh_recv.at[step], inner)

    z_coef = remote(cs, zcs, zc_send, zc_recv, inner)

    halves = (1 - side, side)

    for step in range(1, span):
        coef_copy(step).start()
    for part in range(parts):
        for step in range(1, chips):
            chip_copy(0, part, step).start()
    core_copy(0).start()
    px_copy.start()
    core_copy(1).start()
    for part in range(parts):
        for step in range(1, chips):
            chip_copy(1, part, step).start()

    @pl.when(is_end)
    def _():
        for part in range(parts):
            z_copy(part, 0).start()

    cut = units // 3

    def project(step):
        base = lax.rem(chip + chips - step, chips) * 2
        at = pair_rows(step)
        x = xs[pl.ds(base, 2)].reshape(2 * rows, width)
        for c in range(3):
            columns = slice(c * cut, (c + 1) * cut)
            pre_gate = jnp.dot(x, wg[:, columns], preferred_element_type=F32)
            pre_up = jnp.dot(x, wu[:, columns], preferred_element_type=F32)
            sigmoid_gate = 1.0 / (1.0 + jnp.exp(-pre_gate))
            silu_gate = pre_gate * sigmoid_gate
            hidden[at, columns] = (silu_gate * pre_up).astype(BF16)
            for_up[:, columns] = silu_gate
            for_gate[:, columns] = pre_up * sigmoid_gate * (1.0 + pre_gate * (1.0 - sigmoid_gate))

        @pl.when(is_end)
        def _():
            z_hidden(step).start()

    def weigh(coefs, owner, block):
        row = lax.broadcasted_iota(jnp.int32, (rows, rows), 0)
        diagonal = row == lax.broadcasted_iota(jnp.int32, (rows, rows), 1)
        weight = jnp.sum(jnp.where(diagonal, coefs[owner, pl.ds(expert, 1), :], 0.0), axis=1, keepdims=True)
        return (weight * block.astype(F32)).astype(BF16)

    def differentiate(step):
        base = lax.rem(chip + chips - step, chips) * 2
        at = pair_rows(step)
        for j in range(2):
            owner = base + j
            scaled[pl.ds(pl.multiple_of(owner * rows, rows), rows), :] = weigh(cs, owner, gs[owner])
        block = scaled[at, :]
        for c in range(3):
            columns = slice(c * cut, (c + 1) * cut)
            d_hidden = times_transposed(block, wd[columns, :])
            acts[0, at, columns] = (d_hidden * for_gate[:, columns]).astype(BF16)
            acts[1, at, columns] = (d_hidden * for_up[:, columns]).astype(BF16)
        act_copy(step).start()

    own_x.wait()
    loads[0].wait()
    loads[1].wait()
    core_copy(0).wait_recv()
    project(0)
    own_g.wait()
    loads[2].wait()
    core_copy(1).wait_recv()
    for step in range(1, span):
        coef_copy(step).wait_recv()

    @pl.when(is_end)
    def _():
        z_coef.start()

    differentiate(0)
    px_copy.wait_recv()
    core_copy(2).start()
    for step in range(1, chips):
        pass_on(0, step)
        take_passed(0, step)
        project(step)
        if step == 1:
            for part in range(parts):
                for later in range(1, chips):
                    chip_copy(2, part, later).start()
        pass_on(1, step)
        take_passed(1, step)
        differentiate(step)

    for step in range(1, chips):
        pass_on(2, step)
    for step in range(1, chips):
        take_passed(2, step)
    core_copy(2).wait_recv()
    for step in range(chips):
        act_copy(step).wait_recv()

    def product_at(d):
        columns = pl.ds(pl.multiple_of(d * 2 * feature, 2 * feature), 2 * feature)
        return outer_product(xs[:, :, columns].reshape(span * rows, 2 * feature), acts[side]) + outer_product(
            px[:, :, columns].reshape(span * rows, 2 * feature), pact[...]
        )

    def make(i, carry):
        d = order_at(i)
        product = product_at(d)
        grads[d, 0] = product[:feature].astype(BF16)
        grads[d, 1] = product[feature:].astype(BF16)

        @pl.when(jnp.logical_not(is_fed(d)))
        def _():
            for s in halves:
                gline_copy(d, s).start()

        return carry

    lax.fori_loop(0, outer - 1, make, 0)
    product = product_at(line)
    total[0] = product[:feature]
    total[1] = product[feature:]

    half = units // 2

    def down(helps):
        for part in range(2):
            columns = slice(part * half, (part + 1) * half)
            product = outer_product(hidden[:, columns], scaled[...])
            if helps:
                product = product + outer_product(zhid[:, columns], zg[...].reshape(span * rows, width))
            for at in range(half // shard):
                dgrads[part * (half // shard) + at] = product[at * shard : (at + 1) * shard].astype(BF16)

    @pl.when(is_helper)
    def _():
        for step in range(chips):
            for part in range(parts):
                z_copy(part, step).wait_recv()
                z_forward(part, step, core).start()
        z_coef.wait_recv()
        column = lax.broadcasted_iota(jnp.int32, (1, units), 1) // (2 * shard)
        kept = jnp.where(column == ended, 0.0, 1.0).astype(BF16)
        for step in range(chips):
            z_hidden(step).wait_recv()
        zhid[...] = zhid[...] * kept
        for step in range(chips):
            for part in range(parts):
                z_forward(part, step, core).wait_send()
                z_forward(part, step, 1 - core).wait_recv()
        for owner in range(span):
            zg[owner] = weigh(zcs, owner, zg[owner])
        down(True)

    @pl.when(jnp.logical_not(is_helper))
    def _():
        down(False)

    def start_near(i, carry):
        d = order_at(i)

        @pl.when(jnp.logical_not(is_end) | (d == line))
        def _():
            near_copy(d).start()

        return carry

    lax.fori_loop(0, outer, start_near, 0)

    @pl.when(is_end)
    def _():
        for step in range(chips):
            for part in range(parts):
                z_copy(part, step).wait_send()

    for array in range(2):
        for step in range(1, chips):
            for part in range(parts):
                forward_copy(array, part, step, core).wait_send()

    def route_pair(step, carry):
        base = lax.rem(chip + chips - step, chips) * 2
        at = pair_rows(step)
        product = times_transposed(acts[0, at, :], wg[...]) + times_transposed(acts[1, at, :], wu[...])
        gs[base] = product[:rows].astype(BF16)
        gs[base + 1] = product[rows:].astype(BF16)
        return carry

    lax.fori_loop(0, chips, route_pair, 0)
    for step in range(1, span):
        back_copy(step).start()

    def pass_gates(i, carry):
        d = order_at(i)

        @pl.when(is_fed(d))
        def _():
            for s in halves:
                gline_wait(d, s)
                grads[d, s] = (grads[d, s].astype(F32) + glines[d, s].astype(F32)).astype(BF16)
                gline_copy(d, s).start()

        return carry

    lax.fori_loop(0, outer - 1, pass_gates, 0)

    def pass_down(i, carry):
        d = order_at(i)
        fed = is_fed_down(d)
        at = d * 2 + side

        @pl.when(jnp.logical_not(is_end))
        def _():
            near_copy(d).wait_recv()

            @pl.when(fed)
            def _():
                dline_wait(d)
                dgrads[at] = (dgrads[at].astype(F32) + dnear[d].astype(F32) + dlines[d].astype(F32)).astype(BF16)

            @pl.when(jnp.logical_not(fed))
            def _():
                dgrads[at] = (dgrads[at].astype(F32) + dnear[d].astype(F32)).astype(BF16)

            dline_copy(d).start()

        return carry

    lax.fori_loop(0, outer - 1, pass_down, 0)
    for step in range(1, span):
        back_copy(step).wait_recv()
    route_sum = gs[expert].astype(F32)
    for step in range(1, span):
        route_sum = route_sum + back[step].astype(F32)
    tok_out[...] = route_sum.astype(BF16)

    cross = remote(cross_out, cross_in, cross_send, cross_recv, {"dp": partner})
    for s in halves:

        @pl.when(line > 0)
        def _():
            gline_wait(line, s)
            total[s] += glines[line, s].astype(F32)

        @pl.when(line < outer - 1)
        def _():
            gline_wait(outer, s)
            total[s] += glines[outer, s].astype(F32)

        if s is halves[0]:
            cross_out[...] = total[s].astype(BF16)
            cross.start()

    near_copy(line).wait_recv()
    down_out[...] = (dgrads[me].astype(F32) + dnear[line].astype(F32)) * inverse

    @pl.when(line > 1)
    def _():
        dline_wait(line)
        down_out[...] += dlines[line].astype(F32) * inverse

    @pl.when(line < outer - 2)
    def _():
        dline_wait(outer)
        down_out[...] += dlines[outer].astype(F32) * inverse

    cross.wait_recv()

    @pl.when(side == 0)
    def _():
        gate_out[...] = total[0] * inverse
        up_out[...] = cross_in[...].astype(F32) * inverse

    @pl.when(side == 1)
    def _():
        up_out[...] = total[1] * inverse
        gate_out[...] = cross_in[...].astype(F32) * inverse

    for step in range(1, span):
        coef_copy(step).wait_send()
        back_copy(step).wait_send()
    for array in range(3):
        core_copy(array).wait_send()
        for step in range(1, chips):
            for part in range(parts):
                chip_copy(array, part, step).wait_send()
                if array == 2:
                    forward_copy(array, part, step, core).wait_send()
    px_copy.wait_send()
    for step in range(chips):
        act_copy(step).wait_send()

    @pl.when(is_end)
    def _():
        for step in range(chips):
            z_hidden(step).wait_send()
        z_coef.wait_send()

    def finish(i, carry):
        d = order_at(i)

        @pl.when(jnp.logical_not(is_end) | (d == line))
        def _():
            near_copy(d).wait_send()

        @pl.when(i < outer - 1)
        def _():
            for s in halves:
                gline_copy(d, s).wait_send()

        @pl.when((i < outer - 1) & jnp.logical_not(is_end))
        def _():
            dline_copy(d).wait_send()

        return carry

    lax.fori_loop(0, outer, finish, 0)
    cross.wait_send()


def fused(tokens, d_out, routes, gates, w_gate, w_up, w_down, span, replicas):
    parts = 4
    dma = pltpu.SemaphoreType.DMA
    rows, width = tokens.shape
    units = w_gate.shape[2]
    outer, chips = replicas // 2, span // 2
    feature, shard = width // replicas, units // replicas
    amount = span * rows
    here = pl.BlockSpec(memory_space=pltpu.VMEM)
    away = pl.BlockSpec(memory_space=pltpu.HBM)
    vmem = pltpu.VMEM
    places = max(8, span)
    return pl.pallas_call(
        functools.partial(kernel, span, replicas, parts),
        out_shape=(
            jax.ShapeDtypeStruct((rows, width), BF16),
            jax.ShapeDtypeStruct((feature, units), F32),
            jax.ShapeDtypeStruct((feature, units), F32),
            jax.ShapeDtypeStruct((shard, width), F32),
        ),
        in_specs=[away, away, here, here, away, away, away],
        out_specs=[here] * 4,
        scratch_shapes=[
            vmem((width, units), BF16), vmem((width, units), BF16), vmem((units, width), BF16),
            vmem((span, rows, width), BF16), vmem((span, rows, width), BF16), vmem((span, rows, width), BF16),
            vmem((amount, width), BF16),
            vmem((places, rows), F32), vmem((span, places, rows), F32),
            vmem((2 * rows, units), F32), vmem((2 * rows, units), F32),
            vmem((2, amount, units), BF16), vmem((amount, units), BF16), vmem((amount, units), BF16),
            vmem((outer, 2, feature, units), BF16), vmem((outer + 1, 2, feature, units), BF16),
            vmem((2, feature, units), F32), vmem((feature, units), BF16), vmem((feature, units), BF16),
            vmem((replicas, shard, width), BF16), vmem((outer, shard, width), BF16),
            vmem((outer + 1, shard, width), BF16),
            vmem((span, rows, width), BF16),
            vmem((span, rows, width), BF16), vmem((span, places, rows), F32), vmem((amount, units), BF16),
            dma((3,)), dma((2,)), dma((span,)), dma((span,)), dma((3,)), dma((3,)),
            dma((3, parts, chips)), dma((3, parts, chips)), dma((3, parts, chips)), dma((3, parts, chips)),
            dma, dma, dma((chips,)), dma((chips,)), dma((outer,)), dma((outer,)),
            dma((outer, 2)), dma((outer + 1, 2)), dma((outer,)), dma((outer + 1,)),
            dma((span,)), dma((span,)), dma, dma,
            dma((parts, chips)), dma((parts, chips)), dma((parts, chips)), dma((parts, chips)),
            dma((chips,)), dma((chips,)), dma, dma,
        ],
        compiler_params=pltpu.CompilerParams(
            collective_id=0, has_side_effects=True, vmem_limit_bytes=62 << 20
        ),
        name="fused",
    )(tokens, d_out, routes, gates, w_gate, w_up, w_down)


def body(tokens, d_out, routes, gate_fixed, w_gate, w_up, w_down):
    span = lax.axis_size("expert")
    replicas = lax.axis_size("dp")
    d_tokens, out_gate, out_up, out_down = fused(
        tokens, d_out, routes.T, gate_fixed.T, w_gate, w_up, w_down, span, replicas
    )
    return d_tokens, out_gate[None], out_up[None], out_down[None]


def solution(mesh):
    rows = P(("dp", "expert"), None)
    whole = P("expert", None, None)
    cut = P("expert", "dp", None)
    return jax.shard_map(
        body, mesh=mesh, in_specs=(rows,) * 4 + (whole,) * 3, out_specs=(rows, cut, cut, cut), check_vma=False
    )
```

```python
import functools

import jax
import jax.numpy as jnp
from jax import lax
from jax.experimental import pallas as pl
from jax.experimental.pallas import tpu as pltpu
from jax.sharding import PartitionSpec as P

MESH = pl.DeviceIdType.MESH
BF16 = jnp.bfloat16
F32 = jnp.float32


def greet(targets):
    barrier = pltpu.get_barrier_semaphore()
    for target in targets:
        pl.semaphore_signal(barrier, inc=1, device_id=target, device_id_type=MESH)
    pl.semaphore_wait(barrier, len(targets))


def outer_product(left, right):
    return lax.dot_general(left, right, (((0,), (0,)), ((), ())), preferred_element_type=F32)


def times_transposed(left, right):
    return lax.dot_general(left, right, (((1,), (1,)), ((), ())), preferred_element_type=F32)


def kernel(
    span, replicas, parts,
    x_ref, g_ref, routes_ref, gates_ref, wg_ref, wu_ref, wd_ref,
    tok_out, gate_out, up_out, down_out,
    wg, wu, wd, xs, gs, px, scaled, coef, cs, for_gate, for_up, acts, pact, hidden,
    grads, glines, total, cross_out, cross_in, dgrads, dnear, dlines, back, zg, zcs, zhid,
    w_sem, own_sem, c_send, c_recv, core_send, core_recv, chip_send, chip_recv, fwd_send, fwd_recv,
    px_send, px_recv, far_send, far_recv, act_send, act_recv, near_send, near_recv, gline_send, gline_recv,
    dline_send, dline_recv, back_send, back_recv, cross_send, cross_recv,
    z_send, z_recv, zf_send, zf_recv, zh_send, zh_recv, zc_send, zc_recv,
):
    expert = lax.axis_index("expert")
    me = lax.axis_index("dp")
    core = lax.rem(expert, 2)
    chip = expert // 2
    other = chip * 2 + (1 - core)
    chips = span // 2
    outer = replicas // 2
    side = lax.rem(me, 2)
    line = me // 2
    partner = line * 2 + (1 - side)
    lower = lax.rem(line + outer - 1, outer) * 2 + side
    upper = lax.rem(line + 1, outer) * 2 + side
    rows, width = x_ref.shape
    units = hidden.shape[1]
    feature = width // replicas
    shard = units // replicas
    piece_rows = rows // parts
    near_parts = parts - 1
    every = range(parts)
    half_rows = rows // 2
    inverse = 1.0 / replicas
    is_end = (line == 0) | (line == outer - 1)
    is_helper = (line == 1) | (line == outer - 2)
    inner = {"dp": jnp.where(line == 0, 1, outer - 2) * 2 + side}
    ended = jnp.where(line == 1, 0, outer - 1)

    own_x = pltpu.make_async_copy(x_ref, xs.at[expert], own_sem.at[0])
    own_g = pltpu.make_async_copy(g_ref, gs.at[expert], own_sem.at[1])
    loads = [
        pltpu.make_async_copy(source.at[0], target, w_sem.at[at])
        for at, (source, target) in enumerate(((wg_ref, wg), (wu_ref, wu), (wd_ref, wd)))
    ]
    own_x.start()
    loads[0].start()
    loads[1].start()
    own_g.start()
    loads[2].start()
    places = lax.broadcasted_iota(jnp.int32, coef.shape, 0)
    value = jnp.zeros(coef.shape, F32)
    for k in range(routes_ref.shape[0]):
        gate_value = gates_ref[k : k + 1, :].astype(F32) / 65536.0
        value = value + jnp.where(places == routes_ref[k : k + 1, :], gate_value, 0.0)
    coef[...] = value
    cs[expert] = value

    targets = [{"expert": lax.rem(expert + step, span)} for step in range(1, span)]
    targets += [{"dp": partner}, {"dp": lower}, {"dp": upper}]
    greet(targets)

    def remote(source, target, send, recv, device):
        return pltpu.make_async_remote_copy(
            src_ref=source, dst_ref=target, send_sem=send, recv_sem=recv, device_id=device, device_id_type=MESH
        )

    def piece(ref, part):
        return ref.at[pl.ds(part * piece_rows, piece_rows)]

    sources = (x_ref, g_ref, px.at[expert])
    arrays = (xs, gs, px)

    def coef_copy(step):
        return remote(
            coef, cs.at[expert], c_send.at[step], c_recv.at[step], {"expert": lax.rem(expert + step, span)}
        )

    def core_copy(array):
        return remote(
            sources[array], arrays[array].at[expert], core_send.at[array], core_recv.at[array], {"expert": other}
        )

    def chip_copy(array, part, step):
        there = lax.rem(chip + step, chips) * 2 + core
        return remote(
            piece(sources[array], part), piece(arrays[array].at[expert], part),
            chip_send.at[array, part, step], chip_recv.at[array, part, step], {"expert": there},
        )

    def forward_copy(array, part, step, at_core):
        owner = lax.rem(chip + chips - step, chips) * 2 + at_core
        block = piece(arrays[array].at[owner], part)
        return remote(
            block, block, fwd_send.at[array, part, step], fwd_recv.at[array, part, step], {"expert": other}
        )

    def far_copy(part, step):
        owner = lax.rem(chip + chips - step, chips) * 2 + core
        return remote(
            piece(xs.at[owner], part), piece(px.at[owner], part),
            far_send.at[part, step], far_recv.at[part, step], {"dp": partner},
        )

    def pass_on(array, step, some):
        for part in some:
            if array == 2 and part >= near_parts:
                far_copy(part, step).wait_recv()
            else:
                chip_copy(array, part, step).wait_recv()
            forward_copy(array, part, step, core).start()
            if array == 0 and part >= near_parts:
                far_copy(part, step).start()
            if array == 1:

                @pl.when(is_end)
                def _():
                    z_copy(part, step).start()

    def take_passed(array, step, some):
        for part in some:
            forward_copy(array, part, step, 1 - core).wait_recv()

    px_copy = remote(x_ref, px.at[expert], px_send, px_recv, {"dp": partner})

    def pair_rows(step):
        base = lax.rem(chip + chips - step, chips) * 2
        return pl.ds(pl.multiple_of(base * rows, 2 * rows), 2 * rows)

    def pair_half(step, at):
        base = lax.rem(chip + chips - step, chips) * 2
        return pl.ds(base, 2), pl.ds(at * half_rows, half_rows)

    def act_copy(step, at):
        owners, those = pair_half(step, at)
        return remote(
            acts.at[1 - side, owners, those], pact.at[owners, those],
            act_send.at[step, at], act_recv.at[step, at], {"dp": partner},
        )

    def back_copy(step):
        there = lax.rem(expert + step, span)
        return remote(gs.at[there], back.at[step], back_send.at[step], back_recv.at[step], {"expert": there})

    upside = line >= outer // 2
    nearest = jnp.where(upside, outer - 1 - line, line)

    def order_at(i):
        j = i + jnp.where(i >= 2 * nearest + 1, 1, 0)
        d = jnp.where(lax.rem(j, 2) == 0, outer - 1 - j // 2, j // 2)
        return jnp.where(i == outer - 1, line, jnp.where(upside, outer - 1 - d, d))

    def is_fed(d):
        return ((d > line) & (line > 0)) | ((d < line) & (line < outer - 1))

    def near_copy(d):
        return remote(
            dgrads.at[d * 2 + (1 - side)], dnear.at[d], near_send.at[d], near_recv.at[d], {"dp": partner}
        )

    def hop(d):
        following = jnp.where(d > line, line + 1, line - 1)
        slot = jnp.where((d < line) & (d == following), outer, d)
        return slot, {"dp": following * 2 + side}

    slices = 2
    slice_rows = feature // slices
    slice_width = width // slices

    def gline_copy(d, s, q):
        slot, device = hop(d)
        those = pl.ds(q * slice_rows, slice_rows)
        return remote(
            grads.at[d, s, those], glines.at[slot, s, those],
            gline_send.at[d, s, q], gline_recv.at[slot, s, q], device,
        )

    def gline_wait(slot, s, q):
        block = glines.at[slot, s, pl.ds(q * slice_rows, slice_rows)]
        remote(block, block, gline_send.at[0, s, q], gline_recv.at[slot, s, q], {"dp": upper}).wait_recv()

    def dline_copy(d, q):
        slot, device = hop(d)
        those = pl.ds(q * slice_width, slice_width)
        return remote(
            dgrads.at[d * 2 + side, :, those], dlines.at[slot, :, those],
            dline_send.at[d, q], dline_recv.at[slot, q], device,
        )

    def dline_wait(slot, q):
        block = dlines.at[slot, :, pl.ds(q * slice_width, slice_width)]
        remote(block, block, dline_send.at[0, q], dline_recv.at[slot, q], {"dp": upper}).wait_recv()

    def is_fed_down(d):
        return ((d > line) & (line > 1)) | ((d < line) & (line < outer - 2))

    def z_copy(part, step):
        owner = lax.rem(chip + chips - step, chips) * 2 + core
        source = g_ref if step == 0 else gs.at[owner]
        return remote(
            piece(source, part), piece(zg.at[owner], part), z_send.at[part, step], z_recv.at[part, step], inner
        )

    def z_forward(part, step, at_core):
        owner = lax.rem(chip + chips - step, chips) * 2 + at_core
        block = piece(zg.at[owner], part)
        return remote(block, block, zf_send.at[part, step], zf_recv.at[part, step], {"expert": other})

    def z_hidden(step):
        at = pair_rows(step)
        return remote(hidden.at[at], zhid.at[at], zh_send.at[step], zh_recv.at[step], inner)

    z_coef = remote(cs, zcs, zc_send, zc_recv, inner)

    halves = (1 - side, side)

    for step in range(1, span):
        coef_copy(step).start()
    for part in range(parts):
        for step in range(1, chips):
            chip_copy(0, part, step).start()
    core_copy(0).start()
    px_copy.start()
    core_copy(1).start()
    for part in range(parts):
        for step in range(1, chips):
            chip_copy(1, part, step).start()

    @pl.when(is_end)
    def _():
        for part in range(parts):
            z_copy(part, 0).start()

    cut = units // 3

    def project(step):
        base = lax.rem(chip + chips - step, chips) * 2
        at = pair_rows(step)
        x = xs[pl.ds(base, 2)].reshape(2 * rows, width)
        for c in range(3):
            columns = slice(c * cut, (c + 1) * cut)
            pre_gate = jnp.dot(x, wg[:, columns], preferred_element_type=F32)
            pre_up = jnp.dot(x, wu[:, columns], preferred_element_type=F32)
            sigmoid_gate = 1.0 / (1.0 + jnp.exp(-pre_gate))
            silu_gate = pre_gate * sigmoid_gate
            hidden[at, columns] = (silu_gate * pre_up).astype(BF16)
            for_up[:, :, columns] = silu_gate.reshape(2, rows, cut)
            for_gate[:, :, columns] = (
                pre_up * sigmoid_gate * (1.0 + pre_gate * (1.0 - sigmoid_gate))
            ).reshape(2, rows, cut)

        @pl.when(is_end)
        def _():
            z_hidden(step).start()

    def weights(coefs, owner):
        row = lax.broadcasted_iota(jnp.int32, (rows, rows), 0)
        diagonal = row == lax.broadcasted_iota(jnp.int32, (rows, rows), 1)
        return jnp.sum(jnp.where(diagonal, coefs[owner, pl.ds(expert, 1), :], 0.0), axis=1, keepdims=True)

    def differentiate(step, at):
        base = lax.rem(chip + chips - step, chips) * 2
        owners, those = pair_half(step, at)
        for j in range(2):
            weight = weights(cs, base + j)[at * half_rows : (at + 1) * half_rows]
            scaled[base + j, those] = (weight * gs[base + j, those].astype(F32)).astype(BF16)
        block = scaled[owners, those].reshape(2 * half_rows, width)
        for c in range(3):
            columns = slice(c * cut, (c + 1) * cut)
            d_hidden = times_transposed(block, wd[columns, :]).reshape(2, half_rows, cut)
            acts[0, owners, those, columns] = (d_hidden * for_gate[:, those, columns]).astype(BF16)
            acts[1, owners, those, columns] = (d_hidden * for_up[:, those, columns]).astype(BF16)
        act_copy(step, at).start()

    own_x.wait()
    loads[0].wait()
    loads[1].wait()
    core_copy(0).wait_recv()
    project(0)
    own_g.wait()
    loads[2].wait()
    core_copy(1).wait_recv()
    for step in range(1, span):
        coef_copy(step).wait_recv()

    @pl.when(is_end)
    def _():
        z_coef.start()

    for at in range(2):
        differentiate(0, at)
    px_copy.wait_recv()
    core_copy(2).start()
    for step in range(1, chips):
        pass_on(0, step, every)
        take_passed(0, step, every)
        project(step)
        if step == 1:
            for part in range(near_parts):
                for later in range(1, chips):
                    chip_copy(2, part, later).start()
        for at in range(2):
            some = every[at * parts // 2 : (at + 1) * parts // 2]
            pass_on(1, step, some)
            take_passed(1, step, some)
            differentiate(step, at)

    for step in range(1, chips):
        pass_on(2, step, every)
    for step in range(1, chips):
        take_passed(2, step, every)
    core_copy(2).wait_recv()
    for step in range(chips):
        for at in range(2):
            act_copy(step, at).wait_recv()

    def product_at(d):
        columns = pl.ds(pl.multiple_of(d * 2 * feature, 2 * feature), 2 * feature)
        return outer_product(
            xs[:, :, columns].reshape(span * rows, 2 * feature), acts[side].reshape(span * rows, units)
        ) + outer_product(
            px[:, :, columns].reshape(span * rows, 2 * feature), pact[...].reshape(span * rows, units)
        )

    def make(i, carry):
        d = order_at(i)
        product = product_at(d)
        grads[d, 0] = product[:feature].astype(BF16)
        grads[d, 1] = product[feature:].astype(BF16)

        @pl.when(jnp.logical_not(is_fed(d)))
        def _():
            for s in halves:
                for q in range(slices):
                    gline_copy(d, s, q).start()

        return carry

    lax.fori_loop(0, outer - 1, make, 0)
    product = product_at(line)
    total[0] = product[:feature]
    total[1] = product[feature:]

    half = units // 2

    def down(helps):
        for part in range(2):
            columns = slice(part * half, (part + 1) * half)
            product = outer_product(hidden[:, columns], scaled[...].reshape(span * rows, width))
            if helps:
                product = product + outer_product(zhid[:, columns], zg[...].reshape(span * rows, width))
            for at in range(half // shard):
                dgrads[part * (half // shard) + at] = product[at * shard : (at + 1) * shard].astype(BF16)

    @pl.when(is_helper)
    def _():
        for step in range(chips):
            for part in range(parts):
                z_copy(part, step).wait_recv()
                z_forward(part, step, core).start()
        z_coef.wait_recv()
        column = lax.broadcasted_iota(jnp.int32, (1, units), 1) // (2 * shard)
        kept = jnp.where(column == ended, 0.0, 1.0).astype(BF16)
        for step in range(chips):
            z_hidden(step).wait_recv()
        zhid[...] = zhid[...] * kept
        for step in range(chips):
            for part in range(parts):
                z_forward(part, step, core).wait_send()
                z_forward(part, step, 1 - core).wait_recv()
        for owner in range(span):
            zg[owner] = (weights(zcs, owner) * zg[owner].astype(F32)).astype(BF16)
        down(True)

    @pl.when(jnp.logical_not(is_helper))
    def _():
        down(False)

    def start_near(i, carry):
        d = order_at(i)

        @pl.when(jnp.logical_not(is_end) | (d == line))
        def _():
            near_copy(d).start()

        return carry

    lax.fori_loop(0, outer, start_near, 0)

    @pl.when(is_end)
    def _():
        for step in range(chips):
            for part in range(parts):
                z_copy(part, step).wait_send()

    for array in range(2):
        for step in range(1, chips):
            for part in range(parts):
                forward_copy(array, part, step, core).wait_send()

    def route_pair(step, carry):
        base = lax.rem(chip + chips - step, chips) * 2
        pair = acts[:, pl.ds(base, 2)].reshape(2, 2 * rows, units)
        product = times_transposed(pair[0], wg[...]) + times_transposed(pair[1], wu[...])
        gs[base] = product[:rows].astype(BF16)
        gs[base + 1] = product[rows:].astype(BF16)
        return carry

    lax.fori_loop(0, chips, route_pair, 0)
    for step in range(1, span):
        back_copy(step).start()

    def pass_gates(i, carry):
        d = order_at(i)

        @pl.when(is_fed(d))
        def _():
            for s in halves:
                for q in range(slices):
                    those = pl.ds(q * slice_rows, slice_rows)
                    gline_wait(d, s, q)
                    grads[d, s, those] = (grads[d, s, those].astype(F32) + glines[d, s, those].astype(F32)).astype(BF16)
                    gline_copy(d, s, q).start()

        return carry

    lax.fori_loop(0, outer - 1, pass_gates, 0)

    def pass_down(i, carry):
        d = order_at(i)
        fed = is_fed_down(d)
        at = d * 2 + side

        @pl.when(jnp.logical_not(is_end))
        def _():
            near_copy(d).wait_recv()

            for q in range(slices):
                those = slice(q * slice_width, (q + 1) * slice_width)

                @pl.when(fed)
                def _():
                    dline_wait(d, q)
                    dgrads[at, :, those] = (
                        dgrads[at, :, those].astype(F32) + dnear[d, :, those].astype(F32) + dlines[d, :, those].astype(F32)
                    ).astype(BF16)

                @pl.when(jnp.logical_not(fed))
                def _():
                    dgrads[at, :, those] = (
                        dgrads[at, :, those].astype(F32) + dnear[d, :, those].astype(F32)
                    ).astype(BF16)

                dline_copy(d, q).start()

        return carry

    lax.fori_loop(0, outer - 1, pass_down, 0)
    for step in range(1, span):
        back_copy(step).wait_recv()
    route_sum = gs[expert].astype(F32)
    for step in range(1, span):
        route_sum = route_sum + back[step].astype(F32)
    tok_out[...] = route_sum.astype(BF16)

    cross = remote(cross_out, cross_in, cross_send, cross_recv, {"dp": partner})
    for s in halves:

        @pl.when(line > 0)
        def _():
            for q in range(slices):
                gline_wait(line, s, q)
            total[s] += glines[line, s].astype(F32)

        @pl.when(line < outer - 1)
        def _():
            for q in range(slices):
                gline_wait(outer, s, q)
            total[s] += glines[outer, s].astype(F32)

        if s is halves[0]:
            cross_out[...] = total[s].astype(BF16)
            cross.start()

    near_copy(line).wait_recv()
    down_out[...] = (dgrads[me].astype(F32) + dnear[line].astype(F32)) * inverse

    @pl.when(line > 1)
    def _():
        for q in range(slices):
            those = slice(q * slice_width, (q + 1) * slice_width)
            dline_wait(line, q)
            down_out[:, those] += dlines[line, :, those].astype(F32) * inverse

    @pl.when(line < outer - 2)
    def _():
        for q in range(slices):
            those = slice(q * slice_width, (q + 1) * slice_width)
            dline_wait(outer, q)
            down_out[:, those] += dlines[outer, :, those].astype(F32) * inverse

    cross.wait_recv()

    @pl.when(side == 0)
    def _():
        gate_out[...] = total[0] * inverse
        up_out[...] = cross_in[...].astype(F32) * inverse

    @pl.when(side == 1)
    def _():
        up_out[...] = total[1] * inverse
        gate_out[...] = cross_in[...].astype(F32) * inverse

    for step in range(1, span):
        coef_copy(step).wait_send()
        back_copy(step).wait_send()
    for array in range(3):
        core_copy(array).wait_send()
        for step in range(1, chips):
            for part in range(near_parts if array == 2 else parts):
                chip_copy(array, part, step).wait_send()
    for step in range(1, chips):
        for part in range(parts):
            forward_copy(2, part, step, core).wait_send()
            if part >= near_parts:
                far_copy(part, step).wait_send()
    px_copy.wait_send()
    for step in range(chips):
        for at in range(2):
            act_copy(step, at).wait_send()

    @pl.when(is_end)
    def _():
        for step in range(chips):
            z_hidden(step).wait_send()
        z_coef.wait_send()

    def finish(i, carry):
        d = order_at(i)

        @pl.when(jnp.logical_not(is_end) | (d == line))
        def _():
            near_copy(d).wait_send()

        @pl.when(i < outer - 1)
        def _():
            for s in halves:
                for q in range(slices):
                    gline_copy(d, s, q).wait_send()

        @pl.when((i < outer - 1) & jnp.logical_not(is_end))
        def _():
            for q in range(slices):
                dline_copy(d, q).wait_send()

        return carry

    lax.fori_loop(0, outer, finish, 0)
    cross.wait_send()


def fused(tokens, d_out, routes, gates, w_gate, w_up, w_down, span, replicas):
    parts = 4
    dma = pltpu.SemaphoreType.DMA
    rows, width = tokens.shape
    units = w_gate.shape[2]
    outer, chips = replicas // 2, span // 2
    feature, shard = width // replicas, units // replicas
    amount = span * rows
    here = pl.BlockSpec(memory_space=pltpu.VMEM)
    away = pl.BlockSpec(memory_space=pltpu.HBM)
    vmem = pltpu.VMEM
    places = max(8, span)
    return pl.pallas_call(
        functools.partial(kernel, span, replicas, parts),
        out_shape=(
            vmem((rows, width), BF16), vmem((feature, units), F32), vmem((feature, units), F32),
            vmem((shard, width), F32),
        ),
        in_specs=[away, away, here, here, away, away, away],
        out_specs=[here] * 4,
        scratch_shapes=[
            vmem((width, units), BF16), vmem((width, units), BF16), vmem((units, width), BF16),
            vmem((span, rows, width), BF16), vmem((span, rows, width), BF16), vmem((span, rows, width), BF16),
            vmem((span, rows, width), BF16),
            vmem((places, rows), F32), vmem((span, places, rows), F32),
            vmem((2, rows, units), F32), vmem((2, rows, units), F32),
            vmem((2, span, rows, units), BF16), vmem((span, rows, units), BF16), vmem((amount, units), BF16),
            vmem((outer, 2, feature, units), BF16), vmem((outer + 1, 2, feature, units), BF16),
            vmem((2, feature, units), F32), vmem((feature, units), BF16), vmem((feature, units), BF16),
            vmem((replicas, shard, width), BF16), vmem((outer, shard, width), BF16),
            vmem((outer + 1, shard, width), BF16),
            vmem((span, rows, width), BF16),
            vmem((span, rows, width), BF16), vmem((span, places, rows), F32), vmem((amount, units), BF16),
            dma((3,)), dma((2,)), dma((span,)), dma((span,)), dma((3,)), dma((3,)),
            dma((3, parts, chips)), dma((3, parts, chips)), dma((3, parts, chips)), dma((3, parts, chips)),
            dma, dma, dma((parts, chips)), dma((parts, chips)), dma((chips, 2)), dma((chips, 2)),
            dma((outer,)), dma((outer,)),
            dma((outer, 2, 2)), dma((outer + 1, 2, 2)), dma((outer, 2)), dma((outer + 1, 2)),
            dma((span,)), dma((span,)), dma, dma,
            dma((parts, chips)), dma((parts, chips)), dma((parts, chips)), dma((parts, chips)),
            dma((chips,)), dma((chips,)), dma, dma,
        ],
        compiler_params=pltpu.CompilerParams(
            collective_id=0, has_side_effects=True, vmem_limit_bytes=(54 + span) << 20
        ),
        name="fused",
    )(tokens, d_out, routes, gates, w_gate, w_up, w_down)


def store_kernel(*refs):
    sources, targets, sem = refs[:4], refs[4:8], refs[8]
    copies = [
        pltpu.make_async_copy(source, target if at == 0 else target.at[0], sem.at[at])
        for at, (source, target) in enumerate(zip(sources, targets))
    ]
    for copy in copies:
        copy.start()
    for copy in copies:
        copy.wait()


def store(arrays):
    shapes = [arrays[0].shape] + [(1,) + a.shape for a in arrays[1:]]
    return pl.pallas_call(
        store_kernel,
        out_shape=tuple(jax.ShapeDtypeStruct(s, a.dtype) for s, a in zip(shapes, arrays)),
        in_specs=[pl.BlockSpec(memory_space=pltpu.VMEM)] * 4,
        out_specs=[pl.BlockSpec(memory_space=pltpu.HBM)] * 4,
        scratch_shapes=[pltpu.SemaphoreType.DMA((4,))],
        compiler_params=pltpu.CompilerParams(vmem_limit_bytes=1 << 20),
        name="store",
    )(*arrays)


def body(tokens, d_out, routes, gate_fixed, w_gate, w_up, w_down):
    span = lax.axis_size("expert")
    replicas = lax.axis_size("dp")
    return store(fused(tokens, d_out, routes.T, gate_fixed.T, w_gate, w_up, w_down, span, replicas))


def solution(mesh):
    rows = P(("dp", "expert"), None)
    whole = P("expert", None, None)
    cut = P("expert", "dp", None)
    return jax.shard_map(
        body, mesh=mesh, in_specs=(rows,) * 4 + (whole,) * 3, out_specs=(rows, cut, cut, cut), check_vma=False
    )
```

```python
import functools

import jax
import jax.numpy as jnp
from jax import lax
from jax.experimental import pallas as pl
from jax.experimental.pallas import tpu as pltpu
from jax.sharding import PartitionSpec as P

MESH = pl.DeviceIdType.MESH
BF16 = jnp.bfloat16
F32 = jnp.float32


def greet(targets):
    barrier = pltpu.get_barrier_semaphore()
    for target in targets:
        pl.semaphore_signal(barrier, inc=1, device_id=target, device_id_type=MESH)
    pl.semaphore_wait(barrier, len(targets))


def outer_product(left, right):
    return lax.dot_general(left, right, (((0,), (0,)), ((), ())), preferred_element_type=F32)


def times_transposed(left, right):
    return lax.dot_general(left, right, (((1,), (1,)), ((), ())), preferred_element_type=F32)


def kernel(
    span, replicas, parts,
    x_ref, g_ref, routes_ref, gates_ref, wg_ref, wu_ref, wd_ref,
    tok_out, gate_out, up_out, down_out,
    wg, wu, wd, xs, gs, px, scaled, coef, cs, for_gate, for_up, acts, pact, hidden,
    grads, glines, total, cross_out, cross_in, dgrads, dnear, dlines, back, zg, zcs, zhid,
    w_sem, own_sem, c_send, c_recv, core_send, core_recv, chip_send, chip_recv, fwd_send, fwd_recv,
    px_send, px_recv, far_send, far_recv, act_send, act_recv, near_send, near_recv, gline_send, gline_recv,
    dline_send, dline_recv, back_send, back_recv, cross_send, cross_recv,
    z_send, z_recv, zh_send, zh_recv, zc_send, zc_recv,
):
    expert = lax.axis_index("expert")
    me = lax.axis_index("dp")
    core = lax.rem(expert, 2)
    chip = expert // 2
    other = chip * 2 + (1 - core)
    chips = span // 2
    outer = replicas // 2
    side = lax.rem(me, 2)
    line = me // 2
    partner = line * 2 + (1 - side)
    lower = lax.rem(line + outer - 1, outer) * 2 + side
    upper = lax.rem(line + 1, outer) * 2 + side
    rows, width = x_ref.shape
    units = hidden.shape[1]
    feature = width // replicas
    shard = units // replicas
    piece_rows = rows // parts
    near_parts = parts - 1
    every = range(parts)
    half_rows = rows // 2
    inverse = 1.0 / replicas
    is_end = (line == 0) | (line == outer - 1)
    is_helper = (line == 1) | (line == outer - 2)
    inner = {"dp": jnp.where(line == 0, 1, outer - 2) * 2 + side}
    ended = jnp.where(line == 1, 0, outer - 1)

    own_x = pltpu.make_async_copy(x_ref, xs.at[expert], own_sem.at[0])
    own_g = pltpu.make_async_copy(g_ref, gs.at[expert], own_sem.at[1])
    loads = [
        pltpu.make_async_copy(source.at[0], target, w_sem.at[at])
        for at, (source, target) in enumerate(((wg_ref, wg), (wu_ref, wu), (wd_ref, wd)))
    ]
    own_x.start()
    loads[0].start()
    loads[1].start()
    own_g.start()
    loads[2].start()
    places = lax.broadcasted_iota(jnp.int32, coef.shape, 0)
    value = jnp.zeros(coef.shape, F32)
    for k in range(routes_ref.shape[0]):
        gate_value = gates_ref[k : k + 1, :].astype(F32) / 65536.0
        value = value + jnp.where(places == routes_ref[k : k + 1, :], gate_value, 0.0)
    coef[...] = value
    cs[expert] = value

    targets = [{"expert": lax.rem(expert + step, span)} for step in range(1, span)]
    targets += [{"dp": partner}, {"dp": lower}, {"dp": upper}]
    greet(targets)

    def remote(source, target, send, recv, device):
        return pltpu.make_async_remote_copy(
            src_ref=source, dst_ref=target, send_sem=send, recv_sem=recv, device_id=device, device_id_type=MESH
        )

    def piece(ref, part):
        return ref.at[pl.ds(part * piece_rows, piece_rows)]

    sources = (x_ref, g_ref, px.at[expert], zg.at[expert])
    arrays = (xs, gs, px, zg)

    def coef_copy(step):
        return remote(
            coef, cs.at[expert], c_send.at[step], c_recv.at[step], {"expert": lax.rem(expert + step, span)}
        )

    def core_copy(array):
        return remote(
            sources[array], arrays[array].at[expert], core_send.at[array], core_recv.at[array], {"expert": other}
        )

    def chip_copy(array, part, step):
        there = lax.rem(chip + step, chips) * 2 + core
        return remote(
            piece(sources[array], part), piece(arrays[array].at[expert], part),
            chip_send.at[array, part, step], chip_recv.at[array, part, step], {"expert": there},
        )

    def forward_copy(array, part, step, at_core):
        owner = lax.rem(chip + chips - step, chips) * 2 + at_core
        block = piece(arrays[array].at[owner], part)
        return remote(
            block, block, fwd_send.at[array, part, step], fwd_recv.at[array, part, step], {"expert": other}
        )

    def far_copy(part, step):
        owner = lax.rem(chip + chips - step, chips) * 2 + core
        return remote(
            piece(xs.at[owner], part), piece(px.at[owner], part),
            far_send.at[part, step], far_recv.at[part, step], {"dp": partner},
        )

    def pass_on(array, step, some):
        for part in some:
            if array == 2 and part >= near_parts:
                far_copy(part, step).wait_recv()
            else:
                chip_copy(array, part, step).wait_recv()
            forward_copy(array, part, step, core).start()
            if array == 0 and part >= near_parts:
                far_copy(part, step).start()

    def take_passed(array, step, some):
        for part in some:
            forward_copy(array, part, step, 1 - core).wait_recv()

    px_copy = remote(x_ref, px.at[expert], px_send, px_recv, {"dp": partner})

    def pair_rows(step):
        base = lax.rem(chip + chips - step, chips) * 2
        return pl.ds(pl.multiple_of(base * rows, 2 * rows), 2 * rows)

    def pair_half(step, at):
        base = lax.rem(chip + chips - step, chips) * 2
        return pl.ds(base, 2), pl.ds(at * half_rows, half_rows)

    def act_copy(step, at):
        owners, those = pair_half(step, at)
        return remote(
            acts.at[1 - side, owners, those], pact.at[owners, those],
            act_send.at[step, at], act_recv.at[step, at], {"dp": partner},
        )

    def back_copy(step):
        there = lax.rem(expert + step, span)
        return remote(gs.at[there], back.at[step], back_send.at[step], back_recv.at[step], {"expert": there})

    upside = line >= outer // 2
    nearest = jnp.where(upside, outer - 1 - line, line)

    def order_at(i):
        j = i + jnp.where(i >= 2 * nearest + 1, 1, 0)
        d = jnp.where(lax.rem(j, 2) == 0, outer - 1 - j // 2, j // 2)
        return jnp.where(i == outer - 1, line, jnp.where(upside, outer - 1 - d, d))

    def is_fed(d):
        return ((d > line) & (line > 0)) | ((d < line) & (line < outer - 1))

    def near_copy(d):
        return remote(
            dgrads.at[d * 2 + (1 - side)], dnear.at[d], near_send.at[d], near_recv.at[d], {"dp": partner}
        )

    def hop(d):
        following = jnp.where(d > line, line + 1, line - 1)
        slot = jnp.where((d < line) & (d == following), outer, d)
        return slot, {"dp": following * 2 + side}

    slices = 2
    slice_rows = feature // slices
    slice_width = width // slices

    def gline_copy(d, s, q):
        slot, device = hop(d)
        those = pl.ds(q * slice_rows, slice_rows)
        return remote(
            grads.at[d, s, those], glines.at[slot, s, those],
            gline_send.at[d, s, q], gline_recv.at[slot, s, q], device,
        )

    def gline_wait(slot, s, q):
        block = glines.at[slot, s, pl.ds(q * slice_rows, slice_rows)]
        remote(block, block, gline_send.at[0, s, q], gline_recv.at[slot, s, q], {"dp": upper}).wait_recv()

    def dline_copy(d, q):
        slot, device = hop(d)
        those = pl.ds(q * slice_width, slice_width)
        return remote(
            dgrads.at[d * 2 + side, :, those], dlines.at[slot, :, those],
            dline_send.at[d, q], dline_recv.at[slot, q], device,
        )

    def dline_wait(slot, q):
        block = dlines.at[slot, :, pl.ds(q * slice_width, slice_width)]
        remote(block, block, dline_send.at[0, q], dline_recv.at[slot, q], {"dp": upper}).wait_recv()

    def is_fed_down(d):
        return ((d > line) & (line > 1)) | ((d < line) & (line < outer - 2))

    z_copy = remote(g_ref, zg.at[expert], z_send, z_recv, inner)

    def z_hidden(step):
        at = pair_rows(step)
        return remote(hidden.at[at], zhid.at[at], zh_send.at[step], zh_recv.at[step], inner)

    z_coef = remote(cs, zcs, zc_send, zc_recv, inner)

    halves = (1 - side, side)

    for step in range(1, span):
        coef_copy(step).start()
    for part in range(parts):
        for step in range(1, chips):
            chip_copy(0, part, step).start()
    core_copy(0).start()
    px_copy.start()
    core_copy(1).start()
    for part in range(parts):
        for step in range(1, chips):
            chip_copy(1, part, step).start()

    @pl.when(is_end)
    def _():
        z_copy.start()

    cut = units // 3

    def project(step):
        base = lax.rem(chip + chips - step, chips) * 2
        at = pair_rows(step)
        x = xs[pl.ds(base, 2)].reshape(2 * rows, width)
        for c in range(3):
            columns = slice(c * cut, (c + 1) * cut)
            pre_gate = jnp.dot(x, wg[:, columns], preferred_element_type=F32)
            pre_up = jnp.dot(x, wu[:, columns], preferred_element_type=F32)
            sigmoid_gate = 1.0 / (1.0 + jnp.exp(-pre_gate))
            silu_gate = pre_gate * sigmoid_gate
            hidden[at, columns] = (silu_gate * pre_up).astype(BF16)
            for_up[:, :, columns] = silu_gate.reshape(2, rows, cut)
            for_gate[:, :, columns] = (
                pre_up * sigmoid_gate * (1.0 + pre_gate * (1.0 - sigmoid_gate))
            ).reshape(2, rows, cut)

        @pl.when(is_end)
        def _():
            z_hidden(step).start()

    def weights(coefs, owner):
        row = lax.broadcasted_iota(jnp.int32, (rows, rows), 0)
        diagonal = row == lax.broadcasted_iota(jnp.int32, (rows, rows), 1)
        return jnp.sum(jnp.where(diagonal, coefs[owner, pl.ds(expert, 1), :], 0.0), axis=1, keepdims=True)

    def differentiate(step, at):
        base = lax.rem(chip + chips - step, chips) * 2
        owners, those = pair_half(step, at)
        for j in range(2):
            weight = weights(cs, base + j)[at * half_rows : (at + 1) * half_rows]
            scaled[base + j, those] = (weight * gs[base + j, those].astype(F32)).astype(BF16)
        block = scaled[owners, those].reshape(2 * half_rows, width)
        for c in range(3):
            columns = slice(c * cut, (c + 1) * cut)
            d_hidden = times_transposed(block, wd[columns, :]).reshape(2, half_rows, cut)
            acts[0, owners, those, columns] = (d_hidden * for_gate[:, those, columns]).astype(BF16)
            acts[1, owners, those, columns] = (d_hidden * for_up[:, those, columns]).astype(BF16)
        act_copy(step, at).start()

    own_x.wait()
    loads[0].wait()
    loads[1].wait()
    core_copy(0).wait_recv()
    project(0)
    own_g.wait()
    loads[2].wait()
    core_copy(1).wait_recv()
    for step in range(1, span):
        coef_copy(step).wait_recv()

    @pl.when(is_end)
    def _():
        z_coef.start()

    for at in range(2):
        differentiate(0, at)
    px_copy.wait_recv()
    core_copy(2).start()
    for step in range(1, chips):
        pass_on(0, step, every)
        take_passed(0, step, every)
        project(step)
        if step == 1:
            for part in range(near_parts):
                for later in range(1, chips):
                    chip_copy(2, part, later).start()

            @pl.when(is_helper)
            def _():
                z_copy.wait_recv()
                core_copy(3).start()
                for part in range(parts):
                    for later in range(1, chips):
                        chip_copy(3, part, later).start()

        for at in range(2):
            some = every[at * parts // 2 : (at + 1) * parts // 2]
            pass_on(1, step, some)
            take_passed(1, step, some)
            differentiate(step, at)

    for step in range(1, chips):
        pass_on(2, step, every)
    for step in range(1, chips):
        take_passed(2, step, every)
    core_copy(2).wait_recv()
    for step in range(chips):
        for at in range(2):
            act_copy(step, at).wait_recv()

    def product_at(d):
        columns = pl.ds(pl.multiple_of(d * 2 * feature, 2 * feature), 2 * feature)
        return outer_product(
            xs[:, :, columns].reshape(span * rows, 2 * feature), acts[side].reshape(span * rows, units)
        ) + outer_product(
            px[:, :, columns].reshape(span * rows, 2 * feature), pact[...].reshape(span * rows, units)
        )

    def make(i, carry):
        d = order_at(i)
        product = product_at(d)
        grads[d, 0] = product[:feature].astype(BF16)
        grads[d, 1] = product[feature:].astype(BF16)

        @pl.when(jnp.logical_not(is_fed(d)))
        def _():
            for s in halves:
                for q in range(slices):
                    gline_copy(d, s, q).start()

        return carry

    lax.fori_loop(0, outer - 1, make, 0)
    product = product_at(line)
    total[0] = product[:feature]
    total[1] = product[feature:]

    half = units // 2

    def down(helps):
        for part in range(2):
            columns = slice(part * half, (part + 1) * half)
            product = outer_product(hidden[:, columns], scaled[...].reshape(span * rows, width))
            if helps:
                product = product + outer_product(zhid[:, columns], zg[...].reshape(span * rows, width))
            for at in range(half // shard):
                dgrads[part * (half // shard) + at] = product[at * shard : (at + 1) * shard].astype(BF16)

    @pl.when(is_helper)
    def _():
        z_coef.wait_recv()
        column = lax.broadcasted_iota(jnp.int32, (1, units), 1) // (2 * shard)
        kept = jnp.where(column == ended, 0.0, 1.0).astype(BF16)
        for step in range(chips):
            z_hidden(step).wait_recv()
        zhid[...] = zhid[...] * kept
        for step in range(1, chips):
            pass_on(3, step, every)
        for step in range(1, chips):
            take_passed(3, step, every)
            for part in range(parts):
                forward_copy(3, part, step, core).wait_send()
                chip_copy(3, part, step).wait_send()
        core_copy(3).wait()
        for owner in range(span):
            zg[owner] = (weights(zcs, owner) * zg[owner].astype(F32)).astype(BF16)
        down(True)

    @pl.when(jnp.logical_not(is_helper))
    def _():
        down(False)

    def start_near(i, carry):
        d = order_at(i)

        @pl.when(jnp.logical_not(is_end) | (d == line))
        def _():
            near_copy(d).start()

        return carry

    lax.fori_loop(0, outer, start_near, 0)

    for array in range(2):
        for step in range(1, chips):
            for part in range(parts):
                forward_copy(array, part, step, core).wait_send()

    def route_pair(step, carry):
        base = lax.rem(chip + chips - step, chips) * 2
        pair = acts[:, pl.ds(base, 2)].reshape(2, 2 * rows, units)
        product = times_transposed(pair[0], wg[...]) + times_transposed(pair[1], wu[...])
        gs[base] = product[:rows].astype(BF16)
        gs[base + 1] = product[rows:].astype(BF16)
        return carry

    lax.fori_loop(0, chips, route_pair, 0)
    for step in range(1, span):
        back_copy(step).start()

    def pass_gates(i, carry):
        d = order_at(i)

        @pl.when(is_fed(d))
        def _():
            for s in halves:
                for q in range(slices):
                    those = pl.ds(q * slice_rows, slice_rows)
                    gline_wait(d, s, q)
                    grads[d, s, those] = (grads[d, s, those].astype(F32) + glines[d, s, those].astype(F32)).astype(BF16)
                    gline_copy(d, s, q).start()

        return carry

    lax.fori_loop(0, outer - 1, pass_gates, 0)

    for step in range(1, span):
        back_copy(step).wait_recv()
    route_sum = gs[expert].astype(F32)
    for step in range(1, span):
        route_sum = route_sum + back[step].astype(F32)
    tok_out[...] = route_sum.astype(BF16)

    def start_down(i, carry):
        d = order_at(i)
        at = d * 2 + side

        @pl.when(jnp.logical_not(is_end | is_fed_down(d)))
        def _():
            near_copy(d).wait_recv()
            for q in range(slices):
                those = slice(q * slice_width, (q + 1) * slice_width)
                dgrads[at, :, those] = (
                    dgrads[at, :, those].astype(F32) + dnear[d, :, those].astype(F32)
                ).astype(BF16)
                dline_copy(d, q).start()

        return carry

    lax.fori_loop(0, outer - 1, start_down, 0)

    cross = remote(cross_out, cross_in, cross_send, cross_recv, {"dp": partner})
    for s in halves:

        @pl.when(line > 0)
        def _():
            for q in range(slices):
                gline_wait(line, s, q)
            total[s] += glines[line, s].astype(F32)

        @pl.when(line < outer - 1)
        def _():
            for q in range(slices):
                gline_wait(outer, s, q)
            total[s] += glines[outer, s].astype(F32)

        if s is halves[0]:
            cross_out[...] = total[s].astype(BF16)
            cross.start()

    def pass_down(i, carry):
        d = order_at(i)
        at = d * 2 + side

        @pl.when(jnp.logical_not(is_end) & is_fed_down(d))
        def _():
            near_copy(d).wait_recv()
            for q in range(slices):
                those = slice(q * slice_width, (q + 1) * slice_width)
                dline_wait(d, q)
                dgrads[at, :, those] = (
                    dgrads[at, :, those].astype(F32) + dnear[d, :, those].astype(F32) + dlines[d, :, those].astype(F32)
                ).astype(BF16)
                dline_copy(d, q).start()

        return carry

    lax.fori_loop(0, outer - 1, pass_down, 0)

    near_copy(line).wait_recv()
    down_out[...] = (dgrads[me].astype(F32) + dnear[line].astype(F32)) * inverse

    @pl.when(line > 1)
    def _():
        for q in range(slices):
            those = slice(q * slice_width, (q + 1) * slice_width)
            dline_wait(line, q)
            down_out[:, those] += dlines[line, :, those].astype(F32) * inverse

    @pl.when(line < outer - 2)
    def _():
        for q in range(slices):
            those = slice(q * slice_width, (q + 1) * slice_width)
            dline_wait(outer, q)
            down_out[:, those] += dlines[outer, :, those].astype(F32) * inverse

    cross.wait_recv()

    @pl.when(side == 0)
    def _():
        gate_out[...] = total[0] * inverse
        up_out[...] = cross_in[...].astype(F32) * inverse

    @pl.when(side == 1)
    def _():
        up_out[...] = total[1] * inverse
        gate_out[...] = cross_in[...].astype(F32) * inverse

    for step in range(1, span):
        coef_copy(step).wait_send()
        back_copy(step).wait_send()
    for array in range(3):
        core_copy(array).wait_send()
        for step in range(1, chips):
            for part in range(near_parts if array == 2 else parts):
                chip_copy(array, part, step).wait_send()
    for step in range(1, chips):
        for part in range(parts):
            forward_copy(2, part, step, core).wait_send()
            if part >= near_parts:
                far_copy(part, step).wait_send()
    px_copy.wait_send()
    for step in range(chips):
        for at in range(2):
            act_copy(step, at).wait_send()

    @pl.when(is_end)
    def _():
        for step in range(chips):
            z_hidden(step).wait_send()
        z_copy.wait_send()
        z_coef.wait_send()

    def finish(i, carry):
        d = order_at(i)

        @pl.when(jnp.logical_not(is_end) | (d == line))
        def _():
            near_copy(d).wait_send()

        @pl.when(i < outer - 1)
        def _():
            for s in halves:
                for q in range(slices):
                    gline_copy(d, s, q).wait_send()

        @pl.when((i < outer - 1) & jnp.logical_not(is_end))
        def _():
            for q in range(slices):
                dline_copy(d, q).wait_send()

        return carry

    lax.fori_loop(0, outer, finish, 0)
    cross.wait_send()


def fused(tokens, d_out, routes, gates, w_gate, w_up, w_down, span, replicas):
    parts = 4
    dma = pltpu.SemaphoreType.DMA
    rows, width = tokens.shape
    units = w_gate.shape[2]
    outer, chips = replicas // 2, span // 2
    feature, shard = width // replicas, units // replicas
    amount = span * rows
    here = pl.BlockSpec(memory_space=pltpu.VMEM)
    away = pl.BlockSpec(memory_space=pltpu.HBM)
    vmem = pltpu.VMEM
    places = max(8, span)
    return pl.pallas_call(
        functools.partial(kernel, span, replicas, parts),
        out_shape=(
            vmem((rows, width), BF16), vmem((feature, units), F32), vmem((feature, units), F32),
            vmem((shard, width), F32),
        ),
        in_specs=[away, away, here, here, away, away, away],
        out_specs=[here] * 4,
        scratch_shapes=[
            vmem((width, units), BF16), vmem((width, units), BF16), vmem((units, width), BF16),
            vmem((span, rows, width), BF16), vmem((span, rows, width), BF16), vmem((span, rows, width), BF16),
            vmem((span, rows, width), BF16),
            vmem((places, rows), F32), vmem((span, places, rows), F32),
            vmem((2, rows, units), F32), vmem((2, rows, units), F32),
            vmem((2, span, rows, units), BF16), vmem((span, rows, units), BF16), vmem((amount, units), BF16),
            vmem((outer, 2, feature, units), BF16), vmem((outer + 1, 2, feature, units), BF16),
            vmem((2, feature, units), F32), vmem((feature, units), BF16), vmem((feature, units), BF16),
            vmem((replicas, shard, width), BF16), vmem((outer, shard, width), BF16),
            vmem((outer + 1, shard, width), BF16),
            vmem((span, rows, width), BF16),
            vmem((span, rows, width), BF16), vmem((span, places, rows), F32), vmem((amount, units), BF16),
            dma((3,)), dma((2,)), dma((span,)), dma((span,)), dma((4,)), dma((4,)),
            dma((4, parts, chips)), dma((4, parts, chips)), dma((4, parts, chips)), dma((4, parts, chips)),
            dma, dma, dma((parts, chips)), dma((parts, chips)), dma((chips, 2)), dma((chips, 2)),
            dma((outer,)), dma((outer,)),
            dma((outer, 2, 2)), dma((outer + 1, 2, 2)), dma((outer, 2)), dma((outer + 1, 2)),
            dma((span,)), dma((span,)), dma, dma,
            dma, dma, dma((chips,)), dma((chips,)), dma, dma,
        ],
        compiler_params=pltpu.CompilerParams(
            collective_id=0, has_side_effects=True, vmem_limit_bytes=(54 + span) << 20
        ),
        name="fused",
    )(tokens, d_out, routes, gates, w_gate, w_up, w_down)


def store_kernel(*refs):
    sources, targets, sem = refs[:4], refs[4:8], refs[8]
    copies = [
        pltpu.make_async_copy(source, target if at == 0 else target.at[0], sem.at[at])
        for at, (source, target) in enumerate(zip(sources, targets))
    ]
    for copy in copies:
        copy.start()
    for copy in copies:
        copy.wait()


def store(arrays):
    shapes = [arrays[0].shape] + [(1,) + a.shape for a in arrays[1:]]
    return pl.pallas_call(
        store_kernel,
        out_shape=tuple(jax.ShapeDtypeStruct(s, a.dtype) for s, a in zip(shapes, arrays)),
        in_specs=[pl.BlockSpec(memory_space=pltpu.VMEM)] * 4,
        out_specs=[pl.BlockSpec(memory_space=pltpu.HBM)] * 4,
        scratch_shapes=[pltpu.SemaphoreType.DMA((4,))],
        compiler_params=pltpu.CompilerParams(vmem_limit_bytes=1 << 20),
        name="store",
    )(*arrays)


def body(tokens, d_out, routes, gate_fixed, w_gate, w_up, w_down):
    span = lax.axis_size("expert")
    replicas = lax.axis_size("dp")
    return store(fused(tokens, d_out, routes.T, gate_fixed.T, w_gate, w_up, w_down, span, replicas))


def solution(mesh):
    rows = P(("dp", "expert"), None)
    whole = P("expert", None, None)
    cut = P("expert", "dp", None)
    return jax.shard_map(
        body, mesh=mesh, in_specs=(rows,) * 4 + (whole,) * 3, out_specs=(rows, cut, cut, cut), check_vma=False
    )
```

```python
import functools

import jax
import jax.numpy as jnp
from jax import lax
from jax.experimental import pallas as pl
from jax.experimental.pallas import tpu as pltpu
from jax.sharding import PartitionSpec as P

MESH = pl.DeviceIdType.MESH
BF16 = jnp.bfloat16
F32 = jnp.float32


def greet(targets):
    barrier = pltpu.get_barrier_semaphore()
    for target in targets:
        pl.semaphore_signal(barrier, inc=1, device_id=target, device_id_type=MESH)
    pl.semaphore_wait(barrier, len(targets))


def outer_product(left, right):
    return lax.dot_general(left, right, (((0,), (0,)), ((), ())), preferred_element_type=F32)


def times_transposed(left, right):
    return lax.dot_general(left, right, (((1,), (1,)), ((), ())), preferred_element_type=F32)


def kernel(
    span, replicas, parts,
    x_ref, g_ref, routes_ref, gates_ref, wg_ref, wu_ref, wd_ref,
    tok_out, gate_out, up_out, down_out,
    wg, wu, wd, xs, gs, px, scaled, coef, cs, for_gate, for_up, acts, pact, hidden,
    grads, glines, total, cross_out, cross_in, dgrads, dnear, dlines, back, zg, zcs, zhid,
    w_sem, own_sem, c_send, c_recv, core_send, core_recv, chip_send, chip_recv, fwd_send, fwd_recv,
    px_send, px_recv, far_send, far_recv, act_send, act_recv, near_send, near_recv, gline_send, gline_recv,
    dline_send, dline_recv, back_send, back_recv, cross_send, cross_recv,
    z_send, z_recv, zh_send, zh_recv, zc_send, zc_recv,
):
    expert = lax.axis_index("expert")
    me = lax.axis_index("dp")
    core = lax.rem(expert, 2)
    chip = expert // 2
    other = chip * 2 + (1 - core)
    chips = span // 2
    outer = replicas // 2
    side = lax.rem(me, 2)
    line = me // 2
    partner = line * 2 + (1 - side)
    lower = lax.rem(line + outer - 1, outer) * 2 + side
    upper = lax.rem(line + 1, outer) * 2 + side
    rows, width = x_ref.shape
    units = hidden.shape[1]
    feature = width // replicas
    shard = units // replicas
    piece_rows = rows // parts
    near_parts = parts - 1
    every = range(parts)
    half_rows = rows // 2
    inverse = 1.0 / replicas
    is_end = (line == 0) | (line == outer - 1)
    is_helper = (line == 1) | (line == outer - 2)
    inner = {"dp": jnp.where(line == 0, 1, outer - 2) * 2 + side}
    ended = jnp.where(line == 1, 0, outer - 1)

    own_x = pltpu.make_async_copy(x_ref, xs.at[expert], own_sem.at[0])
    own_g = pltpu.make_async_copy(g_ref, gs.at[expert], own_sem.at[1])
    loads = [
        pltpu.make_async_copy(source.at[0], target, w_sem.at[at])
        for at, (source, target) in enumerate(((wg_ref, wg), (wu_ref, wu), (wd_ref, wd)))
    ]
    own_x.start()
    loads[0].start()
    loads[1].start()
    own_g.start()
    loads[2].start()
    places = lax.broadcasted_iota(jnp.int32, coef.shape, 0)
    value = jnp.zeros(coef.shape, F32)
    for k in range(routes_ref.shape[0]):
        gate_value = gates_ref[k : k + 1, :].astype(F32) / 65536.0
        value = value + jnp.where(places == routes_ref[k : k + 1, :], gate_value, 0.0)
    coef[...] = value
    cs[expert] = value

    targets = [{"expert": lax.rem(expert + step, span)} for step in range(1, span)]
    targets += [{"dp": partner}, {"dp": lower}, {"dp": upper}]
    greet(targets)

    def remote(source, target, send, recv, device):
        return pltpu.make_async_remote_copy(
            src_ref=source, dst_ref=target, send_sem=send, recv_sem=recv, device_id=device, device_id_type=MESH
        )

    def piece(ref, part):
        return ref.at[pl.ds(part * piece_rows, piece_rows)]

    sources = (x_ref, g_ref, px.at[expert], zg.at[expert])
    arrays = (xs, gs, px, zg)

    def coef_copy(step):
        return remote(
            coef, cs.at[expert], c_send.at[step], c_recv.at[step], {"expert": lax.rem(expert + step, span)}
        )

    def core_copy(array):
        return remote(
            sources[array], arrays[array].at[expert], core_send.at[array], core_recv.at[array], {"expert": other}
        )

    def chip_copy(array, part, step):
        there = lax.rem(chip + step, chips) * 2 + core
        return remote(
            piece(sources[array], part), piece(arrays[array].at[expert], part),
            chip_send.at[array, part, step], chip_recv.at[array, part, step], {"expert": there},
        )

    def forward_copy(array, part, step, at_core):
        owner = lax.rem(chip + chips - step, chips) * 2 + at_core
        block = piece(arrays[array].at[owner], part)
        return remote(
            block, block, fwd_send.at[array, part, step], fwd_recv.at[array, part, step], {"expert": other}
        )

    def far_copy(part, step):
        owner = lax.rem(chip + chips - step, chips) * 2 + core
        return remote(
            piece(xs.at[owner], part), piece(px.at[owner], part),
            far_send.at[part, step], far_recv.at[part, step], {"dp": partner},
        )

    def pass_on(array, step, some):
        for part in some:
            if array == 2 and part >= near_parts:
                far_copy(part, step).wait_recv()
            else:
                chip_copy(array, part, step).wait_recv()
            forward_copy(array, part, step, core).start()
            if array == 0 and part >= near_parts:
                far_copy(part, step).start()

    def take_passed(array, step, some):
        for part in some:
            forward_copy(array, part, step, 1 - core).wait_recv()

    px_copy = remote(x_ref, px.at[expert], px_send, px_recv, {"dp": partner})

    def pair_rows(step):
        base = lax.rem(chip + chips - step, chips) * 2
        return pl.ds(pl.multiple_of(base * rows, 2 * rows), 2 * rows)

    def pair_half(step, at):
        base = lax.rem(chip + chips - step, chips) * 2
        return pl.ds(base, 2), pl.ds(at * half_rows, half_rows)

    def act_copy(step, at):
        owners, those = pair_half(step, at)
        return remote(
            acts.at[1 - side, owners, those], pact.at[owners, those],
            act_send.at[step, at], act_recv.at[step, at], {"dp": partner},
        )

    def back_copy(step):
        there = lax.rem(expert + step, span)
        return remote(gs.at[there], back.at[step], back_send.at[step], back_recv.at[step], {"expert": there})

    upside = line >= outer // 2
    nearest = jnp.where(upside, outer - 1 - line, line)

    def order_at(i):
        j = i + jnp.where(i >= 2 * nearest + 1, 1, 0)
        d = jnp.where(lax.rem(j, 2) == 0, outer - 1 - j // 2, j // 2)
        return jnp.where(i == outer - 1, line, jnp.where(upside, outer - 1 - d, d))

    def is_fed(d):
        return ((d > line) & (line > 0)) | ((d < line) & (line < outer - 1))

    def near_copy(d):
        return remote(
            dgrads.at[d * 2 + (1 - side)], dnear.at[d], near_send.at[d], near_recv.at[d], {"dp": partner}
        )

    def hop(d):
        following = jnp.where(d > line, line + 1, line - 1)
        slot = jnp.where((d < line) & (d == following), outer, d)
        return slot, {"dp": following * 2 + side}

    slices = 2
    slice_rows = feature // slices
    slice_width = width // slices

    def gline_copy(d, s, q):
        slot, device = hop(d)
        those = pl.ds(q * slice_rows, slice_rows)
        return remote(
            grads.at[d, s, those], glines.at[slot, s, those],
            gline_send.at[d, s, q], gline_recv.at[slot, s, q], device,
        )

    def gline_wait(slot, s, q):
        block = glines.at[slot, s, pl.ds(q * slice_rows, slice_rows)]
        remote(block, block, gline_send.at[0, s, q], gline_recv.at[slot, s, q], {"dp": upper}).wait_recv()

    def dline_copy(d, q):
        slot, device = hop(d)
        those = pl.ds(q * slice_width, slice_width)
        return remote(
            dgrads.at[d * 2 + side, :, those], dlines.at[slot, :, those],
            dline_send.at[d, q], dline_recv.at[slot, q], device,
        )

    def dline_wait(slot, q):
        block = dlines.at[slot, :, pl.ds(q * slice_width, slice_width)]
        remote(block, block, dline_send.at[0, q], dline_recv.at[slot, q], {"dp": upper}).wait_recv()

    def is_fed_down(d):
        return ((d > line) & (line > 1)) | ((d < line) & (line < outer - 2))

    z_copy = remote(g_ref, zg.at[expert], z_send, z_recv, inner)

    def z_hidden(step):
        at = pair_rows(step)
        return remote(hidden.at[at], zhid.at[at], zh_send.at[step], zh_recv.at[step], inner)

    z_coef = remote(cs, zcs, zc_send, zc_recv, inner)

    halves = (1 - side, side)

    for step in range(1, span):
        coef_copy(step).start()
    for part in range(parts):
        for step in range(1, chips):
            chip_copy(0, part, step).start()
    core_copy(0).start()
    px_copy.start()
    core_copy(1).start()
    for part in range(parts):
        for step in range(1, chips):
            chip_copy(1, part, step).start()

    @pl.when(is_end)
    def _():
        z_copy.start()

    cut = units // 3

    def project(step):
        base = lax.rem(chip + chips - step, chips) * 2
        at = pair_rows(step)
        x = xs[pl.ds(base, 2)].reshape(2 * rows, width)
        for c in range(3):
            columns = slice(c * cut, (c + 1) * cut)
            pre_gate = jnp.dot(x, wg[:, columns], preferred_element_type=F32)
            pre_up = jnp.dot(x, wu[:, columns], preferred_element_type=F32)
            sigmoid_gate = 1.0 / (1.0 + jnp.exp(-pre_gate))
            silu_gate = pre_gate * sigmoid_gate
            hidden[at, columns] = (silu_gate * pre_up).astype(BF16)
            for_up[:, :, columns] = silu_gate.reshape(2, rows, cut)
            for_gate[:, :, columns] = (
                pre_up * sigmoid_gate * (1.0 + pre_gate * (1.0 - sigmoid_gate))
            ).reshape(2, rows, cut)

        @pl.when(is_end)
        def _():
            z_hidden(step).start()

    def weights(coefs, owner):
        row = lax.broadcasted_iota(jnp.int32, (rows, rows), 0)
        diagonal = row == lax.broadcasted_iota(jnp.int32, (rows, rows), 1)
        return jnp.sum(jnp.where(diagonal, coefs[owner, pl.ds(expert, 1), :], 0.0), axis=1, keepdims=True)

    def differentiate(step, at):
        base = lax.rem(chip + chips - step, chips) * 2
        owners, those = pair_half(step, at)
        for j in range(2):
            weight = weights(cs, base + j)[at * half_rows : (at + 1) * half_rows]
            scaled[base + j, those] = (weight * gs[base + j, those].astype(F32)).astype(BF16)
        block = scaled[owners, those].reshape(2 * half_rows, width)
        for c in range(3):
            columns = slice(c * cut, (c + 1) * cut)
            d_hidden = times_transposed(block, wd[columns, :]).reshape(2, half_rows, cut)
            acts[0, owners, those, columns] = (d_hidden * for_gate[:, those, columns]).astype(BF16)
            acts[1, owners, those, columns] = (d_hidden * for_up[:, those, columns]).astype(BF16)
        act_copy(step, at).start()

    own_x.wait()
    loads[0].wait()
    loads[1].wait()
    core_copy(0).wait_recv()
    project(0)
    own_g.wait()
    loads[2].wait()
    core_copy(1).wait_recv()
    for step in range(1, span):
        coef_copy(step).wait_recv()

    @pl.when(is_end)
    def _():
        z_coef.start()

    for at in range(2):
        differentiate(0, at)
    px_copy.wait_recv()
    core_copy(2).start()
    for step in range(1, chips):
        pass_on(0, step, every)
        take_passed(0, step, every)
        project(step)
        if step == 1:
            for part in range(near_parts):
                for later in range(1, chips):
                    chip_copy(2, part, later).start()

            @pl.when(is_helper)
            def _():
                z_copy.wait_recv()
                core_copy(3).start()
                for part in range(parts):
                    for later in range(1, chips):
                        chip_copy(3, part, later).start()

        for at in range(2):
            some = every[at * parts // 2 : (at + 1) * parts // 2]
            pass_on(1, step, some)
            take_passed(1, step, some)
            differentiate(step, at)

    for array in range(2):
        for step in range(1, chips):
            for part in range(parts):
                forward_copy(array, part, step, core).wait_send()

    def route_pair(step, carry):
        base = lax.rem(chip + chips - step, chips) * 2
        pair = acts[:, pl.ds(base, 2)].reshape(2, 2 * rows, units)
        product = times_transposed(pair[0], wg[...]) + times_transposed(pair[1], wu[...])
        gs[base] = product[:rows].astype(BF16)
        gs[base + 1] = product[rows:].astype(BF16)
        return carry

    lax.fori_loop(0, chips, route_pair, 0)

    for step in range(1, chips):
        pass_on(2, step, every)
    for step in range(1, chips):
        take_passed(2, step, every)
    core_copy(2).wait_recv()
    for step in range(chips):
        for at in range(2):
            act_copy(step, at).wait_recv()

    def product_at(d):
        columns = pl.ds(pl.multiple_of(d * 2 * feature, 2 * feature), 2 * feature)
        return outer_product(
            xs[:, :, columns].reshape(span * rows, 2 * feature), acts[side].reshape(span * rows, units)
        ) + outer_product(
            px[:, :, columns].reshape(span * rows, 2 * feature), pact[...].reshape(span * rows, units)
        )

    def make(i, carry):
        d = order_at(i)
        product = product_at(d)
        grads[d, 0] = product[:feature].astype(BF16)
        grads[d, 1] = product[feature:].astype(BF16)

        @pl.when(jnp.logical_not(is_fed(d)))
        def _():
            for s in halves:
                for q in range(slices):
                    gline_copy(d, s, q).start()

        return carry

    lax.fori_loop(0, outer - 1, make, 0)
    product = product_at(line)
    total[0] = product[:feature]
    total[1] = product[feature:]

    for step in range(1, span):
        back_copy(step).start()

    def pass_gate(i, s, q):
        d = order_at(i)
        those = pl.ds(q * slice_rows, slice_rows)

        @pl.when(is_fed(d))
        def _():
            gline_wait(d, s, q)
            grads[d, s, those] = (grads[d, s, those].astype(F32) + glines[d, s, those].astype(F32)).astype(BF16)
            gline_copy(d, s, q).start()

    half = units // 2

    def down(helps, part):
        columns = slice(part * half, (part + 1) * half)
        product = outer_product(hidden[:, columns], scaled[...].reshape(span * rows, width))
        if helps:
            product = product + outer_product(zhid[:, columns], zg[...].reshape(span * rows, width))
        for at in range(half // shard):
            dgrads[part * (half // shard) + at] = product[at * shard : (at + 1) * shard].astype(BF16)

    def down_part(part):
        @pl.when(is_helper)
        def _():
            down(True, part)

        @pl.when(jnp.logical_not(is_helper))
        def _():
            down(False, part)

    pass_gate(0, halves[0], 0)

    @pl.when(is_helper)
    def _():
        column = lax.broadcasted_iota(jnp.int32, (1, units), 1) // (2 * shard)
        kept = jnp.where(column == ended, 0.0, 1.0).astype(BF16)
        for step in range(chips):
            z_hidden(step).wait_recv()
        zhid[...] = zhid[...] * kept
        z_coef.wait_recv()
        for step in range(1, chips):
            pass_on(3, step, every)

    pass_gate(0, halves[0], 1)

    @pl.when(is_helper)
    def _():
        for step in range(1, chips):
            take_passed(3, step, every)
            for part in range(parts):
                forward_copy(3, part, step, core).wait_send()
                chip_copy(3, part, step).wait_send()
        core_copy(3).wait()
        for owner in range(span):
            zg[owner] = (weights(zcs, owner) * zg[owner].astype(F32)).astype(BF16)

    down_part(0)
    pass_gate(0, halves[1], 0)
    down_part(1)

    def start_near(first):
        def at(i, carry):
            d = order_at(i)
            fed = is_fed_down(d) | (d == line)
            wanted = jnp.logical_not(fed | is_end) if first else (fed & jnp.logical_not(is_end)) | (d == line)

            @pl.when(wanted)
            def _():
                near_copy(d).start()

            return carry

        lax.fori_loop(0, outer, at, 0)

    start_near(True)
    start_near(False)
    pass_gate(0, halves[1], 1)

    def pass_gates(i, carry):
        for s in halves:
            for q in range(slices):
                pass_gate(i, s, q)
        return carry

    lax.fori_loop(1, outer - 1, pass_gates, 0)

    def start_down(i, carry):
        d = order_at(i)
        at = d * 2 + side

        @pl.when(jnp.logical_not(is_end | is_fed_down(d)))
        def _():
            near_copy(d).wait_recv()
            for q in range(slices):
                those = slice(q * slice_width, (q + 1) * slice_width)
                dgrads[at, :, those] = (
                    dgrads[at, :, those].astype(F32) + dnear[d, :, those].astype(F32)
                ).astype(BF16)
                dline_copy(d, q).start()

        return carry

    lax.fori_loop(0, outer - 1, start_down, 0)

    for step in range(1, span):
        back_copy(step).wait_recv()
    route_sum = gs[expert].astype(F32)
    for step in range(1, span):
        route_sum = route_sum + back[step].astype(F32)
    tok_out[...] = route_sum.astype(BF16)

    cross = remote(cross_out, cross_in, cross_send, cross_recv, {"dp": partner})
    for s in halves:

        @pl.when(line > 0)
        def _():
            for q in range(slices):
                gline_wait(line, s, q)
            total[s] += glines[line, s].astype(F32)

        @pl.when(line < outer - 1)
        def _():
            for q in range(slices):
                gline_wait(outer, s, q)
            total[s] += glines[outer, s].astype(F32)

        if s is halves[0]:
            cross_out[...] = total[s].astype(BF16)
            cross.start()

    def pass_down(i, carry):
        d = order_at(i)
        at = d * 2 + side

        @pl.when(jnp.logical_not(is_end) & is_fed_down(d))
        def _():
            near_copy(d).wait_recv()
            for q in range(slices):
                those = slice(q * slice_width, (q + 1) * slice_width)
                dline_wait(d, q)
                dgrads[at, :, those] = (
                    dgrads[at, :, those].astype(F32) + dnear[d, :, those].astype(F32) + dlines[d, :, those].astype(F32)
                ).astype(BF16)
                dline_copy(d, q).start()

        return carry

    lax.fori_loop(0, outer - 1, pass_down, 0)

    near_copy(line).wait_recv()
    down_out[...] = (dgrads[me].astype(F32) + dnear[line].astype(F32)) * inverse

    @pl.when(line > 1)
    def _():
        for q in range(slices):
            those = slice(q * slice_width, (q + 1) * slice_width)
            dline_wait(line, q)
            down_out[:, those] += dlines[line, :, those].astype(F32) * inverse

    @pl.when(line < outer - 2)
    def _():
        for q in range(slices):
            those = slice(q * slice_width, (q + 1) * slice_width)
            dline_wait(outer, q)
            down_out[:, those] += dlines[outer, :, those].astype(F32) * inverse

    cross.wait_recv()

    @pl.when(side == 0)
    def _():
        gate_out[...] = total[0] * inverse
        up_out[...] = cross_in[...].astype(F32) * inverse

    @pl.when(side == 1)
    def _():
        up_out[...] = total[1] * inverse
        gate_out[...] = cross_in[...].astype(F32) * inverse

    for step in range(1, span):
        coef_copy(step).wait_send()
        back_copy(step).wait_send()
    for array in range(3):
        core_copy(array).wait_send()
        for step in range(1, chips):
            for part in range(near_parts if array == 2 else parts):
                chip_copy(array, part, step).wait_send()
    for step in range(1, chips):
        for part in range(parts):
            forward_copy(2, part, step, core).wait_send()
            if part >= near_parts:
                far_copy(part, step).wait_send()
    px_copy.wait_send()
    for step in range(chips):
        for at in range(2):
            act_copy(step, at).wait_send()

    @pl.when(is_end)
    def _():
        for step in range(chips):
            z_hidden(step).wait_send()
        z_copy.wait_send()
        z_coef.wait_send()

    def finish(i, carry):
        d = order_at(i)

        @pl.when(jnp.logical_not(is_end) | (d == line))
        def _():
            near_copy(d).wait_send()

        @pl.when(i < outer - 1)
        def _():
            for s in halves:
                for q in range(slices):
                    gline_copy(d, s, q).wait_send()

        @pl.when((i < outer - 1) & jnp.logical_not(is_end))
        def _():
            for q in range(slices):
                dline_copy(d, q).wait_send()

        return carry

    lax.fori_loop(0, outer, finish, 0)
    cross.wait_send()


def fused(tokens, d_out, routes, gates, w_gate, w_up, w_down, span, replicas):
    parts = 4
    dma = pltpu.SemaphoreType.DMA
    rows, width = tokens.shape
    units = w_gate.shape[2]
    outer, chips = replicas // 2, span // 2
    feature, shard = width // replicas, units // replicas
    amount = span * rows
    here = pl.BlockSpec(memory_space=pltpu.VMEM)
    away = pl.BlockSpec(memory_space=pltpu.HBM)
    vmem = pltpu.VMEM
    places = max(8, span)
    return pl.pallas_call(
        functools.partial(kernel, span, replicas, parts),
        out_shape=(
            vmem((rows, width), BF16), vmem((feature, units), F32), vmem((feature, units), F32),
            vmem((shard, width), F32),
        ),
        in_specs=[away, away, here, here, away, away, away],
        out_specs=[here] * 4,
        scratch_shapes=[
            vmem((width, units), BF16), vmem((width, units), BF16), vmem((units, width), BF16),
            vmem((span, rows, width), BF16), vmem((span, rows, width), BF16), vmem((span, rows, width), BF16),
            vmem((span, rows, width), BF16),
            vmem((places, rows), F32), vmem((span, places, rows), F32),
            vmem((2, rows, units), F32), vmem((2, rows, units), F32),
            vmem((2, span, rows, units), BF16), vmem((span, rows, units), BF16), vmem((amount, units), BF16),
            vmem((outer, 2, feature, units), BF16), vmem((outer + 1, 2, feature, units), BF16),
            vmem((2, feature, units), F32), vmem((feature, units), BF16), vmem((feature, units), BF16),
            vmem((replicas, shard, width), BF16), vmem((outer, shard, width), BF16),
            vmem((outer + 1, shard, width), BF16),
            vmem((span, rows, width), BF16),
            vmem((span, rows, width), BF16), vmem((span, places, rows), F32), vmem((amount, units), BF16),
            dma((3,)), dma((2,)), dma((span,)), dma((span,)), dma((4,)), dma((4,)),
            dma((4, parts, chips)), dma((4, parts, chips)), dma((4, parts, chips)), dma((4, parts, chips)),
            dma, dma, dma((parts, chips)), dma((parts, chips)), dma((chips, 2)), dma((chips, 2)),
            dma((outer,)), dma((outer,)),
            dma((outer, 2, 2)), dma((outer + 1, 2, 2)), dma((outer, 2)), dma((outer + 1, 2)),
            dma((span,)), dma((span,)), dma, dma,
            dma, dma, dma((chips,)), dma((chips,)), dma, dma,
        ],
        compiler_params=pltpu.CompilerParams(
            collective_id=0, has_side_effects=True, vmem_limit_bytes=(54 + span) << 20
        ),
        name="fused",
    )(tokens, d_out, routes, gates, w_gate, w_up, w_down)


def store_kernel(*refs):
    sources, targets, sem = refs[:4], refs[4:8], refs[8]
    copies = [
        pltpu.make_async_copy(source, target if at == 0 else target.at[0], sem.at[at])
        for at, (source, target) in enumerate(zip(sources, targets))
    ]
    for copy in copies:
        copy.start()
    for copy in copies:
        copy.wait()


def store(arrays):
    shapes = [arrays[0].shape] + [(1,) + a.shape for a in arrays[1:]]
    return pl.pallas_call(
        store_kernel,
        out_shape=tuple(jax.ShapeDtypeStruct(s, a.dtype) for s, a in zip(shapes, arrays)),
        in_specs=[pl.BlockSpec(memory_space=pltpu.VMEM)] * 4,
        out_specs=[pl.BlockSpec(memory_space=pltpu.HBM)] * 4,
        scratch_shapes=[pltpu.SemaphoreType.DMA((4,))],
        compiler_params=pltpu.CompilerParams(vmem_limit_bytes=1 << 20),
        name="store",
    )(*arrays)


def body(tokens, d_out, routes, gate_fixed, w_gate, w_up, w_down):
    span = lax.axis_size("expert")
    replicas = lax.axis_size("dp")
    return store(fused(tokens, d_out, routes.T, gate_fixed.T, w_gate, w_up, w_down, span, replicas))


def solution(mesh):
    rows = P(("dp", "expert"), None)
    whole = P("expert", None, None)
    cut = P("expert", "dp", None)
    return jax.shard_map(
        body, mesh=mesh, in_specs=(rows,) * 4 + (whole,) * 3, out_specs=(rows, cut, cut, cut), check_vma=False
    )
```

```python
import functools

import jax
import jax.numpy as jnp
from jax import lax
from jax.experimental import pallas as pl
from jax.experimental.pallas import tpu as pltpu
from jax.sharding import PartitionSpec as P

MESH = pl.DeviceIdType.MESH
BF16 = jnp.bfloat16
F32 = jnp.float32


def greet(targets):
    barrier = pltpu.get_barrier_semaphore()
    for target in targets:
        pl.semaphore_signal(barrier, inc=1, device_id=target, device_id_type=MESH)
    pl.semaphore_wait(barrier, len(targets))


def outer_product(left, right):
    return lax.dot_general(left, right, (((0,), (0,)), ((), ())), preferred_element_type=F32)


def times_transposed(left, right):
    return lax.dot_general(left, right, (((1,), (1,)), ((), ())), preferred_element_type=F32)


def kernel(
    span, replicas, parts,
    x_ref, g_ref, routes_ref, gates_ref, wg_ref, wu_ref, wd_ref,
    tok_out, gate_out, up_out, down_out,
    wg, wu, wd, xs, gs, px, scaled, coef, cs, for_gate, for_up, acts, pact, hidden,
    grads, glines, total, cross_out, cross_in, dgrads, dnear, dlines, back, zg, zcs, zhid,
    w_sem, own_sem, c_send, c_recv, core_send, core_recv, chip_send, chip_recv, fwd_send, fwd_recv,
    px_send, px_recv, far_send, far_recv, act_send, act_recv, near_send, near_recv, gline_send, gline_recv,
    dline_send, dline_recv, back_send, back_recv, cross_send, cross_recv,
    z_send, z_recv, zh_send, zh_recv, zc_send, zc_recv, raw_send, raw_recv,
):
    expert = lax.axis_index("expert")
    me = lax.axis_index("dp")
    core = lax.rem(expert, 2)
    chip = expert // 2
    other = chip * 2 + (1 - core)
    chips = span // 2
    outer = replicas // 2
    side = lax.rem(me, 2)
    line = me // 2
    partner = line * 2 + (1 - side)
    lower = lax.rem(line + outer - 1, outer) * 2 + side
    upper = lax.rem(line + 1, outer) * 2 + side
    rows, width = x_ref.shape
    units = hidden.shape[1]
    feature = width // replicas
    shard = units // replicas
    piece_rows = rows // parts
    near_parts = parts - 1
    every = range(parts)
    half_rows = rows // 2
    inverse = 1.0 / replicas
    is_end = (line == 0) | (line == outer - 1)
    is_helper = (line == 1) | (line == outer - 2)
    inner = {"dp": jnp.where(line == 0, 1, outer - 2) * 2 + side}
    ended = jnp.where(line == 1, 0, outer - 1)

    own_x = pltpu.make_async_copy(x_ref, xs.at[expert], own_sem.at[0])
    own_g = pltpu.make_async_copy(g_ref, gs.at[expert], own_sem.at[1])
    loads = [
        pltpu.make_async_copy(source.at[0], target, w_sem.at[at])
        for at, (source, target) in enumerate(((wg_ref, wg), (wu_ref, wu), (wd_ref, wd)))
    ]
    own_x.start()
    loads[0].start()
    loads[1].start()
    own_g.start()
    loads[2].start()
    places = lax.broadcasted_iota(jnp.int32, coef.shape, 0)
    value = jnp.zeros(coef.shape, F32)
    for k in range(routes_ref.shape[0]):
        gate_value = gates_ref[k : k + 1, :].astype(F32) / 65536.0
        value = value + jnp.where(places == routes_ref[k : k + 1, :], gate_value, 0.0)
    coef[...] = value
    cs[expert] = value

    targets = [{"expert": lax.rem(expert + step, span)} for step in range(1, span)]
    targets += [{"dp": partner}, {"dp": lower}, {"dp": upper}]
    greet(targets)

    def remote(source, target, send, recv, device):
        return pltpu.make_async_remote_copy(
            src_ref=source, dst_ref=target, send_sem=send, recv_sem=recv, device_id=device, device_id_type=MESH
        )

    def piece(ref, part):
        return ref.at[pl.ds(part * piece_rows, piece_rows)]

    sources = (x_ref, g_ref, px.at[expert], zg.at[expert])
    arrays = (xs, gs, px, zg)

    def coef_copy(step):
        return remote(
            coef, cs.at[expert], c_send.at[step], c_recv.at[step], {"expert": lax.rem(expert + step, span)}
        )

    def core_copy(array):
        return remote(
            sources[array], arrays[array].at[expert], core_send.at[array], core_recv.at[array], {"expert": other}
        )

    def chip_copy(array, part, step):
        there = lax.rem(chip + step, chips) * 2 + core
        return remote(
            piece(sources[array], part), piece(arrays[array].at[expert], part),
            chip_send.at[array, part, step], chip_recv.at[array, part, step], {"expert": there},
        )

    def forward_copy(array, part, step, at_core):
        owner = lax.rem(chip + chips - step, chips) * 2 + at_core
        block = piece(arrays[array].at[owner], part)
        return remote(
            block, block, fwd_send.at[array, part, step], fwd_recv.at[array, part, step], {"expert": other}
        )

    def far_copy(part, step):
        owner = lax.rem(chip + chips - step, chips) * 2 + core
        return remote(
            piece(xs.at[owner], part), piece(px.at[owner], part),
            far_send.at[part, step], far_recv.at[part, step], {"dp": partner},
        )

    def pass_on(array, step, some):
        for part in some:
            if array == 2 and part >= near_parts:
                far_copy(part, step).wait_recv()
            else:
                chip_copy(array, part, step).wait_recv()
            forward_copy(array, part, step, core).start()
            if array == 0 and part >= near_parts:
                far_copy(part, step).start()

    def take_passed(array, step, some):
        for part in some:
            forward_copy(array, part, step, 1 - core).wait_recv()

    px_copy = remote(x_ref, px.at[expert], px_send, px_recv, {"dp": partner})

    def pair_rows(step):
        base = lax.rem(chip + chips - step, chips) * 2
        return pl.ds(pl.multiple_of(base * rows, 2 * rows), 2 * rows)

    def pair_half(step, at):
        base = lax.rem(chip + chips - step, chips) * 2
        return pl.ds(base, 2), pl.ds(at * half_rows, half_rows)

    def act_copy(step, at):
        owners, those = pair_half(step, at)
        return remote(
            acts.at[1 - side, owners, those], pact.at[owners, those],
            act_send.at[step, at], act_recv.at[step, at], {"dp": partner},
        )

    def back_copy(step):
        there = lax.rem(expert + step, span)
        return remote(gs.at[there], back.at[step], back_send.at[step], back_recv.at[step], {"expert": there})

    upside = line >= outer // 2
    nearest = jnp.where(upside, outer - 1 - line, line)

    def order_at(i):
        j = i + jnp.where(i >= 2 * nearest + 1, 1, 0)
        d = jnp.where(lax.rem(j, 2) == 0, outer - 1 - j // 2, j // 2)
        return jnp.where(i == outer - 1, line, jnp.where(upside, outer - 1 - d, d))

    def is_fed(d):
        return ((d > line) & (line > 0)) | ((d < line) & (line < outer - 1))

    def near_copy(d):
        return remote(
            dgrads.at[d * 2 + (1 - side)], dnear.at[d], near_send.at[d], near_recv.at[d], {"dp": partner}
        )

    def is_near(d):
        return (d == line) | jnp.logical_not(is_end | (is_helper & (d == ended)))

    raw_copy = remote(
        dgrads.at[ended * 2 + (1 - side)], dnear.at[line], raw_send, raw_recv, {"dp": ended * 2 + side}
    )

    def hop(d):
        following = jnp.where(d > line, line + 1, line - 1)
        slot = jnp.where((d < line) & (d == following), outer, d)
        return slot, {"dp": following * 2 + side}

    slices = 2
    slice_rows = feature // slices
    slice_width = width // slices

    def gline_copy(d, s, q):
        slot, device = hop(d)
        those = pl.ds(q * slice_rows, slice_rows)
        return remote(
            grads.at[d, s, those], glines.at[slot, s, those],
            gline_send.at[d, s, q], gline_recv.at[slot, s, q], device,
        )

    def gline_wait(slot, s, q):
        block = glines.at[slot, s, pl.ds(q * slice_rows, slice_rows)]
        remote(block, block, gline_send.at[0, s, q], gline_recv.at[slot, s, q], {"dp": upper}).wait_recv()

    def dline_copy(d, q):
        slot, device = hop(d)
        those = pl.ds(q * slice_width, slice_width)
        return remote(
            dgrads.at[d * 2 + side, :, those], dlines.at[slot, :, those],
            dline_send.at[d, q], dline_recv.at[slot, q], device,
        )

    def dline_wait(slot, q):
        block = dlines.at[slot, :, pl.ds(q * slice_width, slice_width)]
        remote(block, block, dline_send.at[0, q], dline_recv.at[slot, q], {"dp": upper}).wait_recv()

    def is_fed_down(d):
        return ((d > line) & (line > 1)) | ((d < line) & (line < outer - 2))

    z_copy = remote(g_ref, zg.at[expert], z_send, z_recv, inner)

    def z_hidden(step):
        at = pair_rows(step)
        return remote(hidden.at[at], zhid.at[at], zh_send.at[step], zh_recv.at[step], inner)

    z_coef = remote(cs, zcs, zc_send, zc_recv, inner)

    halves = (1 - side, side)

    for step in range(1, span):
        coef_copy(step).start()
    for part in range(parts):
        for step in range(1, chips):
            chip_copy(0, part, step).start()
    core_copy(0).start()
    px_copy.start()
    core_copy(1).start()
    for part in range(parts):
        for step in range(1, chips):
            chip_copy(1, part, step).start()

    @pl.when(is_end)
    def _():
        z_copy.start()

    cut = units // 3

    def project(step):
        base = lax.rem(chip + chips - step, chips) * 2
        at = pair_rows(step)
        x = xs[pl.ds(base, 2)].reshape(2 * rows, width)
        for c in range(3):
            columns = slice(c * cut, (c + 1) * cut)
            pre_gate = jnp.dot(x, wg[:, columns], preferred_element_type=F32)
            pre_up = jnp.dot(x, wu[:, columns], preferred_element_type=F32)
            sigmoid_gate = 1.0 / (1.0 + jnp.exp(-pre_gate))
            silu_gate = pre_gate * sigmoid_gate
            hidden[at, columns] = (silu_gate * pre_up).astype(BF16)
            for_up[:, :, columns] = silu_gate.reshape(2, rows, cut)
            for_gate[:, :, columns] = (
                pre_up * sigmoid_gate * (1.0 + pre_gate * (1.0 - sigmoid_gate))
            ).reshape(2, rows, cut)

        @pl.when(is_end)
        def _():
            z_hidden(step).start()

    def weights(coefs, owner):
        row = lax.broadcasted_iota(jnp.int32, (rows, rows), 0)
        diagonal = row == lax.broadcasted_iota(jnp.int32, (rows, rows), 1)
        return jnp.sum(jnp.where(diagonal, coefs[owner, pl.ds(expert, 1), :], 0.0), axis=1, keepdims=True)

    def differentiate(step, at):
        base = lax.rem(chip + chips - step, chips) * 2
        owners, those = pair_half(step, at)
        for j in range(2):
            weight = weights(cs, base + j)[at * half_rows : (at + 1) * half_rows]
            scaled[base + j, those] = (weight * gs[base + j, those].astype(F32)).astype(BF16)
        block = scaled[owners, those].reshape(2 * half_rows, width)
        for c in range(3):
            columns = slice(c * cut, (c + 1) * cut)
            d_hidden = times_transposed(block, wd[columns, :]).reshape(2, half_rows, cut)
            acts[0, owners, those, columns] = (d_hidden * for_gate[:, those, columns]).astype(BF16)
            acts[1, owners, those, columns] = (d_hidden * for_up[:, those, columns]).astype(BF16)
        act_copy(step, at).start()

    own_x.wait()
    loads[0].wait()
    loads[1].wait()
    core_copy(0).wait_recv()
    project(0)
    own_g.wait()
    loads[2].wait()
    core_copy(1).wait_recv()
    for step in range(1, span):
        coef_copy(step).wait_recv()

    @pl.when(is_end)
    def _():
        z_coef.start()

    for at in range(2):
        differentiate(0, at)
    px_copy.wait_recv()
    core_copy(2).start()
    for step in range(1, chips):
        pass_on(0, step, every)
        take_passed(0, step, every)
        project(step)
        if step == 1:
            for part in range(near_parts):
                for later in range(1, chips):
                    chip_copy(2, part, later).start()

            @pl.when(is_helper)
            def _():
                z_copy.wait_recv()
                core_copy(3).start()
                for part in range(parts):
                    for later in range(1, chips):
                        chip_copy(3, part, later).start()

        for at in range(2):
            some = every[at * parts // 2 : (at + 1) * parts // 2]
            pass_on(1, step, some)
            take_passed(1, step, some)
            differentiate(step, at)

    for array in range(2):
        for step in range(1, chips):
            for part in range(parts):
                forward_copy(array, part, step, core).wait_send()

    def route_pair(step, carry):
        base = lax.rem(chip + chips - step, chips) * 2
        pair = acts[:, pl.ds(base, 2)].reshape(2, 2 * rows, units)
        product = times_transposed(pair[0], wg[...]) + times_transposed(pair[1], wu[...])
        gs[base] = product[:rows].astype(BF16)
        gs[base + 1] = product[rows:].astype(BF16)
        return carry

    lax.fori_loop(0, chips, route_pair, 0)

    for step in range(1, chips):
        pass_on(2, step, every)
    for step in range(1, chips):
        take_passed(2, step, every)
    core_copy(2).wait_recv()
    for step in range(chips):
        for at in range(2):
            act_copy(step, at).wait_recv()

    def product_at(d):
        columns = pl.ds(pl.multiple_of(d * 2 * feature, 2 * feature), 2 * feature)
        return outer_product(
            xs[:, :, columns].reshape(span * rows, 2 * feature), acts[side].reshape(span * rows, units)
        ) + outer_product(
            px[:, :, columns].reshape(span * rows, 2 * feature), pact[...].reshape(span * rows, units)
        )

    def make(i, carry):
        d = order_at(i)
        product = product_at(d)
        grads[d, 0] = product[:feature].astype(BF16)
        grads[d, 1] = product[feature:].astype(BF16)

        @pl.when(jnp.logical_not(is_fed(d)))
        def _():
            for s in halves:
                for q in range(slices):
                    gline_copy(d, s, q).start()

        return carry

    lax.fori_loop(0, outer - 1, make, 0)
    product = product_at(line)
    total[0] = product[:feature]
    total[1] = product[feature:]

    for step in range(1, span):
        back_copy(step).start()

    def pass_gate(i, s, q):
        d = order_at(i)
        those = pl.ds(q * slice_rows, slice_rows)

        @pl.when(is_fed(d))
        def _():
            gline_wait(d, s, q)
            grads[d, s, those] = (grads[d, s, those].astype(F32) + glines[d, s, those].astype(F32)).astype(BF16)
            gline_copy(d, s, q).start()

    half = units // 2

    def down(helps, part):
        columns = pl.ds(pl.multiple_of(part * half, half), half)
        product = outer_product(hidden[:, columns], scaled[...].reshape(span * rows, width))
        if helps:
            product = product + outer_product(zhid[:, columns], zg[...].reshape(span * rows, width))
        for at in range(half // shard):
            dgrads[part * (half // shard) + at] = product[at * shard : (at + 1) * shard].astype(BF16)

    def down_part(part):
        @pl.when(is_helper)
        def _():
            down(True, part)

        @pl.when(jnp.logical_not(is_helper))
        def _():
            down(False, part)

        def start_near(i, carry):
            d = order_at(i)

            @pl.when((d // (outer // 2) == part) & is_near(d) & jnp.logical_not(is_end))
            def _():
                near_copy(d).start()

            return carry

        lax.fori_loop(0, outer, start_near, 0)

    far_part = jnp.where(upside, 0, 1)
    pass_gate(0, halves[0], 0)

    @pl.when(is_helper)
    def _():
        column = lax.broadcasted_iota(jnp.int32, (1, units), 1) // (2 * shard)
        kept = jnp.where(column == ended, 0.0, 1.0).astype(BF16)
        for step in range(chips):
            z_hidden(step).wait_recv()
        zhid[...] = zhid[...] * kept
        z_coef.wait_recv()
        for step in range(1, chips):
            pass_on(3, step, every)

    pass_gate(0, halves[0], 1)

    @pl.when(is_helper)
    def _():
        for step in range(1, chips):
            take_passed(3, step, every)
            for part in range(parts):
                forward_copy(3, part, step, core).wait_send()
                chip_copy(3, part, step).wait_send()
        core_copy(3).wait()
        for owner in range(span):
            zg[owner] = (weights(zcs, owner) * zg[owner].astype(F32)).astype(BF16)

    down_part(far_part)
    pass_gate(0, halves[1], 0)
    down_part(1 - far_part)

    @pl.when(is_helper)
    def _():
        raw_copy.start()

    pass_gate(0, halves[1], 1)

    def pass_gates(i, carry):
        for s in halves:
            for q in range(slices):
                pass_gate(i, s, q)
        return carry

    lax.fori_loop(1, outer - 1, pass_gates, 0)

    @pl.when(is_end)
    def _():
        helper = jnp.where(line == 0, 1, outer - 2)
        remote(
            dnear.at[helper], dnear.at[helper], raw_send, raw_recv, {"dp": partner}
        ).wait_recv()
        at = line * 2 + (1 - side)
        dgrads[at] = (dgrads[at].astype(F32) + dnear[helper].astype(F32)).astype(BF16)
        near_copy(line).start()

    def start_down(i, carry):
        d = order_at(i)
        at = d * 2 + side

        @pl.when(jnp.logical_not(is_end | is_fed_down(d)))
        def _():
            near_copy(d).wait_recv()
            for q in range(slices):
                those = slice(q * slice_width, (q + 1) * slice_width)
                dgrads[at, :, those] = (
                    dgrads[at, :, those].astype(F32) + dnear[d, :, those].astype(F32)
                ).astype(BF16)
                dline_copy(d, q).start()

        return carry

    lax.fori_loop(0, outer - 1, start_down, 0)

    for step in range(1, span):
        back_copy(step).wait_recv()
    route_sum = gs[expert].astype(F32)
    for step in range(1, span):
        route_sum = route_sum + back[step].astype(F32)
    tok_out[...] = route_sum.astype(BF16)

    def pass_down(i, carry):
        d = order_at(i)
        at = d * 2 + side

        @pl.when(jnp.logical_not(is_end) & is_fed_down(d))
        def _():
            @pl.when(is_near(d))
            def _():
                near_copy(d).wait_recv()
                for q in range(slices):
                    those = slice(q * slice_width, (q + 1) * slice_width)
                    dline_wait(d, q)
                    dgrads[at, :, those] = (
                        dgrads[at, :, those].astype(F32)
                        + dnear[d, :, those].astype(F32)
                        + dlines[d, :, those].astype(F32)
                    ).astype(BF16)
                    dline_copy(d, q).start()

            @pl.when(jnp.logical_not(is_near(d)))
            def _():
                for q in range(slices):
                    those = slice(q * slice_width, (q + 1) * slice_width)
                    dline_wait(d, q)
                    dgrads[at, :, those] = (
                        dgrads[at, :, those].astype(F32) + dlines[d, :, those].astype(F32)
                    ).astype(BF16)
                    dline_copy(d, q).start()

        return carry

    lax.fori_loop(0, outer - 1, pass_down, 0)

    cross = remote(cross_out, cross_in, cross_send, cross_recv, {"dp": partner})
    for s in halves:

        @pl.when(line > 0)
        def _():
            for q in range(slices):
                gline_wait(line, s, q)
            total[s] += glines[line, s].astype(F32)

        @pl.when(line < outer - 1)
        def _():
            for q in range(slices):
                gline_wait(outer, s, q)
            total[s] += glines[outer, s].astype(F32)

        if s is halves[0]:
            cross_out[...] = total[s].astype(BF16)
            cross.start()

    near_copy(line).wait_recv()
    down_out[...] = (dgrads[me].astype(F32) + dnear[line].astype(F32)) * inverse

    @pl.when(line > 1)
    def _():
        for q in range(slices):
            those = slice(q * slice_width, (q + 1) * slice_width)
            dline_wait(line, q)
            down_out[:, those] += dlines[line, :, those].astype(F32) * inverse

    @pl.when(line < outer - 2)
    def _():
        for q in range(slices):
            those = slice(q * slice_width, (q + 1) * slice_width)
            dline_wait(outer, q)
            down_out[:, those] += dlines[outer, :, those].astype(F32) * inverse

    cross.wait_recv()

    @pl.when(side == 0)
    def _():
        gate_out[...] = total[0] * inverse
        up_out[...] = cross_in[...].astype(F32) * inverse

    @pl.when(side == 1)
    def _():
        up_out[...] = total[1] * inverse
        gate_out[...] = cross_in[...].astype(F32) * inverse

    for step in range(1, span):
        coef_copy(step).wait_send()
        back_copy(step).wait_send()
    for array in range(3):
        core_copy(array).wait_send()
        for step in range(1, chips):
            for part in range(near_parts if array == 2 else parts):
                chip_copy(array, part, step).wait_send()
    for step in range(1, chips):
        for part in range(parts):
            forward_copy(2, part, step, core).wait_send()
            if part >= near_parts:
                far_copy(part, step).wait_send()
    px_copy.wait_send()
    for step in range(chips):
        for at in range(2):
            act_copy(step, at).wait_send()

    @pl.when(is_end)
    def _():
        for step in range(chips):
            z_hidden(step).wait_send()
        z_copy.wait_send()
        z_coef.wait_send()

    def finish(i, carry):
        d = order_at(i)

        @pl.when(is_near(d))
        def _():
            near_copy(d).wait_send()

        @pl.when(i < outer - 1)
        def _():
            for s in halves:
                for q in range(slices):
                    gline_copy(d, s, q).wait_send()

        @pl.when((i < outer - 1) & jnp.logical_not(is_end))
        def _():
            for q in range(slices):
                dline_copy(d, q).wait_send()

        return carry

    lax.fori_loop(0, outer, finish, 0)
    cross.wait_send()

    @pl.when(is_helper)
    def _():
        raw_copy.wait_send()


def fused(tokens, d_out, routes, gates, w_gate, w_up, w_down, span, replicas):
    parts = 4
    dma = pltpu.SemaphoreType.DMA
    rows, width = tokens.shape
    units = w_gate.shape[2]
    outer, chips = replicas // 2, span // 2
    feature, shard = width // replicas, units // replicas
    amount = span * rows
    here = pl.BlockSpec(memory_space=pltpu.VMEM)
    away = pl.BlockSpec(memory_space=pltpu.HBM)
    vmem = pltpu.VMEM
    places = max(8, span)
    return pl.pallas_call(
        functools.partial(kernel, span, replicas, parts),
        out_shape=(
            vmem((rows, width), BF16), vmem((feature, units), F32), vmem((feature, units), F32),
            vmem((shard, width), F32),
        ),
        in_specs=[away, away, here, here, away, away, away],
        out_specs=[here] * 4,
        scratch_shapes=[
            vmem((width, units), BF16), vmem((width, units), BF16), vmem((units, width), BF16),
            vmem((span, rows, width), BF16), vmem((span, rows, width), BF16), vmem((span, rows, width), BF16),
            vmem((span, rows, width), BF16),
            vmem((places, rows), F32), vmem((span, places, rows), F32),
            vmem((2, rows, units), F32), vmem((2, rows, units), F32),
            vmem((2, span, rows, units), BF16), vmem((span, rows, units), BF16), vmem((amount, units), BF16),
            vmem((outer, 2, feature, units), BF16), vmem((outer + 1, 2, feature, units), BF16),
            vmem((2, feature, units), F32), vmem((feature, units), BF16), vmem((feature, units), BF16),
            vmem((replicas, shard, width), BF16), vmem((outer, shard, width), BF16),
            vmem((outer + 1, shard, width), BF16),
            vmem((span, rows, width), BF16),
            vmem((span, rows, width), BF16), vmem((span, places, rows), F32), vmem((amount, units), BF16),
            dma((3,)), dma((2,)), dma((span,)), dma((span,)), dma((4,)), dma((4,)),
            dma((4, parts, chips)), dma((4, parts, chips)), dma((4, parts, chips)), dma((4, parts, chips)),
            dma, dma, dma((parts, chips)), dma((parts, chips)), dma((chips, 2)), dma((chips, 2)),
            dma((outer,)), dma((outer,)),
            dma((outer, 2, 2)), dma((outer + 1, 2, 2)), dma((outer, 2)), dma((outer + 1, 2)),
            dma((span,)), dma((span,)), dma, dma,
            dma, dma, dma((chips,)), dma((chips,)), dma, dma, dma, dma,
        ],
        compiler_params=pltpu.CompilerParams(
            collective_id=0, has_side_effects=True, vmem_limit_bytes=(54 + span) << 20
        ),
        name="fused",
    )(tokens, d_out, routes, gates, w_gate, w_up, w_down)


def store_kernel(*refs):
    sources, targets, sem = refs[:4], refs[4:8], refs[8]
    copies = [
        pltpu.make_async_copy(source, target if at == 0 else target.at[0], sem.at[at])
        for at, (source, target) in enumerate(zip(sources, targets))
    ]
    for copy in copies:
        copy.start()
    for copy in copies:
        copy.wait()


def store(arrays):
    shapes = [arrays[0].shape] + [(1,) + a.shape for a in arrays[1:]]
    return pl.pallas_call(
        store_kernel,
        out_shape=tuple(jax.ShapeDtypeStruct(s, a.dtype) for s, a in zip(shapes, arrays)),
        in_specs=[pl.BlockSpec(memory_space=pltpu.VMEM)] * 4,
        out_specs=[pl.BlockSpec(memory_space=pltpu.HBM)] * 4,
        scratch_shapes=[pltpu.SemaphoreType.DMA((4,))],
        compiler_params=pltpu.CompilerParams(vmem_limit_bytes=1 << 20),
        name="store",
    )(*arrays)


def body(tokens, d_out, routes, gate_fixed, w_gate, w_up, w_down):
    span = lax.axis_size("expert")
    replicas = lax.axis_size("dp")
    return store(fused(tokens, d_out, routes.T, gate_fixed.T, w_gate, w_up, w_down, span, replicas))


def solution(mesh):
    rows = P(("dp", "expert"), None)
    whole = P("expert", None, None)
    cut = P("expert", "dp", None)
    return jax.shard_map(
        body, mesh=mesh, in_specs=(rows,) * 4 + (whole,) * 3, out_specs=(rows, cut, cut, cut), check_vma=False
    )
```

```python
import functools

import jax
import jax.numpy as jnp
from jax import lax
from jax.experimental import pallas as pl
from jax.experimental.pallas import tpu as pltpu
from jax.sharding import PartitionSpec as P

MESH = pl.DeviceIdType.MESH
BF16 = jnp.bfloat16
F32 = jnp.float32


def greet(targets):
    barrier = pltpu.get_barrier_semaphore()
    for target in targets:
        pl.semaphore_signal(barrier, inc=1, device_id=target, device_id_type=MESH)
    pl.semaphore_wait(barrier, len(targets))


def outer_product(left, right):
    return lax.dot_general(left, right, (((0,), (0,)), ((), ())), preferred_element_type=F32)


def times_transposed(left, right):
    return lax.dot_general(left, right, (((1,), (1,)), ((), ())), preferred_element_type=F32)


def kernel(
    span, replicas, parts,
    x_ref, g_ref, routes_ref, gates_ref, wg_ref, wu_ref, wd_ref,
    tok_out, gate_out, up_out, down_out,
    wg, wu, wd, xs, gs, px, scaled, coef, cs, for_gate, for_up, acts, pact, hidden,
    grads, glines, total, cross_out, cross_in, dgrads, dnear, dlines, back, zg, zcs, zhid,
    w_sem, own_sem, c_send, c_recv, core_send, core_recv, chip_send, chip_recv, fwd_send, fwd_recv,
    px_send, px_recv, far_send, far_recv, act_send, act_recv, near_send, near_recv, gline_send, gline_recv,
    dline_send, dline_recv, back_send, back_recv, cross_send, cross_recv,
    z_send, z_recv, zh_send, zh_recv, zc_send, zc_recv, raw_send, raw_recv,
):
    expert = lax.axis_index("expert")
    me = lax.axis_index("dp")
    core = lax.rem(expert, 2)
    chip = expert // 2
    other = chip * 2 + (1 - core)
    chips = span // 2
    outer = replicas // 2
    side = lax.rem(me, 2)
    line = me // 2
    partner = line * 2 + (1 - side)
    lower = lax.rem(line + outer - 1, outer) * 2 + side
    upper = lax.rem(line + 1, outer) * 2 + side
    rows, width = x_ref.shape
    units = hidden.shape[1]
    feature = width // replicas
    shard = units // replicas
    piece_rows = rows // parts
    near_parts = parts - 1
    every = range(parts)
    inverse = 1.0 / replicas
    is_end = (line == 0) | (line == outer - 1)
    is_helper = (line == 1) | (line == outer - 2)
    inner = {"dp": jnp.where(line == 0, 1, outer - 2) * 2 + side}
    ended = jnp.where(line == 1, 0, outer - 1)

    own_x = pltpu.make_async_copy(x_ref, xs.at[expert], own_sem.at[0])
    own_g = pltpu.make_async_copy(g_ref, gs.at[expert], own_sem.at[1])
    loads = [
        pltpu.make_async_copy(source.at[0], target, w_sem.at[at])
        for at, (source, target) in enumerate(((wg_ref, wg), (wu_ref, wu), (wd_ref, wd)))
    ]
    own_x.start()
    loads[0].start()
    loads[1].start()
    own_g.start()
    loads[2].start()
    places = lax.broadcasted_iota(jnp.int32, coef.shape, 0)
    value = jnp.zeros(coef.shape, F32)
    for k in range(routes_ref.shape[0]):
        gate_value = gates_ref[k : k + 1, :].astype(F32) / 65536.0
        value = value + jnp.where(places == routes_ref[k : k + 1, :], gate_value, 0.0)
    coef[...] = value
    cs[expert] = value

    targets = [{"expert": lax.rem(expert + step, span)} for step in range(1, span)]
    targets += [{"dp": partner}, {"dp": lower}, {"dp": upper}]
    greet(targets)

    def remote(source, target, send, recv, device):
        return pltpu.make_async_remote_copy(
            src_ref=source, dst_ref=target, send_sem=send, recv_sem=recv, device_id=device, device_id_type=MESH
        )

    def piece(ref, part):
        return ref.at[pl.ds(part * piece_rows, piece_rows)]

    sources = (x_ref, g_ref, px.at[expert], zg.at[expert])
    arrays = (xs, gs, px, zg)

    def coef_copy(step):
        return remote(
            coef, cs.at[expert], c_send.at[step], c_recv.at[step], {"expert": lax.rem(expert + step, span)}
        )

    def core_copy(array):
        return remote(
            sources[array], arrays[array].at[expert], core_send.at[array], core_recv.at[array], {"expert": other}
        )

    def chip_copy(array, part, step):
        there = lax.rem(chip + step, chips) * 2 + core
        return remote(
            piece(sources[array], part), piece(arrays[array].at[expert], part),
            chip_send.at[array, part, step], chip_recv.at[array, part, step], {"expert": there},
        )

    def forward_copy(array, part, step, at_core):
        owner = lax.rem(chip + chips - step, chips) * 2 + at_core
        block = piece(arrays[array].at[owner], part)
        return remote(
            block, block, fwd_send.at[array, part, step], fwd_recv.at[array, part, step], {"expert": other}
        )

    def far_copy(part, step):
        owner = lax.rem(chip + chips - step, chips) * 2 + core
        return remote(
            piece(xs.at[owner], part), piece(px.at[owner], part),
            far_send.at[part, step], far_recv.at[part, step], {"dp": partner},
        )

    def pass_on(array, step, some):
        for part in some:
            if array == 2 and part >= near_parts:
                far_copy(part, step).wait_recv()
            else:
                chip_copy(array, part, step).wait_recv()
            forward_copy(array, part, step, core).start()
            if array == 0 and part >= near_parts:
                far_copy(part, step).start()

    def take_passed(array, step, some):
        for part in some:
            forward_copy(array, part, step, 1 - core).wait_recv()

    px_copy = remote(x_ref, px.at[expert], px_send, px_recv, {"dp": partner})

    def pair_rows(step):
        base = lax.rem(chip + chips - step, chips) * 2
        return pl.ds(pl.multiple_of(base * rows, 2 * rows), 2 * rows)

    def pair_piece(step, at):
        base = lax.rem(chip + chips - step, chips) * 2
        return pl.ds(base, 2), pl.ds(at * piece_rows, piece_rows)

    def act_copy(step, at):
        owners, those = pair_piece(step, at)
        return remote(
            acts.at[1 - side, owners, those], pact.at[owners, those],
            act_send.at[step, at], act_recv.at[step, at], {"dp": partner},
        )

    def back_copy(step):
        there = lax.rem(expert + step, span)
        return remote(gs.at[there], back.at[step], back_send.at[step], back_recv.at[step], {"expert": there})

    upside = line >= outer // 2
    nearest = jnp.where(upside, outer - 1 - line, line)

    def order_at(i):
        j = i + jnp.where(i >= 2 * nearest + 1, 1, 0)
        d = jnp.where(lax.rem(j, 2) == 0, outer - 1 - j // 2, j // 2)
        return jnp.where(i == outer - 1, line, jnp.where(upside, outer - 1 - d, d))

    def is_fed(d):
        return ((d > line) & (line > 0)) | ((d < line) & (line < outer - 1))

    def near_copy(d):
        return remote(
            dgrads.at[d * 2 + (1 - side)], dnear.at[d], near_send.at[d], near_recv.at[d], {"dp": partner}
        )

    def is_near(d):
        return (d == line) | jnp.logical_not(is_end | (is_helper & (d == ended)))

    raw_copy = remote(
        dgrads.at[ended * 2 + (1 - side)], dnear.at[line], raw_send, raw_recv, {"dp": ended * 2 + side}
    )

    def hop(d):
        following = jnp.where(d > line, line + 1, line - 1)
        slot = jnp.where((d < line) & (d == following), outer, d)
        return slot, {"dp": following * 2 + side}

    slices = 2
    fine = 4
    slice_rows = feature // fine
    slice_width = width // slices

    def gline_copy(d, s, q):
        slot, device = hop(d)
        those = pl.ds(q * slice_rows, slice_rows)
        return remote(
            grads.at[d, s, those], glines.at[slot, s, those],
            gline_send.at[d, s, q], gline_recv.at[slot, s, q], device,
        )

    def gline_wait(slot, s, q):
        block = glines.at[slot, s, pl.ds(q * slice_rows, slice_rows)]
        remote(block, block, gline_send.at[0, s, q], gline_recv.at[slot, s, q], {"dp": upper}).wait_recv()

    def dline_copy(d, q):
        slot, device = hop(d)
        those = pl.ds(q * slice_width, slice_width)
        return remote(
            dgrads.at[d * 2 + side, :, those], dlines.at[slot, :, those],
            dline_send.at[d, q], dline_recv.at[slot, q], device,
        )

    def dline_wait(slot, q):
        block = dlines.at[slot, :, pl.ds(q * slice_width, slice_width)]
        remote(block, block, dline_send.at[0, q], dline_recv.at[slot, q], {"dp": upper}).wait_recv()

    def is_fed_down(d):
        return ((d > line) & (line > 1)) | ((d < line) & (line < outer - 2))

    z_copy = remote(g_ref, zg.at[expert], z_send, z_recv, inner)

    def z_hidden(step):
        at = pair_rows(step)
        return remote(hidden.at[at], zhid.at[at], zh_send.at[step], zh_recv.at[step], inner)

    z_coef = remote(cs, zcs, zc_send, zc_recv, inner)

    halves = (1 - side, side)

    for step in range(1, span):
        coef_copy(step).start()
    for part in range(parts):
        for step in range(1, chips):
            chip_copy(0, part, step).start()
    core_copy(0).start()
    px_copy.start()
    core_copy(1).start()
    for part in range(parts):
        for step in range(1, chips):
            chip_copy(1, part, step).start()

    @pl.when(is_end)
    def _():
        z_copy.start()

    cut = units // 3

    def project(step):
        base = lax.rem(chip + chips - step, chips) * 2
        at = pair_rows(step)
        x = xs[pl.ds(base, 2)].reshape(2 * rows, width)
        for c in range(3):
            columns = slice(c * cut, (c + 1) * cut)
            pre_gate = jnp.dot(x, wg[:, columns], preferred_element_type=F32)
            pre_up = jnp.dot(x, wu[:, columns], preferred_element_type=F32)
            sigmoid_gate = 1.0 / (1.0 + jnp.exp(-pre_gate))
            silu_gate = pre_gate * sigmoid_gate
            hidden[at, columns] = (silu_gate * pre_up).astype(BF16)
            for_up[:, :, columns] = silu_gate.reshape(2, rows, cut)
            for_gate[:, :, columns] = (
                pre_up * sigmoid_gate * (1.0 + pre_gate * (1.0 - sigmoid_gate))
            ).reshape(2, rows, cut)

        @pl.when(is_end)
        def _():
            z_hidden(step).start()

    def weights(coefs, owner):
        row = lax.broadcasted_iota(jnp.int32, (rows, rows), 0)
        diagonal = row == lax.broadcasted_iota(jnp.int32, (rows, rows), 1)
        return jnp.sum(jnp.where(diagonal, coefs[owner, pl.ds(expert, 1), :], 0.0), axis=1, keepdims=True)

    def differentiate(step, at):
        base = lax.rem(chip + chips - step, chips) * 2
        owners, those = pair_piece(step, at)
        for j in range(2):
            weight = weights(cs, base + j)[at * piece_rows : (at + 1) * piece_rows]
            scaled[base + j, those] = (weight * gs[base + j, those].astype(F32)).astype(BF16)
        block = scaled[owners, those].reshape(2 * piece_rows, width)
        for c in range(3):
            columns = slice(c * cut, (c + 1) * cut)
            d_hidden = times_transposed(block, wd[columns, :]).reshape(2, piece_rows, cut)
            acts[0, owners, those, columns] = (d_hidden * for_gate[:, those, columns]).astype(BF16)
            acts[1, owners, those, columns] = (d_hidden * for_up[:, those, columns]).astype(BF16)
        act_copy(step, at).start()

    own_x.wait()
    loads[0].wait()
    loads[1].wait()
    core_copy(0).wait_recv()
    project(0)
    own_g.wait()
    loads[2].wait()
    core_copy(1).wait_recv()
    for step in range(1, span):
        coef_copy(step).wait_recv()

    @pl.when(is_end)
    def _():
        z_coef.start()

    for at in every:
        differentiate(0, at)
    px_copy.wait_recv()
    core_copy(2).start()
    for step in range(1, chips):
        pass_on(0, step, every)
        take_passed(0, step, every)
        project(step)
        if step == 1:
            for part in range(near_parts):
                for later in range(1, chips):
                    chip_copy(2, part, later).start()

            @pl.when(is_helper)
            def _():
                z_copy.wait_recv()
                core_copy(3).start()
                for part in range(parts):
                    for later in range(1, chips):
                        chip_copy(3, part, later).start()

        for at in every:
            pass_on(1, step, (at,))
            take_passed(1, step, (at,))
            differentiate(step, at)

    for array in range(2):
        for step in range(1, chips):
            for part in range(parts):
                forward_copy(array, part, step, core).wait_send()

    def route_pair(step, carry):
        base = lax.rem(chip + chips - step, chips) * 2
        pair = acts[:, pl.ds(base, 2)].reshape(2, 2 * rows, units)
        product = times_transposed(pair[0], wg[...]) + times_transposed(pair[1], wu[...])
        gs[base] = product[:rows].astype(BF16)
        gs[base + 1] = product[rows:].astype(BF16)
        return carry

    lax.fori_loop(0, chips, route_pair, 0)

    for step in range(1, chips):
        pass_on(2, step, every)
    for step in range(1, chips):
        take_passed(2, step, every)
    core_copy(2).wait_recv()
    for step in range(chips):
        for at in every:
            act_copy(step, at).wait_recv()

    def product_at(d):
        columns = pl.ds(pl.multiple_of(d * 2 * feature, 2 * feature), 2 * feature)
        return outer_product(
            xs[:, :, columns].reshape(span * rows, 2 * feature), acts[side].reshape(span * rows, units)
        ) + outer_product(
            px[:, :, columns].reshape(span * rows, 2 * feature), pact[...].reshape(span * rows, units)
        )

    def make(i, carry):
        d = order_at(i)
        product = product_at(d)
        grads[d, 0] = product[:feature].astype(BF16)
        grads[d, 1] = product[feature:].astype(BF16)

        @pl.when(jnp.logical_not(is_fed(d)))
        def _():
            for s in halves:
                for q in range(fine):
                    gline_copy(d, s, q).start()

        return carry

    lax.fori_loop(0, outer - 1, make, 0)
    product = product_at(line)
    total[0] = product[:feature]
    total[1] = product[feature:]

    for step in range(1, span):
        back_copy(step).start()

    def pass_gate(i, s, q):
        d = order_at(i)
        those = pl.ds(q * slice_rows, slice_rows)

        @pl.when(is_fed(d))
        def _():
            gline_wait(d, s, q)
            grads[d, s, those] = (grads[d, s, those].astype(F32) + glines[d, s, those].astype(F32)).astype(BF16)
            gline_copy(d, s, q).start()

    half = units // 2

    def down(helps, part):
        columns = pl.ds(pl.multiple_of(part * half, half), half)
        product = outer_product(hidden[:, columns], scaled[...].reshape(span * rows, width))
        if helps:
            product = product + outer_product(zhid[:, columns], zg[...].reshape(span * rows, width))
        for at in range(half // shard):
            dgrads[part * (half // shard) + at] = product[at * shard : (at + 1) * shard].astype(BF16)

    def down_part(part):
        @pl.when(is_helper)
        def _():
            down(True, part)

        @pl.when(jnp.logical_not(is_helper))
        def _():
            down(False, part)

        def start_near(i, carry):
            d = order_at(i)

            @pl.when((d // (outer // 2) == part) & is_near(d) & jnp.logical_not(is_end))
            def _():
                near_copy(d).start()

            return carry

        lax.fori_loop(0, outer, start_near, 0)

    far_part = jnp.where(upside, 0, 1)
    for q in range(3):
        pass_gate(0, halves[0], q)

    @pl.when(is_helper)
    def _():
        column = lax.broadcasted_iota(jnp.int32, (1, units), 1) // (2 * shard)
        kept = jnp.where(column == ended, 0.0, 1.0).astype(BF16)
        for step in range(chips):
            z_hidden(step).wait_recv()
        zhid[...] = zhid[...] * kept
        z_coef.wait_recv()
        for step in range(1, chips):
            pass_on(3, step, every)

    pass_gate(0, halves[0], 3)

    @pl.when(is_helper)
    def _():
        for step in range(1, chips):
            take_passed(3, step, every)
            for part in range(parts):
                forward_copy(3, part, step, core).wait_send()
                chip_copy(3, part, step).wait_send()
        core_copy(3).wait()
        for owner in range(span):
            zg[owner] = (weights(zcs, owner) * zg[owner].astype(F32)).astype(BF16)

    down_part(far_part)
    pass_gate(0, halves[1], 0)
    pass_gate(0, halves[1], 1)
    down_part(1 - far_part)

    @pl.when(is_helper)
    def _():
        raw_copy.start()

    pass_gate(0, halves[1], 2)
    pass_gate(0, halves[1], 3)

    def pass_gates(i, carry):
        for s in halves:
            for q in range(fine):
                pass_gate(i, s, q)
        return carry

    lax.fori_loop(1, outer - 1, pass_gates, 0)

    @pl.when(is_end)
    def _():
        helper = jnp.where(line == 0, 1, outer - 2)
        remote(
            dnear.at[helper], dnear.at[helper], raw_send, raw_recv, {"dp": partner}
        ).wait_recv()
        at = line * 2 + (1 - side)
        dgrads[at] = (dgrads[at].astype(F32) + dnear[helper].astype(F32)).astype(BF16)
        near_copy(line).start()

    def start_down(i, carry):
        d = order_at(i)
        at = d * 2 + side

        @pl.when(jnp.logical_not(is_end | is_fed_down(d)))
        def _():
            near_copy(d).wait_recv()
            for q in range(slices):
                those = slice(q * slice_width, (q + 1) * slice_width)
                dgrads[at, :, those] = (
                    dgrads[at, :, those].astype(F32) + dnear[d, :, those].astype(F32)
                ).astype(BF16)
                dline_copy(d, q).start()

        return carry

    lax.fori_loop(0, outer - 1, start_down, 0)

    for step in range(1, span):
        back_copy(step).wait_recv()
    route_sum = gs[expert].astype(F32)
    for step in range(1, span):
        route_sum = route_sum + back[step].astype(F32)
    tok_out[...] = route_sum.astype(BF16)

    def pass_down(i, carry):
        d = order_at(i)
        at = d * 2 + side

        @pl.when(jnp.logical_not(is_end) & is_fed_down(d))
        def _():
            @pl.when(is_near(d))
            def _():
                near_copy(d).wait_recv()
                for q in range(slices):
                    those = slice(q * slice_width, (q + 1) * slice_width)
                    dline_wait(d, q)
                    dgrads[at, :, those] = (
                        dgrads[at, :, those].astype(F32)
                        + dnear[d, :, those].astype(F32)
                        + dlines[d, :, those].astype(F32)
                    ).astype(BF16)
                    dline_copy(d, q).start()

            @pl.when(jnp.logical_not(is_near(d)))
            def _():
                for q in range(slices):
                    those = slice(q * slice_width, (q + 1) * slice_width)
                    dline_wait(d, q)
                    dgrads[at, :, those] = (
                        dgrads[at, :, those].astype(F32) + dlines[d, :, those].astype(F32)
                    ).astype(BF16)
                    dline_copy(d, q).start()

        return carry

    lax.fori_loop(0, outer - 1, pass_down, 0)

    cross = remote(cross_out, cross_in, cross_send, cross_recv, {"dp": partner})
    for s in halves:

        @pl.when(line > 0)
        def _():
            for q in range(fine):
                gline_wait(line, s, q)
            total[s] += glines[line, s].astype(F32)

        @pl.when(line < outer - 1)
        def _():
            for q in range(fine):
                gline_wait(outer, s, q)
            total[s] += glines[outer, s].astype(F32)

        if s is halves[0]:
            cross_out[...] = total[s].astype(BF16)
            cross.start()

    @pl.when(side == 0)
    def _():
        gate_out[...] = total[0] * inverse

    @pl.when(side == 1)
    def _():
        up_out[...] = total[1] * inverse

    near_copy(line).wait_recv()
    down_out[...] = (dgrads[me].astype(F32) + dnear[line].astype(F32)) * inverse
    cross.wait_recv()

    @pl.when(side == 0)
    def _():
        up_out[...] = cross_in[...].astype(F32) * inverse

    @pl.when(side == 1)
    def _():
        gate_out[...] = cross_in[...].astype(F32) * inverse

    @pl.when(line > 1)
    def _():
        for q in range(slices):
            those = slice(q * slice_width, (q + 1) * slice_width)
            dline_wait(line, q)
            down_out[:, those] += dlines[line, :, those].astype(F32) * inverse

    @pl.when(line < outer - 2)
    def _():
        for q in range(slices):
            those = slice(q * slice_width, (q + 1) * slice_width)
            dline_wait(outer, q)
            down_out[:, those] += dlines[outer, :, those].astype(F32) * inverse

    for step in range(1, span):
        coef_copy(step).wait_send()
        back_copy(step).wait_send()
    for array in range(3):
        core_copy(array).wait_send()
        for step in range(1, chips):
            for part in range(near_parts if array == 2 else parts):
                chip_copy(array, part, step).wait_send()
    for step in range(1, chips):
        for part in range(parts):
            forward_copy(2, part, step, core).wait_send()
            if part >= near_parts:
                far_copy(part, step).wait_send()
    px_copy.wait_send()
    for step in range(chips):
        for at in every:
            act_copy(step, at).wait_send()

    @pl.when(is_end)
    def _():
        for step in range(chips):
            z_hidden(step).wait_send()
        z_copy.wait_send()
        z_coef.wait_send()

    def finish(i, carry):
        d = order_at(i)

        @pl.when(is_near(d))
        def _():
            near_copy(d).wait_send()

        @pl.when(i < outer - 1)
        def _():
            for s in halves:
                for q in range(fine):
                    gline_copy(d, s, q).wait_send()

        @pl.when((i < outer - 1) & jnp.logical_not(is_end))
        def _():
            for q in range(slices):
                dline_copy(d, q).wait_send()

        return carry

    lax.fori_loop(0, outer, finish, 0)
    cross.wait_send()

    @pl.when(is_helper)
    def _():
        raw_copy.wait_send()


def fused(tokens, d_out, routes, gates, w_gate, w_up, w_down, span, replicas):
    parts = 4
    dma = pltpu.SemaphoreType.DMA
    rows, width = tokens.shape
    units = w_gate.shape[2]
    outer, chips = replicas // 2, span // 2
    feature, shard = width // replicas, units // replicas
    amount = span * rows
    here = pl.BlockSpec(memory_space=pltpu.VMEM)
    away = pl.BlockSpec(memory_space=pltpu.HBM)
    vmem = pltpu.VMEM
    places = max(8, span)
    return pl.pallas_call(
        functools.partial(kernel, span, replicas, parts),
        out_shape=(
            vmem((rows, width), BF16), vmem((feature, units), F32), vmem((feature, units), F32),
            vmem((shard, width), F32),
        ),
        in_specs=[away, away, here, here, away, away, away],
        out_specs=[here] * 4,
        scratch_shapes=[
            vmem((width, units), BF16), vmem((width, units), BF16), vmem((units, width), BF16),
            vmem((span, rows, width), BF16), vmem((span, rows, width), BF16), vmem((span, rows, width), BF16),
            vmem((span, rows, width), BF16),
            vmem((places, rows), F32), vmem((span, places, rows), F32),
            vmem((2, rows, units), F32), vmem((2, rows, units), F32),
            vmem((2, span, rows, units), BF16), vmem((span, rows, units), BF16), vmem((amount, units), BF16),
            vmem((outer, 2, feature, units), BF16), vmem((outer + 1, 2, feature, units), BF16),
            vmem((2, feature, units), F32), vmem((feature, units), BF16), vmem((feature, units), BF16),
            vmem((replicas, shard, width), BF16), vmem((outer, shard, width), BF16),
            vmem((outer + 1, shard, width), BF16),
            vmem((span, rows, width), BF16),
            vmem((span, rows, width), BF16), vmem((span, places, rows), F32), vmem((amount, units), BF16),
            dma((3,)), dma((2,)), dma((span,)), dma((span,)), dma((4,)), dma((4,)),
            dma((4, parts, chips)), dma((4, parts, chips)), dma((4, parts, chips)), dma((4, parts, chips)),
            dma, dma, dma((parts, chips)), dma((parts, chips)), dma((chips, parts)), dma((chips, parts)),
            dma((outer,)), dma((outer,)),
            dma((outer, 2, 4)), dma((outer + 1, 2, 4)), dma((outer, 2)), dma((outer + 1, 2)),
            dma((span,)), dma((span,)), dma, dma,
            dma, dma, dma((chips,)), dma((chips,)), dma, dma, dma, dma,
        ],
        compiler_params=pltpu.CompilerParams(
            collective_id=0, has_side_effects=True, vmem_limit_bytes=(54 + span) << 20
        ),
        name="fused",
    )(tokens, d_out, routes, gates, w_gate, w_up, w_down)


def store_kernel(*refs):
    sources, targets, sem = refs[:4], refs[4:8], refs[8]
    copies = [
        pltpu.make_async_copy(source, target if at == 0 else target.at[0], sem.at[at])
        for at, (source, target) in enumerate(zip(sources, targets))
    ]
    for copy in copies:
        copy.start()
    for copy in copies:
        copy.wait()


def store(arrays):
    shapes = [arrays[0].shape] + [(1,) + a.shape for a in arrays[1:]]
    return pl.pallas_call(
        store_kernel,
        out_shape=tuple(jax.ShapeDtypeStruct(s, a.dtype) for s, a in zip(shapes, arrays)),
        in_specs=[pl.BlockSpec(memory_space=pltpu.VMEM)] * 4,
        out_specs=[pl.BlockSpec(memory_space=pltpu.HBM)] * 4,
        scratch_shapes=[pltpu.SemaphoreType.DMA((4,))],
        compiler_params=pltpu.CompilerParams(vmem_limit_bytes=1 << 20),
        name="store",
    )(*arrays)


def body(tokens, d_out, routes, gate_fixed, w_gate, w_up, w_down):
    span = lax.axis_size("expert")
    replicas = lax.axis_size("dp")
    return store(fused(tokens, d_out, routes.T, gate_fixed.T, w_gate, w_up, w_down, span, replicas))


def solution(mesh):
    rows = P(("dp", "expert"), None)
    whole = P("expert", None, None)
    cut = P("expert", "dp", None)
    return jax.shard_map(
        body, mesh=mesh, in_specs=(rows,) * 4 + (whole,) * 3, out_specs=(rows, cut, cut, cut), check_vma=False
    )
```

```python
import functools

import jax
import jax.numpy as jnp
from jax import lax
from jax.experimental import pallas as pl
from jax.experimental.pallas import tpu as pltpu
from jax.sharding import PartitionSpec as P

MESH = pl.DeviceIdType.MESH
BF16 = jnp.bfloat16
F32 = jnp.float32


def greet(targets):
    barrier = pltpu.get_barrier_semaphore()
    for target in targets:
        pl.semaphore_signal(barrier, inc=1, device_id=target, device_id_type=MESH)
    pl.semaphore_wait(barrier, len(targets))


def outer_product(left, right):
    return lax.dot_general(left, right, (((0,), (0,)), ((), ())), preferred_element_type=F32)


def times_transposed(left, right):
    return lax.dot_general(left, right, (((1,), (1,)), ((), ())), preferred_element_type=F32)


def kernel(
    span, replicas, parts,
    x_ref, g_ref, routes_ref, gates_ref, wg_ref, wu_ref, wd_ref,
    tok_out, gate_out, up_out, down_out,
    wg, wu, wd, xs, gs, px, scaled, coef, cs, for_gate, for_up, acts, pact, hidden,
    grads, glines, total, cross_out, cross_in, dgrads, dnear, dlines, back, zg, zcs, zhid,
    w_sem, own_sem, c_send, c_recv, core_send, core_recv, chip_send, chip_recv, fwd_send, fwd_recv,
    px_send, px_recv, far_send, far_recv, act_send, act_recv, near_send, near_recv, gline_send, gline_recv,
    dline_send, dline_recv, back_send, back_recv, cross_send, cross_recv,
    z_send, z_recv, zh_send, zh_recv, zc_send, zc_recv, raw_send, raw_recv,
):
    expert = lax.axis_index("expert")
    me = lax.axis_index("dp")
    core = lax.rem(expert, 2)
    chip = expert // 2
    other = chip * 2 + (1 - core)
    chips = span // 2
    outer = replicas // 2
    side = lax.rem(me, 2)
    line = me // 2
    partner = line * 2 + (1 - side)
    lower = lax.rem(line + outer - 1, outer) * 2 + side
    upper = lax.rem(line + 1, outer) * 2 + side
    rows, width = x_ref.shape
    units = hidden.shape[1]
    feature = width // replicas
    shard = units // replicas
    piece_rows = rows // parts
    near_parts = parts - 1
    every = range(parts)
    inverse = 1.0 / replicas
    is_end = (line == 0) | (line == outer - 1)
    is_helper = (line == 1) | (line == outer - 2)
    inner = {"dp": jnp.where(line == 0, 1, outer - 2) * 2 + side}
    ended = jnp.where(line == 1, 0, outer - 1)

    own_x = pltpu.make_async_copy(x_ref, xs.at[expert], own_sem.at[0])
    own_g = pltpu.make_async_copy(g_ref, gs.at[expert], own_sem.at[1])
    loads = [
        pltpu.make_async_copy(source.at[0], target, w_sem.at[at])
        for at, (source, target) in enumerate(((wg_ref, wg), (wu_ref, wu), (wd_ref, wd)))
    ]
    own_x.start()
    loads[0].start()
    loads[1].start()
    own_g.start()
    loads[2].start()
    places = lax.broadcasted_iota(jnp.int32, coef.shape, 0)
    value = jnp.zeros(coef.shape, F32)
    for k in range(routes_ref.shape[0]):
        gate_value = gates_ref[k : k + 1, :].astype(F32) / 65536.0
        value = value + jnp.where(places == routes_ref[k : k + 1, :], gate_value, 0.0)
    coef[...] = value
    cs[expert] = value

    targets = [{"expert": lax.rem(expert + step, span)} for step in range(1, span)]
    targets += [{"dp": partner}, {"dp": lower}, {"dp": upper}]
    greet(targets)

    def remote(source, target, send, recv, device):
        return pltpu.make_async_remote_copy(
            src_ref=source, dst_ref=target, send_sem=send, recv_sem=recv, device_id=device, device_id_type=MESH
        )

    def piece(ref, part):
        return ref.at[pl.ds(part * piece_rows, piece_rows)]

    sources = (x_ref, g_ref, px.at[expert], zg.at[expert])
    arrays = (xs, gs, px, zg)

    def coef_copy(step):
        return remote(
            coef, cs.at[expert], c_send.at[step], c_recv.at[step], {"expert": lax.rem(expert + step, span)}
        )

    def core_copy(array):
        return remote(
            sources[array], arrays[array].at[expert], core_send.at[array], core_recv.at[array], {"expert": other}
        )

    def chip_copy(array, part, step):
        there = lax.rem(chip + step, chips) * 2 + core
        return remote(
            piece(sources[array], part), piece(arrays[array].at[expert], part),
            chip_send.at[array, part, step], chip_recv.at[array, part, step], {"expert": there},
        )

    def forward_copy(array, part, step, at_core):
        owner = lax.rem(chip + chips - step, chips) * 2 + at_core
        block = piece(arrays[array].at[owner], part)
        return remote(
            block, block, fwd_send.at[array, part, step], fwd_recv.at[array, part, step], {"expert": other}
        )

    def far_copy(part, step):
        owner = lax.rem(chip + chips - step, chips) * 2 + core
        return remote(
            piece(xs.at[owner], part), piece(px.at[owner], part),
            far_send.at[part, step], far_recv.at[part, step], {"dp": partner},
        )

    def pass_on(array, step, some):
        for part in some:
            if array == 2 and part >= near_parts:
                far_copy(part, step).wait_recv()
            else:
                chip_copy(array, part, step).wait_recv()
            forward_copy(array, part, step, core).start()
            if array == 0 and part >= near_parts:
                far_copy(part, step).start()

    def take_passed(array, step, some):
        for part in some:
            forward_copy(array, part, step, 1 - core).wait_recv()

    px_copy = remote(x_ref, px.at[expert], px_send, px_recv, {"dp": partner})

    def pair_rows(step):
        base = lax.rem(chip + chips - step, chips) * 2
        return pl.ds(pl.multiple_of(base * rows, 2 * rows), 2 * rows)

    def pair_piece(step, at):
        base = lax.rem(chip + chips - step, chips) * 2
        return pl.ds(base, 2), pl.ds(at * piece_rows, piece_rows)

    def act_copy(step, at):
        owners, those = pair_piece(step, at)
        return remote(
            acts.at[1 - side, owners, those], pact.at[owners, those],
            act_send.at[step, at], act_recv.at[step, at], {"dp": partner},
        )

    def back_copy(step):
        there = lax.rem(expert + step, span)
        return remote(gs.at[there], back.at[step], back_send.at[step], back_recv.at[step], {"expert": there})

    upside = line >= outer // 2
    nearest = jnp.where(upside, outer - 1 - line, line)

    def order_at(i):
        j = i + jnp.where(i >= 2 * nearest + 1, 1, 0)
        d = jnp.where(lax.rem(j, 2) == 0, outer - 1 - j // 2, j // 2)
        return jnp.where(i == outer - 1, line, jnp.where(upside, outer - 1 - d, d))

    def is_fed(d):
        return ((d > line) & (line > 0)) | ((d < line) & (line < outer - 1))

    def near_copy(d):
        return remote(
            dgrads.at[d * 2 + (1 - side)], dnear.at[d], near_send.at[d], near_recv.at[d], {"dp": partner}
        )

    def is_near(d):
        return (d == line) | jnp.logical_not(is_end | (is_helper & (d == ended)))

    raw_copy = remote(
        dgrads.at[ended * 2 + (1 - side)], dnear.at[line], raw_send, raw_recv, {"dp": ended * 2 + side}
    )

    def hop(d):
        following = jnp.where(d > line, line + 1, line - 1)
        slot = jnp.where((d < line) & (d == following), outer, d)
        return slot, {"dp": following * 2 + side}

    slices = 2
    fine = 4
    slice_rows = feature // fine
    slice_width = width // slices

    def gline_copy(d, s, q):
        slot, device = hop(d)
        those = pl.ds(q * slice_rows, slice_rows)
        return remote(
            grads.at[d, s, those], glines.at[slot, s, those],
            gline_send.at[d, s, q], gline_recv.at[slot, s, q], device,
        )

    def gline_wait(slot, s, q):
        block = glines.at[slot, s, pl.ds(q * slice_rows, slice_rows)]
        remote(block, block, gline_send.at[0, s, q], gline_recv.at[slot, s, q], {"dp": upper}).wait_recv()

    def dline_copy(d, q):
        slot, device = hop(d)
        those = pl.ds(q * slice_width, slice_width)
        return remote(
            dgrads.at[d * 2 + side, :, those], dlines.at[slot, :, those],
            dline_send.at[d, q], dline_recv.at[slot, q], device,
        )

    def dline_wait(slot, q):
        block = dlines.at[slot, :, pl.ds(q * slice_width, slice_width)]
        remote(block, block, dline_send.at[0, q], dline_recv.at[slot, q], {"dp": upper}).wait_recv()

    def is_fed_down(d):
        return ((d > line) & (line > 1)) | ((d < line) & (line < outer - 2))

    z_copy = remote(g_ref, zg.at[expert], z_send, z_recv, inner)

    def z_hidden(step):
        at = pair_rows(step)
        return remote(hidden.at[at], zhid.at[at], zh_send.at[step], zh_recv.at[step], inner)

    z_coef = remote(cs, zcs, zc_send, zc_recv, inner)

    halves = (1 - side, side)

    for step in range(1, span):
        coef_copy(step).start()
    for part in range(parts):
        for step in range(1, chips):
            chip_copy(0, part, step).start()
    core_copy(0).start()
    px_copy.start()
    core_copy(1).start()
    for part in range(parts):
        for step in range(1, chips):
            chip_copy(1, part, step).start()

    @pl.when(is_end)
    def _():
        z_copy.start()

    cut = units // 3

    def project(step):
        base = lax.rem(chip + chips - step, chips) * 2
        at = pair_rows(step)
        x = xs[pl.ds(base, 2)].reshape(2 * rows, width)
        for c in range(3):
            columns = slice(c * cut, (c + 1) * cut)
            pre_gate = jnp.dot(x, wg[:, columns], preferred_element_type=F32)
            pre_up = jnp.dot(x, wu[:, columns], preferred_element_type=F32)
            sigmoid_gate = 1.0 / (1.0 + jnp.exp(-pre_gate))
            silu_gate = pre_gate * sigmoid_gate
            hidden[at, columns] = (silu_gate * pre_up).astype(BF16)
            for_up[:, :, columns] = silu_gate.reshape(2, rows, cut)
            for_gate[:, :, columns] = (
                pre_up * sigmoid_gate * (1.0 + pre_gate * (1.0 - sigmoid_gate))
            ).reshape(2, rows, cut)

        @pl.when(is_end)
        def _():
            z_hidden(step).start()

    def weights(coefs, owner):
        row = lax.broadcasted_iota(jnp.int32, (rows, rows), 0)
        diagonal = row == lax.broadcasted_iota(jnp.int32, (rows, rows), 1)
        return jnp.sum(jnp.where(diagonal, coefs[owner, pl.ds(expert, 1), :], 0.0), axis=1, keepdims=True)

    def differentiate(step, at):
        base = lax.rem(chip + chips - step, chips) * 2
        owners, those = pair_piece(step, at)
        for j in range(2):
            weight = weights(cs, base + j)[at * piece_rows : (at + 1) * piece_rows]
            scaled[base + j, those] = (weight * gs[base + j, those].astype(F32)).astype(BF16)
        block = scaled[owners, those].reshape(2 * piece_rows, width)
        for c in range(3):
            columns = slice(c * cut, (c + 1) * cut)
            d_hidden = times_transposed(block, wd[columns, :]).reshape(2, piece_rows, cut)
            acts[0, owners, those, columns] = (d_hidden * for_gate[:, those, columns]).astype(BF16)
            acts[1, owners, those, columns] = (d_hidden * for_up[:, those, columns]).astype(BF16)
        act_copy(step, at).start()

    own_x.wait()
    loads[0].wait()
    loads[1].wait()
    core_copy(0).wait_recv()
    project(0)
    own_g.wait()
    loads[2].wait()
    core_copy(1).wait_recv()
    for step in range(1, span):
        coef_copy(step).wait_recv()

    @pl.when(is_end)
    def _():
        z_coef.start()

    for at in every:
        differentiate(0, at)
    px_copy.wait_recv()
    core_copy(2).start()
    for step in range(1, chips):
        pass_on(0, step, every)
        take_passed(0, step, every)
        project(step)
        if step == 1:
            for part in range(near_parts):
                for later in range(1, chips):
                    chip_copy(2, part, later).start()

            @pl.when(is_helper)
            def _():
                z_copy.wait_recv()
                core_copy(3).start()
                for part in range(parts):
                    for later in range(1, chips):
                        chip_copy(3, part, later).start()

        for at in every:
            pass_on(1, step, (at,))
            take_passed(1, step, (at,))
            differentiate(step, at)

    for array in range(2):
        for step in range(1, chips):
            for part in range(parts):
                forward_copy(array, part, step, core).wait_send()

    def route_pair(step, carry):
        base = lax.rem(chip + chips - step, chips) * 2
        pair = acts[:, pl.ds(base, 2)].reshape(2, 2 * rows, units)
        product = times_transposed(pair[0], wg[...]) + times_transposed(pair[1], wu[...])
        gs[base] = product[:rows].astype(BF16)
        gs[base + 1] = product[rows:].astype(BF16)
        return carry

    lax.fori_loop(0, chips, route_pair, 0)

    for step in range(1, chips):
        pass_on(2, step, every)
    for step in range(1, chips):
        take_passed(2, step, every)
    core_copy(2).wait_recv()
    for step in range(chips):
        for at in every:
            act_copy(step, at).wait_recv()

    def product_at(d):
        columns = pl.ds(pl.multiple_of(d * 2 * feature, 2 * feature), 2 * feature)
        return outer_product(
            xs[:, :, columns].reshape(span * rows, 2 * feature), acts[side].reshape(span * rows, units)
        ) + outer_product(
            px[:, :, columns].reshape(span * rows, 2 * feature), pact[...].reshape(span * rows, units)
        )

    def make(i, carry):
        d = order_at(i)
        product = product_at(d)
        grads[d, 0] = product[:feature].astype(BF16)
        grads[d, 1] = product[feature:].astype(BF16)

        @pl.when(jnp.logical_not(is_fed(d)))
        def _():
            for s in halves:
                for q in range(fine):
                    gline_copy(d, s, q).start()

        return carry

    lax.fori_loop(0, outer - 1, make, 0)
    product = product_at(line)
    total[0] = product[:feature]
    total[1] = product[feature:]

    for step in range(1, span):
        back_copy(step).start()

    def pass_gate(i, s, q):
        d = order_at(i)
        those = pl.ds(q * slice_rows, slice_rows)

        @pl.when(is_fed(d))
        def _():
            gline_wait(d, s, q)
            grads[d, s, those] = (grads[d, s, those].astype(F32) + glines[d, s, those].astype(F32)).astype(BF16)
            gline_copy(d, s, q).start()

    half = units // 2

    def down(helps, part):
        columns = pl.ds(pl.multiple_of(part * half, half), half)
        product = outer_product(hidden[:, columns], scaled[...].reshape(span * rows, width))
        if helps:
            product = product + outer_product(zhid[:, columns], zg[...].reshape(span * rows, width))
        for at in range(half // shard):
            dgrads[part * (half // shard) + at] = product[at * shard : (at + 1) * shard].astype(BF16)

    def down_part(part):
        @pl.when(is_helper)
        def _():
            down(True, part)

        @pl.when(jnp.logical_not(is_helper))
        def _():
            down(False, part)

        def start_near(i, carry):
            d = order_at(i)

            @pl.when((d // (outer // 2) == part) & is_near(d) & jnp.logical_not(is_end))
            def _():
                near_copy(d).start()

            return carry

        lax.fori_loop(0, outer, start_near, 0)

    far_part = jnp.where(upside, 0, 1)
    for q in range(3):
        pass_gate(0, halves[0], q)

    @pl.when(is_helper)
    def _():
        column = lax.broadcasted_iota(jnp.int32, (1, units), 1) // (2 * shard)
        kept = jnp.where(column == ended, 0.0, 1.0).astype(BF16)
        for step in range(chips):
            z_hidden(step).wait_recv()
        zhid[...] = zhid[...] * kept
        z_coef.wait_recv()
        for step in range(1, chips):
            pass_on(3, step, every)

    pass_gate(0, halves[0], 3)

    @pl.when(is_helper)
    def _():
        for step in range(1, chips):
            take_passed(3, step, every)
            for part in range(parts):
                forward_copy(3, part, step, core).wait_send()
                chip_copy(3, part, step).wait_send()
        core_copy(3).wait()
        for owner in range(span):
            zg[owner] = (weights(zcs, owner) * zg[owner].astype(F32)).astype(BF16)

    down_part(far_part)
    pass_gate(0, halves[1], 0)
    pass_gate(0, halves[1], 1)
    down_part(1 - far_part)

    @pl.when(is_helper)
    def _():
        raw_copy.start()

    pass_gate(0, halves[1], 2)
    pass_gate(0, halves[1], 3)

    def start_down(i, carry):
        d = order_at(i)
        at = d * 2 + side

        @pl.when(jnp.logical_not(is_end | is_fed_down(d)))
        def _():
            near_copy(d).wait_recv()
            for q in range(slices):
                those = slice(q * slice_width, (q + 1) * slice_width)
                dgrads[at, :, those] = (
                    dgrads[at, :, those].astype(F32) + dnear[d, :, those].astype(F32)
                ).astype(BF16)
                dline_copy(d, q).start()

        return carry

    def pass_gates(i, carry):
        for s in halves:
            for q in range(fine):
                pass_gate(i, s, q)
        return carry

    lax.fori_loop(1, 2, pass_gates, 0)
    start_down(0, 0)
    lax.fori_loop(2, outer - 1, pass_gates, 0)

    @pl.when(is_end)
    def _():
        helper = jnp.where(line == 0, 1, outer - 2)
        remote(
            dnear.at[helper], dnear.at[helper], raw_send, raw_recv, {"dp": partner}
        ).wait_recv()
        at = line * 2 + (1 - side)
        dgrads[at] = (dgrads[at].astype(F32) + dnear[helper].astype(F32)).astype(BF16)
        near_copy(line).start()

    lax.fori_loop(1, outer - 1, start_down, 0)

    for step in range(1, span):
        back_copy(step).wait_recv()
    route_sum = gs[expert].astype(F32)
    for step in range(1, span):
        route_sum = route_sum + back[step].astype(F32)
    tok_out[...] = route_sum.astype(BF16)

    def pass_down(i, carry):
        d = order_at(i)
        at = d * 2 + side

        @pl.when(jnp.logical_not(is_end) & is_fed_down(d))
        def _():
            @pl.when(is_near(d))
            def _():
                near_copy(d).wait_recv()
                for q in range(slices):
                    those = slice(q * slice_width, (q + 1) * slice_width)
                    dline_wait(d, q)
                    dgrads[at, :, those] = (
                        dgrads[at, :, those].astype(F32)
                        + dnear[d, :, those].astype(F32)
                        + dlines[d, :, those].astype(F32)
                    ).astype(BF16)
                    dline_copy(d, q).start()

            @pl.when(jnp.logical_not(is_near(d)))
            def _():
                for q in range(slices):
                    those = slice(q * slice_width, (q + 1) * slice_width)
                    dline_wait(d, q)
                    dgrads[at, :, those] = (
                        dgrads[at, :, those].astype(F32) + dlines[d, :, those].astype(F32)
                    ).astype(BF16)
                    dline_copy(d, q).start()

        return carry

    lax.fori_loop(0, outer - 1, pass_down, 0)

    cross = remote(cross_out, cross_in, cross_send, cross_recv, {"dp": partner})
    for s in halves:

        @pl.when(line > 0)
        def _():
            for q in range(fine):
                gline_wait(line, s, q)
            total[s] += glines[line, s].astype(F32)

        @pl.when(line < outer - 1)
        def _():
            for q in range(fine):
                gline_wait(outer, s, q)
            total[s] += glines[outer, s].astype(F32)

        if s is halves[0]:
            cross_out[...] = total[s].astype(BF16)
            cross.start()

    @pl.when(side == 0)
    def _():
        gate_out[...] = total[0] * inverse

    @pl.when(side == 1)
    def _():
        up_out[...] = total[1] * inverse

    near_copy(line).wait_recv()
    down_out[...] = (dgrads[me].astype(F32) + dnear[line].astype(F32)) * inverse
    cross.wait_recv()

    @pl.when(side == 0)
    def _():
        up_out[...] = cross_in[...].astype(F32) * inverse

    @pl.when(side == 1)
    def _():
        gate_out[...] = cross_in[...].astype(F32) * inverse

    @pl.when(line > 1)
    def _():
        for q in range(slices):
            those = slice(q * slice_width, (q + 1) * slice_width)
            dline_wait(line, q)
            down_out[:, those] += dlines[line, :, those].astype(F32) * inverse

    @pl.when(line < outer - 2)
    def _():
        for q in range(slices):
            those = slice(q * slice_width, (q + 1) * slice_width)
            dline_wait(outer, q)
            down_out[:, those] += dlines[outer, :, those].astype(F32) * inverse

    for step in range(1, span):
        coef_copy(step).wait_send()
        back_copy(step).wait_send()
    for array in range(3):
        core_copy(array).wait_send()
        for step in range(1, chips):
            for part in range(near_parts if array == 2 else parts):
                chip_copy(array, part, step).wait_send()
    for step in range(1, chips):
        for part in range(parts):
            forward_copy(2, part, step, core).wait_send()
            if part >= near_parts:
                far_copy(part, step).wait_send()
    px_copy.wait_send()
    for step in range(chips):
        for at in every:
            act_copy(step, at).wait_send()

    @pl.when(is_end)
    def _():
        for step in range(chips):
            z_hidden(step).wait_send()
        z_copy.wait_send()
        z_coef.wait_send()

    def finish(i, carry):
        d = order_at(i)

        @pl.when(is_near(d))
        def _():
            near_copy(d).wait_send()

        @pl.when(i < outer - 1)
        def _():
            for s in halves:
                for q in range(fine):
                    gline_copy(d, s, q).wait_send()

        @pl.when((i < outer - 1) & jnp.logical_not(is_end))
        def _():
            for q in range(slices):
                dline_copy(d, q).wait_send()

        return carry

    lax.fori_loop(0, outer, finish, 0)
    cross.wait_send()

    @pl.when(is_helper)
    def _():
        raw_copy.wait_send()


def fused(tokens, d_out, routes, gates, w_gate, w_up, w_down, span, replicas):
    parts = 4
    dma = pltpu.SemaphoreType.DMA
    rows, width = tokens.shape
    units = w_gate.shape[2]
    outer, chips = replicas // 2, span // 2
    feature, shard = width // replicas, units // replicas
    amount = span * rows
    here = pl.BlockSpec(memory_space=pltpu.VMEM)
    away = pl.BlockSpec(memory_space=pltpu.HBM)
    vmem = pltpu.VMEM
    places = max(8, span)
    return pl.pallas_call(
        functools.partial(kernel, span, replicas, parts),
        out_shape=(
            vmem((rows, width), BF16), vmem((feature, units), F32), vmem((feature, units), F32),
            vmem((shard, width), F32),
        ),
        in_specs=[away, away, here, here, away, away, away],
        out_specs=[here] * 4,
        scratch_shapes=[
            vmem((width, units), BF16), vmem((width, units), BF16), vmem((units, width), BF16),
            vmem((span, rows, width), BF16), vmem((span, rows, width), BF16), vmem((span, rows, width), BF16),
            vmem((span, rows, width), BF16),
            vmem((places, rows), F32), vmem((span, places, rows), F32),
            vmem((2, rows, units), F32), vmem((2, rows, units), F32),
            vmem((2, span, rows, units), BF16), vmem((span, rows, units), BF16), vmem((amount, units), BF16),
            vmem((outer, 2, feature, units), BF16), vmem((outer + 1, 2, feature, units), BF16),
            vmem((2, feature, units), F32), vmem((feature, units), BF16), vmem((feature, units), BF16),
            vmem((replicas, shard, width), BF16), vmem((outer, shard, width), BF16),
            vmem((outer + 1, shard, width), BF16),
            vmem((span, rows, width), BF16),
            vmem((span, rows, width), BF16), vmem((span, places, rows), F32), vmem((amount, units), BF16),
            dma((3,)), dma((2,)), dma((span,)), dma((span,)), dma((4,)), dma((4,)),
            dma((4, parts, chips)), dma((4, parts, chips)), dma((4, parts, chips)), dma((4, parts, chips)),
            dma, dma, dma((parts, chips)), dma((parts, chips)), dma((chips, parts)), dma((chips, parts)),
            dma((outer,)), dma((outer,)),
            dma((outer, 2, 4)), dma((outer + 1, 2, 4)), dma((outer, 2)), dma((outer + 1, 2)),
            dma((span,)), dma((span,)), dma, dma,
            dma, dma, dma((chips,)), dma((chips,)), dma, dma, dma, dma,
        ],
        compiler_params=pltpu.CompilerParams(
            collective_id=0, has_side_effects=True, vmem_limit_bytes=(54 + span) << 20
        ),
        name="fused",
    )(tokens, d_out, routes, gates, w_gate, w_up, w_down)


def store_kernel(*refs):
    sources, targets, sem = refs[:4], refs[4:8], refs[8]
    copies = [
        pltpu.make_async_copy(source, target if at == 0 else target.at[0], sem.at[at])
        for at, (source, target) in enumerate(zip(sources, targets))
    ]
    for copy in copies:
        copy.start()
    for copy in copies:
        copy.wait()


def store(arrays):
    shapes = [arrays[0].shape] + [(1,) + a.shape for a in arrays[1:]]
    return pl.pallas_call(
        store_kernel,
        out_shape=tuple(jax.ShapeDtypeStruct(s, a.dtype) for s, a in zip(shapes, arrays)),
        in_specs=[pl.BlockSpec(memory_space=pltpu.VMEM)] * 4,
        out_specs=[pl.BlockSpec(memory_space=pltpu.HBM)] * 4,
        scratch_shapes=[pltpu.SemaphoreType.DMA((4,))],
        compiler_params=pltpu.CompilerParams(vmem_limit_bytes=1 << 20),
        name="store",
    )(*arrays)


def body(tokens, d_out, routes, gate_fixed, w_gate, w_up, w_down):
    span = lax.axis_size("expert")
    replicas = lax.axis_size("dp")
    return store(fused(tokens, d_out, routes.T, gate_fixed.T, w_gate, w_up, w_down, span, replicas))


def solution(mesh):
    rows = P(("dp", "expert"), None)
    whole = P("expert", None, None)
    cut = P("expert", "dp", None)
    return jax.shard_map(
        body, mesh=mesh, in_specs=(rows,) * 4 + (whole,) * 3, out_specs=(rows, cut, cut, cut), check_vma=False
    )
```

```python
import functools

import jax
import jax.numpy as jnp
from jax import lax
from jax.experimental import pallas as pl
from jax.experimental.pallas import tpu as pltpu
from jax.sharding import PartitionSpec as P

MESH = pl.DeviceIdType.MESH
BF16 = jnp.bfloat16
F32 = jnp.float32


def greet(targets):
    barrier = pltpu.get_barrier_semaphore()
    for target in targets:
        pl.semaphore_signal(barrier, inc=1, device_id=target, device_id_type=MESH)
    pl.semaphore_wait(barrier, len(targets))


def outer_product(left, right):
    return lax.dot_general(left, right, (((0,), (0,)), ((), ())), preferred_element_type=F32)


def times_transposed(left, right):
    return lax.dot_general(left, right, (((1,), (1,)), ((), ())), preferred_element_type=F32)


def kernel(
    span, replicas, parts,
    x_ref, g_ref, routes_ref, gates_ref, wg_ref, wu_ref, wd_ref,
    tok_out, gate_out, up_out, down_out,
    wg, wu, wd, xs, gs, px, scaled, coef, cs, for_gate, for_up, acts, pact, hidden,
    grads, glines, total, cross_out, cross_in, dgrads, dnear, dlines, back, zg, zcs, zhid,
    w_sem, own_sem, c_send, c_recv, core_send, core_recv, chip_send, chip_recv, fwd_send, fwd_recv,
    px_send, px_recv, far_send, far_recv, act_send, act_recv, near_send, near_recv, gline_send, gline_recv,
    dline_send, dline_recv, back_send, back_recv, cross_send, cross_recv,
    z_send, z_recv, zh_send, zh_recv, zc_send, zc_recv, raw_send, raw_recv,
):
    expert = lax.axis_index("expert")
    me = lax.axis_index("dp")
    core = lax.rem(expert, 2)
    chip = expert // 2
    other = chip * 2 + (1 - core)
    chips = span // 2
    outer = replicas // 2
    side = lax.rem(me, 2)
    line = me // 2
    partner = line * 2 + (1 - side)
    lower = lax.rem(line + outer - 1, outer) * 2 + side
    upper = lax.rem(line + 1, outer) * 2 + side
    rows, width = x_ref.shape
    units = hidden.shape[1]
    feature = width // replicas
    shard = units // replicas
    piece_rows = rows // parts
    near_parts = parts - 1
    every = range(parts)
    inverse = 1.0 / replicas
    is_end = (line == 0) | (line == outer - 1)
    is_helper = (line == 1) | (line == outer - 2)
    inner = {"dp": jnp.where(line == 0, 1, outer - 2) * 2 + side}
    ended = jnp.where(line == 1, 0, outer - 1)

    own_x = pltpu.make_async_copy(x_ref, xs.at[expert], own_sem.at[0])
    own_g = pltpu.make_async_copy(g_ref, gs.at[expert], own_sem.at[1])
    loads = [
        pltpu.make_async_copy(source.at[0], target, w_sem.at[at])
        for at, (source, target) in enumerate(((wg_ref, wg), (wu_ref, wu), (wd_ref, wd)))
    ]
    own_x.start()
    loads[0].start()
    loads[1].start()
    own_g.start()
    loads[2].start()
    places = lax.broadcasted_iota(jnp.int32, coef.shape, 0)
    value = jnp.zeros(coef.shape, F32)
    for k in range(routes_ref.shape[0]):
        gate_value = gates_ref[k : k + 1, :].astype(F32) / 65536.0
        value = value + jnp.where(places == routes_ref[k : k + 1, :], gate_value, 0.0)
    coef[...] = value
    cs[expert] = value

    targets = [{"expert": lax.rem(expert + step, span)} for step in range(1, span)]
    targets += [{"dp": partner}, {"dp": lower}, {"dp": upper}]
    greet(targets)

    def remote(source, target, send, recv, device):
        return pltpu.make_async_remote_copy(
            src_ref=source, dst_ref=target, send_sem=send, recv_sem=recv, device_id=device, device_id_type=MESH
        )

    def piece(ref, part):
        return ref.at[pl.ds(part * piece_rows, piece_rows)]

    sources = (x_ref, g_ref, px.at[expert], zg.at[expert])
    arrays = (xs, gs, px, zg)

    def coef_copy(step):
        return remote(
            coef, cs.at[expert], c_send.at[step], c_recv.at[step], {"expert": lax.rem(expert + step, span)}
        )

    def core_copy(array):
        return remote(
            sources[array], arrays[array].at[expert], core_send.at[array], core_recv.at[array], {"expert": other}
        )

    def chip_copy(array, part, step):
        there = lax.rem(chip + step, chips) * 2 + core
        return remote(
            piece(sources[array], part), piece(arrays[array].at[expert], part),
            chip_send.at[array, part, step], chip_recv.at[array, part, step], {"expert": there},
        )

    def forward_copy(array, part, step, at_core):
        owner = lax.rem(chip + chips - step, chips) * 2 + at_core
        block = piece(arrays[array].at[owner], part)
        return remote(
            block, block, fwd_send.at[array, part, step], fwd_recv.at[array, part, step], {"expert": other}
        )

    def far_copy(part, step):
        owner = lax.rem(chip + chips - step, chips) * 2 + core
        return remote(
            piece(xs.at[owner], part), piece(px.at[owner], part),
            far_send.at[part, step], far_recv.at[part, step], {"dp": partner},
        )

    def pass_on(array, step, some):
        for part in some:
            if array == 2 and part >= near_parts:
                far_copy(part, step).wait_recv()
            else:
                chip_copy(array, part, step).wait_recv()
            forward_copy(array, part, step, core).start()
            if array == 0 and part >= near_parts:
                far_copy(part, step).start()

    def take_passed(array, step, some):
        for part in some:
            forward_copy(array, part, step, 1 - core).wait_recv()

    px_copy = remote(x_ref, px.at[expert], px_send, px_recv, {"dp": partner})

    def pair_rows(step):
        base = lax.rem(chip + chips - step, chips) * 2
        return pl.ds(pl.multiple_of(base * rows, 2 * rows), 2 * rows)

    def pair_piece(step, at):
        base = lax.rem(chip + chips - step, chips) * 2
        return pl.ds(base, 2), pl.ds(at * piece_rows, piece_rows)

    def act_copy(step, at):
        owners, those = pair_piece(step, at)
        return remote(
            acts.at[1 - side, owners, those], pact.at[owners, those],
            act_send.at[step, at], act_recv.at[step, at], {"dp": partner},
        )

    def back_copy(step):
        there = lax.rem(expert + step, span)
        return remote(gs.at[there], back.at[step], back_send.at[step], back_recv.at[step], {"expert": there})

    upside = line >= outer // 2
    nearest = jnp.where(upside, outer - 1 - line, line)

    def order_at(i):
        j = i + jnp.where(i >= 2 * nearest + 1, 1, 0)
        d = jnp.where(lax.rem(j, 2) == 0, outer - 1 - j // 2, j // 2)
        return jnp.where(i == outer - 1, line, jnp.where(upside, outer - 1 - d, d))

    def is_fed(d):
        return ((d > line) & (line > 0)) | ((d < line) & (line < outer - 1))

    def near_copy(d):
        return remote(
            dgrads.at[d * 2 + (1 - side)], dnear.at[d], near_send.at[d], near_recv.at[d], {"dp": partner}
        )

    def is_near(d):
        return (d == line) | jnp.logical_not(is_end | (is_helper & (d == ended)))

    raw_copy = remote(
        dgrads.at[ended * 2 + (1 - side)], dnear.at[line], raw_send, raw_recv, {"dp": ended * 2 + side}
    )

    def hop(d):
        following = jnp.where(d > line, line + 1, line - 1)
        slot = jnp.where((d < line) & (d == following), outer, d)
        return slot, {"dp": following * 2 + side}

    slices = 2
    fine = 4
    slice_rows = feature // fine
    slice_width = width // slices

    def gline_copy(d, s, q):
        slot, device = hop(d)
        those = pl.ds(q * slice_rows, slice_rows)
        return remote(
            grads.at[d, s, those], glines.at[slot, s, those],
            gline_send.at[d, s, q], gline_recv.at[slot, s, q], device,
        )

    def gline_wait(slot, s, q):
        block = glines.at[slot, s, pl.ds(q * slice_rows, slice_rows)]
        remote(block, block, gline_send.at[0, s, q], gline_recv.at[slot, s, q], {"dp": upper}).wait_recv()

    def dline_copy(d, q):
        slot, device = hop(d)
        those = pl.ds(q * slice_width, slice_width)
        return remote(
            dgrads.at[d * 2 + side, :, those], dlines.at[slot, :, those],
            dline_send.at[d, q], dline_recv.at[slot, q], device,
        )

    def dline_wait(slot, q):
        block = dlines.at[slot, :, pl.ds(q * slice_width, slice_width)]
        remote(block, block, dline_send.at[0, q], dline_recv.at[slot, q], {"dp": upper}).wait_recv()

    def is_fed_down(d):
        return ((d > line) & (line > 1)) | ((d < line) & (line < outer - 2))

    z_copy = remote(g_ref, zg.at[expert], z_send, z_recv, inner)

    def z_hidden(step):
        at = pair_rows(step)
        return remote(hidden.at[at], zhid.at[at], zh_send.at[step], zh_recv.at[step], inner)

    z_coef = remote(cs, zcs, zc_send, zc_recv, inner)

    halves = (1 - side, side)

    for step in range(1, span):
        coef_copy(step).start()
    for part in range(parts):
        for step in range(1, chips):
            chip_copy(0, part, step).start()
    core_copy(0).start()
    px_copy.start()
    core_copy(1).start()
    for part in range(parts):
        for step in range(1, chips):
            chip_copy(1, part, step).start()

    @pl.when(is_end)
    def _():
        z_copy.start()

    cut = units // 3

    def project(step):
        base = lax.rem(chip + chips - step, chips) * 2
        at = pair_rows(step)
        x = xs[pl.ds(base, 2)].reshape(2 * rows, width)
        for c in range(3):
            columns = slice(c * cut, (c + 1) * cut)
            pre_gate = jnp.dot(x, wg[:, columns], preferred_element_type=F32)
            pre_up = jnp.dot(x, wu[:, columns], preferred_element_type=F32)
            sigmoid_gate = 1.0 / (1.0 + jnp.exp(-pre_gate))
            silu_gate = pre_gate * sigmoid_gate
            hidden[at, columns] = (silu_gate * pre_up).astype(BF16)
            for_up[:, :, columns] = silu_gate.reshape(2, rows, cut)
            for_gate[:, :, columns] = (
                pre_up * sigmoid_gate * (1.0 + pre_gate * (1.0 - sigmoid_gate))
            ).reshape(2, rows, cut)

        @pl.when(is_end)
        def _():
            z_hidden(step).start()

    def weights(coefs, owner):
        row = lax.broadcasted_iota(jnp.int32, (rows, rows), 0)
        diagonal = row == lax.broadcasted_iota(jnp.int32, (rows, rows), 1)
        return jnp.sum(jnp.where(diagonal, coefs[owner, pl.ds(expert, 1), :], 0.0), axis=1, keepdims=True)

    def differentiate(step, at):
        base = lax.rem(chip + chips - step, chips) * 2
        owners, those = pair_piece(step, at)
        for j in range(2):
            weight = weights(cs, base + j)[at * piece_rows : (at + 1) * piece_rows]
            scaled[base + j, those] = (weight * gs[base + j, those].astype(F32)).astype(BF16)
        block = scaled[owners, those].reshape(2 * piece_rows, width)
        for c in range(3):
            columns = slice(c * cut, (c + 1) * cut)
            d_hidden = times_transposed(block, wd[columns, :]).reshape(2, piece_rows, cut)
            acts[0, owners, those, columns] = (d_hidden * for_gate[:, those, columns]).astype(BF16)
            acts[1, owners, those, columns] = (d_hidden * for_up[:, those, columns]).astype(BF16)
        act_copy(step, at).start()

    own_x.wait()
    loads[0].wait()
    loads[1].wait()
    core_copy(0).wait_recv()
    project(0)
    own_g.wait()
    loads[2].wait()
    core_copy(1).wait_recv()
    for step in range(1, span):
        coef_copy(step).wait_recv()

    @pl.when(is_end)
    def _():
        z_coef.start()

    for at in every:
        differentiate(0, at)
    px_copy.wait_recv()
    core_copy(2).start()
    for step in range(1, chips):
        pass_on(0, step, every)
        take_passed(0, step, every)
        project(step)
        if step == 1:
            for part in range(near_parts):
                for later in range(1, chips):
                    chip_copy(2, part, later).start()

            @pl.when(is_helper)
            def _():
                z_copy.wait_recv()
                core_copy(3).start()
                for part in range(parts):
                    for later in range(1, chips):
                        chip_copy(3, part, later).start()

        for at in every:
            pass_on(1, step, (at,))
            take_passed(1, step, (at,))
            differentiate(step, at)

    for array in range(2):
        for step in range(1, chips):
            for part in range(parts):
                forward_copy(array, part, step, core).wait_send()

    def route_pair(step, carry):
        base = lax.rem(chip + chips - step, chips) * 2
        pair = acts[:, pl.ds(base, 2)].reshape(2, 2 * rows, units)
        product = times_transposed(pair[0], wg[...]) + times_transposed(pair[1], wu[...])
        gs[base] = product[:rows].astype(BF16)
        gs[base + 1] = product[rows:].astype(BF16)
        return carry

    lax.fori_loop(0, chips, route_pair, 0)

    for step in range(1, chips):
        pass_on(2, step, every)
    for step in range(1, chips):
        take_passed(2, step, every)
    core_copy(2).wait_recv()
    for step in range(chips):
        for at in every:
            act_copy(step, at).wait_recv()

    def product_at(d):
        columns = pl.ds(pl.multiple_of(d * 2 * feature, 2 * feature), 2 * feature)
        return outer_product(
            xs[:, :, columns].reshape(span * rows, 2 * feature), acts[side].reshape(span * rows, units)
        ) + outer_product(
            px[:, :, columns].reshape(span * rows, 2 * feature), pact[...].reshape(span * rows, units)
        )

    def make(i, carry):
        d = order_at(i)
        product = product_at(d)
        grads[d, 0] = product[:feature].astype(BF16)
        grads[d, 1] = product[feature:].astype(BF16)

        @pl.when(jnp.logical_not(is_fed(d)))
        def _():
            for s in halves:
                for q in range(fine):
                    gline_copy(d, s, q).start()

        return carry

    lax.fori_loop(0, outer - 1, make, 0)

    for step in range(1, span):
        back_copy(step).start()

    def pass_gate(i, s, q):
        d = order_at(i)
        those = pl.ds(q * slice_rows, slice_rows)

        @pl.when(is_fed(d))
        def _():
            gline_wait(d, s, q)
            grads[d, s, those] = (grads[d, s, those].astype(F32) + glines[d, s, those].astype(F32)).astype(BF16)
            gline_copy(d, s, q).start()

    half = units // 2

    def down(helps, part):
        columns = pl.ds(pl.multiple_of(part * half, half), half)
        product = outer_product(hidden[:, columns], scaled[...].reshape(span * rows, width))
        if helps:
            product = product + outer_product(zhid[:, columns], zg[...].reshape(span * rows, width))
        for at in range(half // shard):
            dgrads[part * (half // shard) + at] = product[at * shard : (at + 1) * shard].astype(BF16)

    def down_part(part):
        @pl.when(is_helper)
        def _():
            down(True, part)

        @pl.when(jnp.logical_not(is_helper))
        def _():
            down(False, part)

        def start_near(i, carry):
            d = order_at(i)

            @pl.when((d // (outer // 2) == part) & is_near(d) & jnp.logical_not(is_end))
            def _():
                near_copy(d).start()

            return carry

        lax.fori_loop(0, outer, start_near, 0)

    far_part = jnp.where(upside, 0, 1)
    pass_gate(0, halves[0], 0)
    product = product_at(line)
    total[0] = product[:feature]
    total[1] = product[feature:]
    pass_gate(0, halves[0], 1)
    pass_gate(0, halves[0], 2)

    @pl.when(is_helper)
    def _():
        column = lax.broadcasted_iota(jnp.int32, (1, units), 1) // (2 * shard)
        kept = jnp.where(column == ended, 0.0, 1.0).astype(BF16)
        for step in range(chips):
            z_hidden(step).wait_recv()
        zhid[...] = zhid[...] * kept
        z_coef.wait_recv()
        for step in range(1, chips):
            pass_on(3, step, every)

    pass_gate(0, halves[0], 3)

    @pl.when(is_helper)
    def _():
        for step in range(1, chips):
            take_passed(3, step, every)
            for part in range(parts):
                forward_copy(3, part, step, core).wait_send()
                chip_copy(3, part, step).wait_send()
        core_copy(3).wait()
        for owner in range(span):
            zg[owner] = (weights(zcs, owner) * zg[owner].astype(F32)).astype(BF16)

    down_part(far_part)
    pass_gate(0, halves[1], 0)
    pass_gate(0, halves[1], 1)
    down_part(1 - far_part)

    @pl.when(is_helper)
    def _():
        raw_copy.start()

    pass_gate(0, halves[1], 2)
    pass_gate(0, halves[1], 3)

    def start_down(i, carry):
        d = order_at(i)
        at = d * 2 + side

        @pl.when(jnp.logical_not(is_end | is_fed_down(d)))
        def _():
            near_copy(d).wait_recv()
            for q in range(slices):
                those = slice(q * slice_width, (q + 1) * slice_width)
                dgrads[at, :, those] = (
                    dgrads[at, :, those].astype(F32) + dnear[d, :, those].astype(F32)
                ).astype(BF16)
                dline_copy(d, q).start()

        return carry

    def pass_gates(i, carry):
        for s in halves:
            for q in range(fine):
                pass_gate(i, s, q)
        return carry

    lax.fori_loop(1, 2, pass_gates, 0)
    start_down(0, 0)
    lax.fori_loop(2, outer - 1, pass_gates, 0)

    @pl.when(is_end)
    def _():
        helper = jnp.where(line == 0, 1, outer - 2)
        remote(
            dnear.at[helper], dnear.at[helper], raw_send, raw_recv, {"dp": partner}
        ).wait_recv()
        at = line * 2 + (1 - side)
        dgrads[at] = (dgrads[at].astype(F32) + dnear[helper].astype(F32)).astype(BF16)
        near_copy(line).start()

    lax.fori_loop(1, outer - 1, start_down, 0)

    for step in range(1, span):
        back_copy(step).wait_recv()
    route_sum = gs[expert].astype(F32)
    for step in range(1, span):
        route_sum = route_sum + back[step].astype(F32)
    tok_out[...] = route_sum.astype(BF16)

    def pass_down(i, carry):
        d = order_at(i)
        at = d * 2 + side

        @pl.when(jnp.logical_not(is_end) & is_fed_down(d))
        def _():
            @pl.when(is_near(d))
            def _():
                near_copy(d).wait_recv()
                for q in range(slices):
                    those = slice(q * slice_width, (q + 1) * slice_width)
                    dline_wait(d, q)
                    dgrads[at, :, those] = (
                        dgrads[at, :, those].astype(F32)
                        + dnear[d, :, those].astype(F32)
                        + dlines[d, :, those].astype(F32)
                    ).astype(BF16)
                    dline_copy(d, q).start()

            @pl.when(jnp.logical_not(is_near(d)))
            def _():
                for q in range(slices):
                    those = slice(q * slice_width, (q + 1) * slice_width)
                    dline_wait(d, q)
                    dgrads[at, :, those] = (
                        dgrads[at, :, those].astype(F32) + dlines[d, :, those].astype(F32)
                    ).astype(BF16)
                    dline_copy(d, q).start()

        return carry

    lax.fori_loop(0, outer - 1, pass_down, 0)

    cross = remote(cross_out, cross_in, cross_send, cross_recv, {"dp": partner})
    for s in halves:

        @pl.when(line > 0)
        def _():
            for q in range(fine):
                gline_wait(line, s, q)
            total[s] += glines[line, s].astype(F32)

        @pl.when(line < outer - 1)
        def _():
            for q in range(fine):
                gline_wait(outer, s, q)
            total[s] += glines[outer, s].astype(F32)

        if s is halves[0]:
            cross_out[...] = total[s].astype(BF16)
            cross.start()

    @pl.when(side == 0)
    def _():
        gate_out[...] = total[0] * inverse

    @pl.when(side == 1)
    def _():
        up_out[...] = total[1] * inverse

    near_copy(line).wait_recv()
    down_out[...] = (dgrads[me].astype(F32) + dnear[line].astype(F32)) * inverse
    cross.wait_recv()

    @pl.when(side == 0)
    def _():
        up_out[...] = cross_in[...].astype(F32) * inverse

    @pl.when(side == 1)
    def _():
        gate_out[...] = cross_in[...].astype(F32) * inverse

    @pl.when(line > 1)
    def _():
        for q in range(slices):
            those = slice(q * slice_width, (q + 1) * slice_width)
            dline_wait(line, q)
            down_out[:, those] += dlines[line, :, those].astype(F32) * inverse

    @pl.when(line < outer - 2)
    def _():
        for q in range(slices):
            those = slice(q * slice_width, (q + 1) * slice_width)
            dline_wait(outer, q)
            down_out[:, those] += dlines[outer, :, those].astype(F32) * inverse

    for step in range(1, span):
        coef_copy(step).wait_send()
        back_copy(step).wait_send()
    for array in range(3):
        core_copy(array).wait_send()
        for step in range(1, chips):
            for part in range(near_parts if array == 2 else parts):
                chip_copy(array, part, step).wait_send()
    for step in range(1, chips):
        for part in range(parts):
            forward_copy(2, part, step, core).wait_send()
            if part >= near_parts:
                far_copy(part, step).wait_send()
    px_copy.wait_send()
    for step in range(chips):
        for at in every:
            act_copy(step, at).wait_send()

    @pl.when(is_end)
    def _():
        for step in range(chips):
            z_hidden(step).wait_send()
        z_copy.wait_send()
        z_coef.wait_send()

    def finish(i, carry):
        d = order_at(i)

        @pl.when(is_near(d))
        def _():
            near_copy(d).wait_send()

        @pl.when(i < outer - 1)
        def _():
            for s in halves:
                for q in range(fine):
                    gline_copy(d, s, q).wait_send()

        @pl.when((i < outer - 1) & jnp.logical_not(is_end))
        def _():
            for q in range(slices):
                dline_copy(d, q).wait_send()

        return carry

    lax.fori_loop(0, outer, finish, 0)
    cross.wait_send()

    @pl.when(is_helper)
    def _():
        raw_copy.wait_send()


def fused(tokens, d_out, routes, gates, w_gate, w_up, w_down, span, replicas):
    parts = 4
    dma = pltpu.SemaphoreType.DMA
    rows, width = tokens.shape
    units = w_gate.shape[2]
    outer, chips = replicas // 2, span // 2
    feature, shard = width // replicas, units // replicas
    amount = span * rows
    here = pl.BlockSpec(memory_space=pltpu.VMEM)
    away = pl.BlockSpec(memory_space=pltpu.HBM)
    vmem = pltpu.VMEM
    places = max(8, span)
    return pl.pallas_call(
        functools.partial(kernel, span, replicas, parts),
        out_shape=(
            vmem((rows, width), BF16), vmem((feature, units), F32), vmem((feature, units), F32),
            vmem((shard, width), F32),
        ),
        in_specs=[away, away, here, here, away, away, away],
        out_specs=[here] * 4,
        scratch_shapes=[
            vmem((width, units), BF16), vmem((width, units), BF16), vmem((units, width), BF16),
            vmem((span, rows, width), BF16), vmem((span, rows, width), BF16), vmem((span, rows, width), BF16),
            vmem((span, rows, width), BF16),
            vmem((places, rows), F32), vmem((span, places, rows), F32),
            vmem((2, rows, units), F32), vmem((2, rows, units), F32),
            vmem((2, span, rows, units), BF16), vmem((span, rows, units), BF16), vmem((amount, units), BF16),
            vmem((outer, 2, feature, units), BF16), vmem((outer + 1, 2, feature, units), BF16),
            vmem((2, feature, units), F32), vmem((feature, units), BF16), vmem((feature, units), BF16),
            vmem((replicas, shard, width), BF16), vmem((outer, shard, width), BF16),
            vmem((outer + 1, shard, width), BF16),
            vmem((span, rows, width), BF16),
            vmem((span, rows, width), BF16), vmem((span, places, rows), F32), vmem((amount, units), BF16),
            dma((3,)), dma((2,)), dma((span,)), dma((span,)), dma((4,)), dma((4,)),
            dma((4, parts, chips)), dma((4, parts, chips)), dma((4, parts, chips)), dma((4, parts, chips)),
            dma, dma, dma((parts, chips)), dma((parts, chips)), dma((chips, parts)), dma((chips, parts)),
            dma((outer,)), dma((outer,)),
            dma((outer, 2, 4)), dma((outer + 1, 2, 4)), dma((outer, 2)), dma((outer + 1, 2)),
            dma((span,)), dma((span,)), dma, dma,
            dma, dma, dma((chips,)), dma((chips,)), dma, dma, dma, dma,
        ],
        compiler_params=pltpu.CompilerParams(
            collective_id=0, has_side_effects=True, vmem_limit_bytes=(54 + span) << 20
        ),
        name="fused",
    )(tokens, d_out, routes, gates, w_gate, w_up, w_down)


def store_kernel(*refs):
    sources, targets, sem = refs[:4], refs[4:8], refs[8]
    copies = [
        pltpu.make_async_copy(source, target if at == 0 else target.at[0], sem.at[at])
        for at, (source, target) in enumerate(zip(sources, targets))
    ]
    for copy in copies:
        copy.start()
    for copy in copies:
        copy.wait()


def store(arrays):
    shapes = [arrays[0].shape] + [(1,) + a.shape for a in arrays[1:]]
    return pl.pallas_call(
        store_kernel,
        out_shape=tuple(jax.ShapeDtypeStruct(s, a.dtype) for s, a in zip(shapes, arrays)),
        in_specs=[pl.BlockSpec(memory_space=pltpu.VMEM)] * 4,
        out_specs=[pl.BlockSpec(memory_space=pltpu.HBM)] * 4,
        scratch_shapes=[pltpu.SemaphoreType.DMA((4,))],
        compiler_params=pltpu.CompilerParams(vmem_limit_bytes=1 << 20),
        name="store",
    )(*arrays)


def body(tokens, d_out, routes, gate_fixed, w_gate, w_up, w_down):
    span = lax.axis_size("expert")
    replicas = lax.axis_size("dp")
    return store(fused(tokens, d_out, routes.T, gate_fixed.T, w_gate, w_up, w_down, span, replicas))


def solution(mesh):
    rows = P(("dp", "expert"), None)
    whole = P("expert", None, None)
    cut = P("expert", "dp", None)
    return jax.shard_map(
        body, mesh=mesh, in_specs=(rows,) * 4 + (whole,) * 3, out_specs=(rows, cut, cut, cut), check_vma=False
    )
```

```python
import functools

import jax
import jax.numpy as jnp
from jax import lax
from jax.experimental import pallas as pl
from jax.experimental.pallas import tpu as pltpu
from jax.sharding import PartitionSpec as P

MESH = pl.DeviceIdType.MESH
BF16 = jnp.bfloat16
F32 = jnp.float32


def greet(targets):
    barrier = pltpu.get_barrier_semaphore()
    for target in targets:
        pl.semaphore_signal(barrier, inc=1, device_id=target, device_id_type=MESH)
    pl.semaphore_wait(barrier, len(targets))


def outer_product(left, right):
    return lax.dot_general(left, right, (((0,), (0,)), ((), ())), preferred_element_type=F32)


def times_transposed(left, right):
    return lax.dot_general(left, right, (((1,), (1,)), ((), ())), preferred_element_type=F32)


def kernel(
    span, replicas, parts,
    x_ref, g_ref, routes_ref, gates_ref, wg_ref, wu_ref, wd_ref,
    tok_out, gate_out, up_out, down_out,
    wg, wu, wd, xs, gs, px, scaled, coef, cs, for_gate, for_up, acts, pact, hidden,
    grads, glines, total, cross_out, cross_in, dgrads, dnear, dlines, back, zg, zcs, zhid,
    w_sem, own_sem, c_send, c_recv, core_send, core_recv, chip_send, chip_recv, fwd_send, fwd_recv,
    px_send, px_recv, far_send, far_recv, act_send, act_recv, near_send, near_recv, gline_send, gline_recv,
    dline_send, dline_recv, back_send, back_recv, cross_send, cross_recv,
    z_send, z_recv, zh_send, zh_recv, zc_send, zc_recv, raw_send, raw_recv,
):
    expert = lax.axis_index("expert")
    me = lax.axis_index("dp")
    core = lax.rem(expert, 2)
    chip = expert // 2
    other = chip * 2 + (1 - core)
    chips = span // 2
    outer = replicas // 2
    side = lax.rem(me, 2)
    line = me // 2
    partner = line * 2 + (1 - side)
    lower = lax.rem(line + outer - 1, outer) * 2 + side
    upper = lax.rem(line + 1, outer) * 2 + side
    rows, width = x_ref.shape
    units = hidden.shape[1]
    feature = width // replicas
    shard = units // replicas
    piece_rows = rows // parts
    near_parts = parts - 1
    every = range(parts)
    inverse = 1.0 / replicas
    is_end = (line == 0) | (line == outer - 1)
    is_helper = (line == 1) | (line == outer - 2)
    inner = {"dp": jnp.where(line == 0, 1, outer - 2) * 2 + side}
    ended = jnp.where(line == 1, 0, outer - 1)

    own_x = pltpu.make_async_copy(x_ref, xs.at[expert], own_sem.at[0])
    own_g = pltpu.make_async_copy(g_ref, gs.at[expert], own_sem.at[1])
    loads = [
        pltpu.make_async_copy(source.at[0], target, w_sem.at[at])
        for at, (source, target) in enumerate(((wg_ref, wg), (wu_ref, wu), (wd_ref, wd)))
    ]
    own_x.start()
    loads[0].start()
    loads[1].start()
    own_g.start()
    loads[2].start()
    places = lax.broadcasted_iota(jnp.int32, coef.shape, 0)
    value = jnp.zeros(coef.shape, F32)
    for k in range(routes_ref.shape[0]):
        gate_value = gates_ref[k : k + 1, :].astype(F32) / 65536.0
        value = value + jnp.where(places == routes_ref[k : k + 1, :], gate_value, 0.0)
    coef[...] = value
    cs[expert] = value

    targets = [{"expert": lax.rem(expert + step, span)} for step in range(1, span)]
    targets += [{"dp": partner}, {"dp": lower}, {"dp": upper}]
    greet(targets)

    def remote(source, target, send, recv, device):
        return pltpu.make_async_remote_copy(
            src_ref=source, dst_ref=target, send_sem=send, recv_sem=recv, device_id=device, device_id_type=MESH
        )

    def piece(ref, part):
        return ref.at[pl.ds(part * piece_rows, piece_rows)]

    sources = (x_ref, g_ref, px.at[expert], zg.at[expert])
    arrays = (xs, gs, px, zg)

    def coef_copy(step):
        return remote(
            coef, cs.at[expert], c_send.at[step], c_recv.at[step], {"expert": lax.rem(expert + step, span)}
        )

    def core_copy(array):
        return remote(
            sources[array], arrays[array].at[expert], core_send.at[array], core_recv.at[array], {"expert": other}
        )

    def chip_copy(array, part, step):
        there = lax.rem(chip + step, chips) * 2 + core
        return remote(
            piece(sources[array], part), piece(arrays[array].at[expert], part),
            chip_send.at[array, part, step], chip_recv.at[array, part, step], {"expert": there},
        )

    def forward_copy(array, part, step, at_core):
        owner = lax.rem(chip + chips - step, chips) * 2 + at_core
        block = piece(arrays[array].at[owner], part)
        return remote(
            block, block, fwd_send.at[array, part, step], fwd_recv.at[array, part, step], {"expert": other}
        )

    def far_copy(part, step):
        owner = lax.rem(chip + chips - step, chips) * 2 + core
        return remote(
            piece(xs.at[owner], part), piece(px.at[owner], part),
            far_send.at[part, step], far_recv.at[part, step], {"dp": partner},
        )

    def pass_on(array, step, some):
        for part in some:
            if array == 2 and part >= near_parts:
                far_copy(part, step).wait_recv()
            else:
                chip_copy(array, part, step).wait_recv()
            forward_copy(array, part, step, core).start()
            if array == 0 and part >= near_parts:
                far_copy(part, step).start()

    def take_passed(array, step, some):
        for part in some:
            forward_copy(array, part, step, 1 - core).wait_recv()

    px_copy = remote(x_ref, px.at[expert], px_send, px_recv, {"dp": partner})

    def pair_rows(step):
        base = lax.rem(chip + chips - step, chips) * 2
        return pl.ds(pl.multiple_of(base * rows, 2 * rows), 2 * rows)

    def pair_piece(step, at):
        base = lax.rem(chip + chips - step, chips) * 2
        return pl.ds(base, 2), pl.ds(at * piece_rows, piece_rows)

    def act_copy(step, at):
        owners, those = pair_piece(step, at)
        return remote(
            acts.at[1 - side, owners, those], pact.at[owners, those],
            act_send.at[step, at], act_recv.at[step, at], {"dp": partner},
        )

    def back_copy(step):
        there = lax.rem(expert + step, span)
        return remote(gs.at[there], back.at[step], back_send.at[step], back_recv.at[step], {"expert": there})

    upside = line >= outer // 2
    nearest = jnp.where(upside, outer - 1 - line, line)

    def order_at(i):
        j = i + jnp.where(i >= 2 * nearest + 1, 1, 0)
        d = jnp.where(lax.rem(j, 2) == 0, outer - 1 - j // 2, j // 2)
        return jnp.where(i == outer - 1, line, jnp.where(upside, outer - 1 - d, d))

    def is_fed(d):
        return ((d > line) & (line > 0)) | ((d < line) & (line < outer - 1))

    def near_copy(d):
        return remote(
            dgrads.at[d * 2 + (1 - side)], dnear.at[d], near_send.at[d], near_recv.at[d], {"dp": partner}
        )

    def is_near(d):
        return (d == line) | jnp.logical_not(is_end | (is_helper & (d == ended)))

    raw_copy = remote(
        dgrads.at[ended * 2 + (1 - side)], dnear.at[line], raw_send, raw_recv, {"dp": ended * 2 + side}
    )

    def hop(d):
        following = jnp.where(d > line, line + 1, line - 1)
        slot = jnp.where((d < line) & (d == following), outer, d)
        return slot, {"dp": following * 2 + side}

    slices = 2
    fine = 4
    slice_rows = feature // fine
    slice_width = width // slices

    def gline_copy(d, s, q):
        slot, device = hop(d)
        those = pl.ds(q * slice_rows, slice_rows)
        return remote(
            grads.at[d, s, those], glines.at[slot, s, those],
            gline_send.at[d, s, q], gline_recv.at[slot, s, q], device,
        )

    def gline_wait(slot, s, q):
        block = glines.at[slot, s, pl.ds(q * slice_rows, slice_rows)]
        remote(block, block, gline_send.at[0, s, q], gline_recv.at[slot, s, q], {"dp": upper}).wait_recv()

    def dline_copy(d, q):
        slot, device = hop(d)
        those = pl.ds(q * slice_width, slice_width)
        return remote(
            dgrads.at[d * 2 + side, :, those], dlines.at[slot, :, those],
            dline_send.at[d, q], dline_recv.at[slot, q], device,
        )

    def dline_wait(slot, q):
        block = dlines.at[slot, :, pl.ds(q * slice_width, slice_width)]
        remote(block, block, dline_send.at[0, q], dline_recv.at[slot, q], {"dp": upper}).wait_recv()

    def is_fed_down(d):
        return ((d > line) & (line > 1)) | ((d < line) & (line < outer - 2))

    z_copy = remote(g_ref, zg.at[expert], z_send, z_recv, inner)

    def z_hidden(step):
        at = pair_rows(step)
        return remote(hidden.at[at], zhid.at[at], zh_send.at[step], zh_recv.at[step], inner)

    z_coef = remote(cs, zcs, zc_send, zc_recv, inner)

    halves = (1 - side, side)

    for step in range(1, span):
        coef_copy(step).start()
    for part in range(parts):
        for step in range(1, chips):
            chip_copy(0, part, step).start()
    core_copy(0).start()
    px_copy.start()
    core_copy(1).start()
    for part in range(parts):
        for step in range(1, chips):
            chip_copy(1, part, step).start()

    @pl.when(is_end)
    def _():
        z_copy.start()

    cut = units // 3

    def project(step):
        base = lax.rem(chip + chips - step, chips) * 2
        at = pair_rows(step)
        x = xs[pl.ds(base, 2)].reshape(2 * rows, width)
        for c in range(3):
            columns = slice(c * cut, (c + 1) * cut)
            pre_gate = jnp.dot(x, wg[:, columns], preferred_element_type=F32)
            pre_up = jnp.dot(x, wu[:, columns], preferred_element_type=F32)
            sigmoid_gate = 1.0 / (1.0 + jnp.exp(-pre_gate))
            silu_gate = pre_gate * sigmoid_gate
            hidden[at, columns] = (silu_gate * pre_up).astype(BF16)
            for_up[:, :, columns] = silu_gate.reshape(2, rows, cut)
            for_gate[:, :, columns] = (
                pre_up * sigmoid_gate * (1.0 + pre_gate * (1.0 - sigmoid_gate))
            ).reshape(2, rows, cut)

        @pl.when(is_end)
        def _():
            z_hidden(step).start()

    def weights(coefs, owner):
        row = lax.broadcasted_iota(jnp.int32, (rows, rows), 0)
        diagonal = row == lax.broadcasted_iota(jnp.int32, (rows, rows), 1)
        return jnp.sum(jnp.where(diagonal, coefs[owner, pl.ds(expert, 1), :], 0.0), axis=1, keepdims=True)

    def differentiate(step, at):
        base = lax.rem(chip + chips - step, chips) * 2
        owners, those = pair_piece(step, at)
        for j in range(2):
            weight = weights(cs, base + j)[at * piece_rows : (at + 1) * piece_rows]
            scaled[base + j, those] = (weight * gs[base + j, those].astype(F32)).astype(BF16)
        block = scaled[owners, those].reshape(2 * piece_rows, width)
        for c in range(3):
            columns = slice(c * cut, (c + 1) * cut)
            d_hidden = times_transposed(block, wd[columns, :]).reshape(2, piece_rows, cut)
            acts[0, owners, those, columns] = (d_hidden * for_gate[:, those, columns]).astype(BF16)
            acts[1, owners, those, columns] = (d_hidden * for_up[:, those, columns]).astype(BF16)
        act_copy(step, at).start()

    own_x.wait()
    loads[0].wait()
    loads[1].wait()
    core_copy(0).wait_recv()
    project(0)
    own_g.wait()
    loads[2].wait()
    core_copy(1).wait_recv()
    for step in range(1, span):
        coef_copy(step).wait_recv()

    @pl.when(is_end)
    def _():
        z_coef.start()

    for at in every:
        differentiate(0, at)
    px_copy.wait_recv()
    core_copy(2).start()
    for step in range(1, chips):
        pass_on(0, step, every)
        take_passed(0, step, every)
        project(step)
        if step == 1:
            for part in range(near_parts):
                for later in range(1, chips):
                    chip_copy(2, part, later).start()

            @pl.when(is_helper)
            def _():
                z_copy.wait_recv()
                core_copy(3).start()
                for part in range(parts):
                    for later in range(1, chips):
                        chip_copy(3, part, later).start()

        for at in every:
            pass_on(1, step, (at,))
            take_passed(1, step, (at,))
            differentiate(step, at)

    for array in range(2):
        for step in range(1, chips):
            for part in range(parts):
                forward_copy(array, part, step, core).wait_send()

    def route_pair(step, carry):
        base = lax.rem(chip + chips - step, chips) * 2
        pair = acts[:, pl.ds(base, 2)].reshape(2, 2 * rows, units)
        product = times_transposed(pair[0], wg[...]) + times_transposed(pair[1], wu[...])
        gs[base] = product[:rows].astype(BF16)
        gs[base + 1] = product[rows:].astype(BF16)
        return carry

    lax.fori_loop(0, chips, route_pair, 0)

    for step in range(1, chips):
        pass_on(2, step, every)
    for step in range(1, chips):
        take_passed(2, step, every)
    core_copy(2).wait_recv()
    for step in range(chips):
        for at in every:
            act_copy(step, at).wait_recv()

    def product_at(d):
        columns = pl.ds(pl.multiple_of(d * 2 * feature, 2 * feature), 2 * feature)
        return outer_product(
            xs[:, :, columns].reshape(span * rows, 2 * feature), acts[side].reshape(span * rows, units)
        ) + outer_product(
            px[:, :, columns].reshape(span * rows, 2 * feature), pact[...].reshape(span * rows, units)
        )

    def make(i, carry):
        d = order_at(i)
        product = product_at(d)
        grads[d, 0] = product[:feature].astype(BF16)
        grads[d, 1] = product[feature:].astype(BF16)

        @pl.when(jnp.logical_not(is_fed(d)))
        def _():
            for s in halves:
                for q in range(fine):
                    gline_copy(d, s, q).start()

        return carry

    lax.fori_loop(0, outer - 1, make, 0)
    product = product_at(line)
    total[0] = product[:feature]
    total[1] = product[feature:]

    for step in range(1, span):
        back_copy(step).start()

    def pass_gate(i, s, q):
        d = order_at(i)
        those = pl.ds(q * slice_rows, slice_rows)

        @pl.when(is_fed(d))
        def _():
            gline_wait(d, s, q)
            grads[d, s, those] = (grads[d, s, those].astype(F32) + glines[d, s, those].astype(F32)).astype(BF16)
            gline_copy(d, s, q).start()

    half = units // 2

    def down(helps, part):
        columns = pl.ds(pl.multiple_of(part * half, half), half)
        product = outer_product(hidden[:, columns], scaled[...].reshape(span * rows, width))
        if helps:
            product = product + outer_product(zhid[:, columns], zg[...].reshape(span * rows, width))
        for at in range(half // shard):
            dgrads[part * (half // shard) + at] = product[at * shard : (at + 1) * shard].astype(BF16)

    def down_part(part):
        @pl.when(is_helper)
        def _():
            down(True, part)

        @pl.when(jnp.logical_not(is_helper))
        def _():
            down(False, part)

        def start_near(i, carry):
            d = order_at(i)

            @pl.when((d // (outer // 2) == part) & is_near(d) & jnp.logical_not(is_end))
            def _():
                near_copy(d).start()

            return carry

        lax.fori_loop(0, outer, start_near, 0)

    far_part = jnp.where(upside, 0, 1)
    for q in range(3):
        pass_gate(0, halves[0], q)

    @pl.when(is_helper)
    def _():
        column = lax.broadcasted_iota(jnp.int32, (1, units), 1) // (2 * shard)
        kept = jnp.where(column == ended, 0.0, 1.0).astype(BF16)
        for step in range(chips):
            z_hidden(step).wait_recv()
        zhid[...] = zhid[...] * kept
        z_coef.wait_recv()
        for step in range(1, chips):
            pass_on(3, step, every)

    pass_gate(0, halves[0], 3)

    @pl.when(is_helper)
    def _():
        for step in range(1, chips):
            take_passed(3, step, every)
            for part in range(parts):
                forward_copy(3, part, step, core).wait_send()
                chip_copy(3, part, step).wait_send()
        core_copy(3).wait()
        for owner in range(span):
            zg[owner] = (weights(zcs, owner) * zg[owner].astype(F32)).astype(BF16)

    down_part(far_part)
    pass_gate(0, halves[1], 0)
    pass_gate(0, halves[1], 1)
    down_part(1 - far_part)

    @pl.when(is_helper)
    def _():
        raw_copy.start()

    pass_gate(0, halves[1], 2)
    pass_gate(0, halves[1], 3)

    def start_down(i, carry):
        d = order_at(i)
        at = d * 2 + side

        @pl.when(jnp.logical_not(is_end | is_fed_down(d)))
        def _():
            near_copy(d).wait_recv()
            for q in range(slices):
                those = slice(q * slice_width, (q + 1) * slice_width)
                dgrads[at, :, those] = (
                    dgrads[at, :, those].astype(F32) + dnear[d, :, those].astype(F32)
                ).astype(BF16)
                dline_copy(d, q).start()

        return carry

    def pass_gates(i, carry):
        for s in halves:
            for q in range(fine):
                pass_gate(i, s, q)
        return carry

    lax.fori_loop(1, 2, pass_gates, 0)
    start_down(0, 0)
    lax.fori_loop(2, outer - 1, pass_gates, 0)

    @pl.when(is_end)
    def _():
        helper = jnp.where(line == 0, 1, outer - 2)
        remote(
            dnear.at[helper], dnear.at[helper], raw_send, raw_recv, {"dp": partner}
        ).wait_recv()
        at = line * 2 + (1 - side)
        dgrads[at] = (dgrads[at].astype(F32) + dnear[helper].astype(F32)).astype(BF16)
        near_copy(line).start()

    lax.fori_loop(1, outer - 1, start_down, 0)

    def pass_down(i, carry):
        d = order_at(i)
        at = d * 2 + side

        @pl.when(jnp.logical_not(is_end) & is_fed_down(d))
        def _():
            @pl.when(is_near(d))
            def _():
                near_copy(d).wait_recv()
                for q in range(slices):
                    those = slice(q * slice_width, (q + 1) * slice_width)
                    dline_wait(d, q)
                    dgrads[at, :, those] = (
                        dgrads[at, :, those].astype(F32)
                        + dnear[d, :, those].astype(F32)
                        + dlines[d, :, those].astype(F32)
                    ).astype(BF16)
                    dline_copy(d, q).start()

            @pl.when(jnp.logical_not(is_near(d)))
            def _():
                for q in range(slices):
                    those = slice(q * slice_width, (q + 1) * slice_width)
                    dline_wait(d, q)
                    dgrads[at, :, those] = (
                        dgrads[at, :, those].astype(F32) + dlines[d, :, those].astype(F32)
                    ).astype(BF16)
                    dline_copy(d, q).start()

        return carry

    lax.fori_loop(0, outer - 1, pass_down, 0)

    cross = remote(cross_out, cross_in, cross_send, cross_recv, {"dp": partner})
    for s in halves:

        @pl.when(line > 0)
        def _():
            for q in range(fine):
                gline_wait(line, s, q)
            total[s] += glines[line, s].astype(F32)

        @pl.when(line < outer - 1)
        def _():
            for q in range(fine):
                gline_wait(outer, s, q)
            total[s] += glines[outer, s].astype(F32)

        if s is halves[0]:
            cross_out[...] = total[s].astype(BF16)
            cross.start()

    @pl.when(side == 0)
    def _():
        gate_out[...] = total[0] * inverse

    @pl.when(side == 1)
    def _():
        up_out[...] = total[1] * inverse

    for step in range(1, span):
        back_copy(step).wait_recv()
    route_sum = gs[expert].astype(F32)
    for step in range(1, span):
        route_sum = route_sum + back[step].astype(F32)
    tok_out[...] = route_sum.astype(BF16)

    near_copy(line).wait_recv()
    down_out[...] = (dgrads[me].astype(F32) + dnear[line].astype(F32)) * inverse
    cross.wait_recv()

    @pl.when(side == 0)
    def _():
        up_out[...] = cross_in[...].astype(F32) * inverse

    @pl.when(side == 1)
    def _():
        gate_out[...] = cross_in[...].astype(F32) * inverse

    @pl.when(line > 1)
    def _():
        for q in range(slices):
            those = slice(q * slice_width, (q + 1) * slice_width)
            dline_wait(line, q)
            down_out[:, those] += dlines[line, :, those].astype(F32) * inverse

    @pl.when(line < outer - 2)
    def _():
        for q in range(slices):
            those = slice(q * slice_width, (q + 1) * slice_width)
            dline_wait(outer, q)
            down_out[:, those] += dlines[outer, :, those].astype(F32) * inverse

    for step in range(1, span):
        coef_copy(step).wait_send()
        back_copy(step).wait_send()
    for array in range(3):
        core_copy(array).wait_send()
        for step in range(1, chips):
            for part in range(near_parts if array == 2 else parts):
                chip_copy(array, part, step).wait_send()
    for step in range(1, chips):
        for part in range(parts):
            forward_copy(2, part, step, core).wait_send()
            if part >= near_parts:
                far_copy(part, step).wait_send()
    px_copy.wait_send()
    for step in range(chips):
        for at in every:
            act_copy(step, at).wait_send()

    @pl.when(is_end)
    def _():
        for step in range(chips):
            z_hidden(step).wait_send()
        z_copy.wait_send()
        z_coef.wait_send()

    def finish(i, carry):
        d = order_at(i)

        @pl.when(is_near(d))
        def _():
            near_copy(d).wait_send()

        @pl.when(i < outer - 1)
        def _():
            for s in halves:
                for q in range(fine):
                    gline_copy(d, s, q).wait_send()

        @pl.when((i < outer - 1) & jnp.logical_not(is_end))
        def _():
            for q in range(slices):
                dline_copy(d, q).wait_send()

        return carry

    lax.fori_loop(0, outer, finish, 0)
    cross.wait_send()

    @pl.when(is_helper)
    def _():
        raw_copy.wait_send()


def fused(tokens, d_out, routes, gates, w_gate, w_up, w_down, span, replicas):
    parts = 4
    dma = pltpu.SemaphoreType.DMA
    rows, width = tokens.shape
    units = w_gate.shape[2]
    outer, chips = replicas // 2, span // 2
    feature, shard = width // replicas, units // replicas
    amount = span * rows
    here = pl.BlockSpec(memory_space=pltpu.VMEM)
    away = pl.BlockSpec(memory_space=pltpu.HBM)
    vmem = pltpu.VMEM
    places = max(8, span)
    return pl.pallas_call(
        functools.partial(kernel, span, replicas, parts),
        out_shape=(
            vmem((rows, width), BF16), vmem((feature, units), F32), vmem((feature, units), F32),
            vmem((shard, width), F32),
        ),
        in_specs=[away, away, here, here, away, away, away],
        out_specs=[here] * 4,
        scratch_shapes=[
            vmem((width, units), BF16), vmem((width, units), BF16), vmem((units, width), BF16),
            vmem((span, rows, width), BF16), vmem((span, rows, width), BF16), vmem((span, rows, width), BF16),
            vmem((span, rows, width), BF16),
            vmem((places, rows), F32), vmem((span, places, rows), F32),
            vmem((2, rows, units), F32), vmem((2, rows, units), F32),
            vmem((2, span, rows, units), BF16), vmem((span, rows, units), BF16), vmem((amount, units), BF16),
            vmem((outer, 2, feature, units), BF16), vmem((outer + 1, 2, feature, units), BF16),
            vmem((2, feature, units), F32), vmem((feature, units), BF16), vmem((feature, units), BF16),
            vmem((replicas, shard, width), BF16), vmem((outer, shard, width), BF16),
            vmem((outer + 1, shard, width), BF16),
            vmem((span, rows, width), BF16),
            vmem((span, rows, width), BF16), vmem((span, places, rows), F32), vmem((amount, units), BF16),
            dma((3,)), dma((2,)), dma((span,)), dma((span,)), dma((4,)), dma((4,)),
            dma((4, parts, chips)), dma((4, parts, chips)), dma((4, parts, chips)), dma((4, parts, chips)),
            dma, dma, dma((parts, chips)), dma((parts, chips)), dma((chips, parts)), dma((chips, parts)),
            dma((outer,)), dma((outer,)),
            dma((outer, 2, 4)), dma((outer + 1, 2, 4)), dma((outer, 2)), dma((outer + 1, 2)),
            dma((span,)), dma((span,)), dma, dma,
            dma, dma, dma((chips,)), dma((chips,)), dma, dma, dma, dma,
        ],
        compiler_params=pltpu.CompilerParams(
            collective_id=0, has_side_effects=True, vmem_limit_bytes=(54 + span) << 20
        ),
        name="fused",
    )(tokens, d_out, routes, gates, w_gate, w_up, w_down)


def store_kernel(*refs):
    sources, targets, sem = refs[:4], refs[4:8], refs[8]
    copies = [
        pltpu.make_async_copy(source, target if at == 0 else target.at[0], sem.at[at])
        for at, (source, target) in enumerate(zip(sources, targets))
    ]
    for copy in copies:
        copy.start()
    for copy in copies:
        copy.wait()


def store(arrays):
    shapes = [arrays[0].shape] + [(1,) + a.shape for a in arrays[1:]]
    return pl.pallas_call(
        store_kernel,
        out_shape=tuple(jax.ShapeDtypeStruct(s, a.dtype) for s, a in zip(shapes, arrays)),
        in_specs=[pl.BlockSpec(memory_space=pltpu.VMEM)] * 4,
        out_specs=[pl.BlockSpec(memory_space=pltpu.HBM)] * 4,
        scratch_shapes=[pltpu.SemaphoreType.DMA((4,))],
        compiler_params=pltpu.CompilerParams(vmem_limit_bytes=1 << 20),
        name="store",
    )(*arrays)


def body(tokens, d_out, routes, gate_fixed, w_gate, w_up, w_down):
    span = lax.axis_size("expert")
    replicas = lax.axis_size("dp")
    return store(fused(tokens, d_out, routes.T, gate_fixed.T, w_gate, w_up, w_down, span, replicas))


def solution(mesh):
    rows = P(("dp", "expert"), None)
    whole = P("expert", None, None)
    cut = P("expert", "dp", None)
    return jax.shard_map(
        body, mesh=mesh, in_specs=(rows,) * 4 + (whole,) * 3, out_specs=(rows, cut, cut, cut), check_vma=False
    )
```
